32 devices in a mesh: groups: 2 (over x), wide: 16 (over z, y, core).
Axes of the slice: x: 2, y: 2, z: 4, core: 2. Of those that a mesh axis runs over, the one named last changes fastest.
Arguments:
- residual: bfloat16 [4096, 2048], P(('groups', 'wide')), parts along dimension 0, may hold values from -6 to 6
- queries: bfloat16 [4096, 2048], P(('groups', 'wide')), parts along dimension 0, may hold values from -160 to 160
- new_keys: bfloat16 [4096, 256], P(('groups', 'wide')), parts along dimension 0, may hold values from -6 to 6
- new_values: bfloat16 [4096, 256], P(('groups', 'wide')), parts along dimension 0, may hold values from -6 to 6
- cache_keys: bfloat16 [32, 2048, 256], P(('groups', 'wide')), parts along dimension 0, may hold values from -6 to 6
- cache_values: bfloat16 [32, 2048, 256], P(('groups', 'wide')), parts along dimension 0, may hold values from -6 to 6
- cache_len: int32 [32], P('groups'), parts along dimension 0, may hold values from 1 to 2048, 16384 in all
- o_weight: bfloat16 [2048, 2048], P('wide'), may hold values from -0.75 to 0.75
- norm_gain: float32 [2048], replicated, may hold values from 0.5 to 2
- expert_ids: int32 [4096, 8], P(('groups', 'wide')), parts along dimension 0, may hold values from 0 to 15, all different within a row; in each aligned block of 128 rows (0 to 127, 128 to 255, ...) at most 72 rows name the same one
- gate_raw: float32 [4096, 8], P(('groups', 'wide')), parts along dimension 0, may hold values from 0.1 to 1
- w_gate: bfloat16 [16, 2048, 768], P('wide'), may hold values from -0.125 to 0.125
- w_up: bfloat16 [16, 2048, 768], P('wide'), may hold values from -0.125 to 0.125
- w_down: bfloat16 [16, 768, 2048], P('wide'), may hold values from -0.4375 to 0.4375
Outputs:
- layer_out: bfloat16 [4096, 2048], P(('groups', 'wide')), parts along dimension 0
The draws below stay inside these ranges and needn't reach their ends.
There are 2 independent parts, one for each index of `groups`. The reference program is written for one: setup_inputs(seed, part) draws one part's arguments, and reference() takes and returns one part's arrays. A program takes and returns all parts, laid end to end along the dimension named above; an argument that names none is the same for every part. Nothing has to cross between parts.
Inputs may be any that keep to these rules, and one draw needn't show every extreme that they name: `cache_len`: each span's cache holds 1 or more positions; in every part some span has a full cache of 2048 positions and the lengths sum to 16384. `expert_ids`: each token names 8 different experts; among the 128 tokens of one span no expert is named more than 72 times, and in every draw some span names some expert exactly 72 times.
All inputs are finite; a program needn't handle non-finite values.
Results may differ from the reference program's by a relative error of at most 0.01.
Values may be sent and summed in bfloat16 or wider, within the bound.
A program may use at most 128 MiB of HBM per device.

```python
import math
import jax
import jax.numpy as jnp
import numpy as np
from jax import lax

D = 2048
HEADS = 16
KV_HEADS = 2
HEAD = 128
FF = 768
TOPK = 8
SPAN = 128
CACHE = 2048
EXPERTS = 16
TOKENS = 2048
CAP = 72
N_WIDE = 16


def attention_fields(key):
    cached = jnp.clip(jax.random.normal(jax.random.fold_in(key, 11), (N_WIDE, CACHE, KV_HEADS * HEAD), jnp.float32), -4.5, 4.5)
    fresh = jnp.clip(jax.random.normal(jax.random.fold_in(key, 12), (TOKENS, KV_HEADS * HEAD), jnp.float32), -6.0, 6.0)
    asked = jnp.clip(jax.random.normal(jax.random.fold_in(key, 13), (TOKENS, HEADS * HEAD), jnp.float32), -6.0, 6.0)
    return (cached, fresh, asked)


def draw_cache_keys(key, part):
    return attention_fields(key)[0].astype(jnp.bfloat16)


def draw_new_keys(key, part):
    return attention_fields(key)[1].astype(jnp.bfloat16)


def draw_queries(key, part):
    return attention_fields(key)[2].astype(jnp.bfloat16)


def shard_levels(key, dims, shards, smallest, top_value):
    factor_of = 1.0
    for dim, blocks in shards:
        steps = jax.random.uniform(jax.random.fold_in(jax.random.fold_in(key, 6), dim), (blocks,), jnp.float32, smallest / len(shards), top_value / len(shards))
        factor_of = factor_of * jnp.repeat(jnp.exp(steps), dims[dim] // blocks).reshape((-1,) + (1,) * (len(dims) - 1 - dim))
    return factor_of


def length_profile(amount, total, most, slope):
    loads = [(1 << 20) // math.isqrt(grade ** slope) + 1 for grade in range(2, amount + 1)]
    rest, given = total - most - (amount - 1), [1] * (amount - 1)
    while rest > 0:
        movable = [i for i in range(amount - 1) if given[i] < most]
        whole, budget = sum([loads[i] for i in movable]), rest
        for i in movable:
            addition = min(most - given[i], max(1, budget * loads[i] // whole), rest)
            given[i] = given[i] + addition
            rest = rest - addition
    return np.array([most] + given)


def uneven(key, number_of, total, bound, slope):
    if number_of == 2:
        one = jax.random.randint(key, (), max(1, total - bound), min(bound, total - 1) + 1)
        return jnp.stack([one, total - one])
    tallies = jnp.asarray(length_profile(number_of, total, bound, slope), jnp.int32)
    pairs = (number_of - 1) // 2
    source_of, receiver = tallies[1:1 + 2 * pairs:2], tallies[2:2 + 2 * pairs:2]
    room = jnp.minimum(source_of - 1, bound - receiver)
    passed = jax.random.randint(jax.random.fold_in(key, 1), (pairs,), 0, 1 << 20) % (room + 1)
    tallies = tallies.at[1:1 + 2 * pairs:2].set(source_of - passed).at[2:2 + 2 * pairs:2].set(receiver + passed)
    return tallies[jax.random.permutation(jax.random.fold_in(key, 2), number_of)]


def routed_block(rng, own, number, rows, amount, top, most, slope):
    order = jax.random.permutation(rng, amount)
    packed, usual = portions_of(amount, rows * top, most, slope, True), portions_of(amount, rows * top, most, slope, False)
    places = jnp.arange(amount)

    def named(sizes, turn):
        used = int((sizes > 0).sum())
        fixed = max(1, used // 4)
        moved = fixed + (places - fixed + turn * (used - fixed)) % max(1, amount - fixed)
        return jnp.zeros((amount,), jnp.int32).at[order[jnp.where(places < fixed, places, moved)]].set(jnp.asarray(sizes, jnp.int32))

    sizes = jnp.where(number % 4 == 0, named(packed, number // 4), named(usual, number - number // 4 - 1))
    mixed = jax.random.permutation(jax.random.fold_in(own, 3), amount)
    source_of, receiver = mixed[0:amount // 2 * 2:2], mixed[1:amount // 2 * 2:2]
    margin = jnp.minimum(sizes[source_of] - 1, most - sizes[receiver]) // 2
    margin = jnp.where((source_of == order[0]) | (receiver == order[0]) | (sizes[receiver] == 0), 0, jnp.maximum(margin, 0))
    moved = jax.random.randint(jax.random.fold_in(own, 4), (amount // 2,), 0, 1 << 20) % (margin + 1)
    sizes = sizes.at[source_of].add(-moved).at[receiver].add(moved)
    members = jnp.searchsorted(jnp.cumsum(sizes), jnp.arange(rows * top), side="right").astype(jnp.int32)
    grid = members.reshape(top, rows).T
    grid = grid[jax.random.permutation(jax.random.fold_in(own, 1), rows)]
    turn = jax.random.randint(jax.random.fold_in(own, 2), (rows, 1), 0, top)
    return jnp.take_along_axis(grid, (jnp.arange(top)[None, :] + turn) % top, axis=1)


def portions_of(count, total, reach, skew, full):
    weights = [(1 << 20) // math.isqrt(rank ** skew) + 1 for rank in range(1, count + 1)]
    largest = reach if full else min(reach, max(-(-total // count), total * weights[0] // sum(weights)))
    least = 1 if total - largest >= count - 1 else 0
    counts, rest = [largest] + [least] * (count - 1), total - largest - least * (count - 1)
    while rest > 0:
        free = [i for i in range(1, count) if counts[i] < largest] or [i for i in range(1, count) if counts[i] < reach]
        pool, budget = sum([weights[i] for i in free]), rest
        for i in free:
            addition = min(reach - counts[i], max(1, budget * weights[i] // pool), rest)
            counts[i] = counts[i] + addition
            rest = rest - addition
    return np.array(counts)


def gaussian(stream_key, dims, spread, limit, split=(), dtype=jnp.bfloat16):
    entries = jax.random.normal(stream_key, dims, jnp.float32) * spread
    if len(split) > 0:
        entries = shard_levels(stream_key, dims, split, -0.22, 0.18) * entries
    return jnp.clip(entries, min=-limit, max=limit).astype(dtype)


def setup_inputs(seed: int = 0, part: int = 0) -> dict:
    streams_of = jax.random.split(jax.random.key(seed), 15)
    part_keys = jax.random.split(jax.random.fold_in(streams_of[14], part), 15)
    residual = gaussian(part_keys[0], (TOKENS, D), 1.0, 6.0, ((0, 16),))
    queries = draw_queries(jax.random.fold_in(jax.random.fold_in(streams_of[14], part), 71), part)
    new_keys = draw_new_keys(jax.random.fold_in(jax.random.fold_in(streams_of[14], part), 71), part)
    new_values = gaussian(part_keys[3], (TOKENS, KV_HEADS * HEAD), 1.0, 6.0, ((0, 16),))
    cache_keys = draw_cache_keys(jax.random.fold_in(jax.random.fold_in(streams_of[14], part), 71), part)
    cache_values = gaussian(part_keys[5], (N_WIDE, CACHE, KV_HEADS * HEAD), 1.0, 6.0, ((0, 16),))
    cache_len = uneven(part_keys[6], N_WIDE, N_WIDE * CACHE // 2, CACHE, 2).astype(jnp.int32)
    o_weight = gaussian(streams_of[7], (HEADS * HEAD, D), (D // 32) ** -0.5, 0.75, ((0, 16),))
    norm_gain = jnp.clip(jnp.exp(jax.random.uniform(streams_of[8], (D,), jnp.float32, math.log(0.5), math.log(2.0))), 0.5, 2.0)
    expert_ids_keys = jax.random.split(jax.random.fold_in(part_keys[9], 1), TOKENS // SPAN)
    expert_ids_turns = jax.random.permutation(jax.random.fold_in(part_keys[9], 3), TOKENS // SPAN)
    expert_ids = jax.vmap(lambda own, number: routed_block(jax.random.fold_in(part_keys[9], 2), own, number, SPAN, EXPERTS, TOPK, CAP, 1))(expert_ids_keys, expert_ids_turns).reshape((TOKENS, TOPK))
    gate_raw = jnp.clip(jnp.exp(math.log(1.0) - 2.3025851 * jax.random.uniform(part_keys[10], (TOKENS, TOPK), jnp.float32) ** shard_levels(part_keys[10], (TOKENS, TOPK), ((0, 16),), -0.2, 0.2)), 0.1, 1.0)
    w_gate = gaussian(streams_of[11], (EXPERTS, D, FF), D ** -0.5, 0.125, ((0, 16),))
    w_up = gaussian(streams_of[12], (EXPERTS, D, FF), D ** -0.5, 0.125, ((0, 16),))
    w_down = gaussian(streams_of[13], (EXPERTS, FF, D), (FF // 4) ** -0.5, 0.4375, ((0, 16),))
    return {"residual": residual, "queries": queries, "new_keys": new_keys, "new_values": new_values, "cache_keys": cache_keys, "cache_values": cache_values, "cache_len": cache_len, "o_weight": o_weight, "norm_gain": norm_gain, "expert_ids": expert_ids, "gate_raw": gate_raw, "w_gate": w_gate, "w_up": w_up, "w_down": w_down}


def attend_span(inputs):
    query_rows, key_new, value_new, key_cache, value_cache, length = inputs
    group_size = HEADS // KV_HEADS
    query_four = query_rows.astype(jnp.float32).reshape(SPAN, KV_HEADS, group_size, HEAD)
    key_all = jnp.concatenate([key_cache, key_new], axis=0).astype(jnp.float32).reshape(CACHE + SPAN, KV_HEADS, HEAD)
    value_all = jnp.concatenate([value_cache, value_new], axis=0).astype(jnp.float32).reshape(CACHE + SPAN, KV_HEADS, HEAD)
    scores = jnp.einsum('tgrd,kgd->grtk', query_four, key_all) * HEAD ** (-0.5)
    positions = jnp.arange(CACHE + SPAN).astype(jnp.int32)
    token_rows = jnp.arange(SPAN).astype(jnp.int32)
    visible = jnp.where(positions[None, :] < CACHE, positions[None, :] < length, positions[None, :] - CACHE <= token_rows[:, None])
    scores = jnp.where(visible[None, None], scores, jnp.float32(-1e+30))
    row_max = lax.optimization_barrier(jnp.max(scores, axis=-1, keepdims=True))
    weights = jnp.exp(scores - row_max)
    denominator = lax.optimization_barrier(jnp.sum(weights, axis=-1))
    rounded = lax.optimization_barrier(weights.astype(jnp.bfloat16)).astype(jnp.float32)
    numerator = jnp.einsum('grtk,kgd->grtd', rounded, value_all)
    output = numerator / denominator[..., None]
    return jnp.transpose(output, (2, 0, 1, 3)).reshape(SPAN, HEADS * HEAD).astype(jnp.bfloat16)

def reference(residual, queries, new_keys, new_values, cache_keys, cache_values, cache_len, o_weight, norm_gain, expert_ids, gate_raw, w_gate, w_up, w_down):
    attn = lax.map(attend_span, (queries.reshape(N_WIDE, SPAN, HEADS * HEAD), new_keys.reshape(N_WIDE, SPAN, KV_HEADS * HEAD), new_values.reshape(N_WIDE, SPAN, KV_HEADS * HEAD), cache_keys, cache_values, cache_len))
    attn = attn.reshape(TOKENS, HEADS * HEAD)
    projected = jnp.dot(attn, o_weight, preferred_element_type=jnp.float32)
    mixed = residual.astype(jnp.float32) + projected
    normed = (mixed * lax.rsqrt(lax.optimization_barrier(jnp.mean(mixed * mixed, axis=-1, keepdims=True)) + 1e-06) * norm_gain).astype(jnp.bfloat16)
    shares = gate_raw / lax.optimization_barrier(jnp.sum(gate_raw, axis=-1, keepdims=True))
    flat_ids = expert_ids.reshape(N_WIDE, SPAN * TOPK)
    one_hot = (flat_ids[..., None] == jnp.arange(EXPERTS).astype(jnp.int32)[None, None, :]).astype(jnp.int32)
    ranks = (lax.optimization_barrier(jnp.sum(jnp.cumsum(one_hot, axis=1) * one_hot, axis=-1)) - 1).astype(jnp.int32)
    source = jnp.arange(N_WIDE).astype(jnp.int32)[:, None]
    destination = (flat_ids * (N_WIDE * CAP) + source * CAP + ranks).astype(jnp.int32).reshape(-1)
    global_tokens = (source * SPAN + (jnp.arange(SPAN * TOPK).astype(jnp.int32) // TOPK)[None, :]).astype(jnp.int32).reshape(-1)
    token_table = jnp.full((EXPERTS * N_WIDE * CAP,), TOKENS, jnp.int32).at[destination].set(global_tokens).reshape(EXPERTS, N_WIDE * CAP)
    share_table = jnp.zeros((EXPERTS * N_WIDE * CAP,), jnp.float32).at[destination].set(shares.reshape(-1)).reshape(EXPERTS, N_WIDE * CAP)
    padded = jnp.concatenate([normed, jnp.zeros((1, D), jnp.bfloat16)], axis=0)

    def expert_step(carry, inputs):
        table_row, share_row, gate_w, up_w, down_w = inputs
        rows_in = padded[table_row]
        gate_part = jnp.dot(rows_in, gate_w, preferred_element_type=jnp.float32)
        up_part = jnp.dot(rows_in, up_w, preferred_element_type=jnp.float32)
        activated = (jax.nn.silu(gate_part) * up_part).astype(jnp.bfloat16)
        expert_rows = jnp.dot(activated, down_w, preferred_element_type=jnp.float32).astype(jnp.bfloat16)
        carry = carry.at[table_row].add(expert_rows.astype(jnp.float32) * share_row[:, None])
        return (carry, None)
    routed, unused = lax.scan(expert_step, jnp.zeros((TOKENS + 1, D), jnp.float32), (token_table, share_table, w_gate, w_up, w_down))
    return (mixed + routed[:TOKENS]).astype(jnp.bfloat16)
```

```python
import functools
import jax
import jax.numpy as jnp
from jax import lax
from jax.experimental import pallas as pl
from jax.experimental.pallas import tpu as pltpu
from jax.sharding import PartitionSpec as P

D = 2048
HEADS = 16
KV_HEADS = 2
HEAD = 128
TOPK = 8
SPAN = 128
PACK = 2
EXP2_SCALE = HEAD ** (-0.5) * 1.4426950408889634


def attention_kernel(length_ref, q_ref, nk_ref, nv_ref, k_ref, v_ref, out_ref):
    tokens = q_ref.shape[0]
    rows = PACK * tokens
    cache = k_ref.shape[1]
    q = jnp.concatenate([q_ref[:, i * HEAD : (i + 1) * HEAD] for i in range(PACK)], axis=0)
    dims = (((1,), (1,)), ((), ()))
    s = lax.dot_general(q, k_ref[0], dims, preferred_element_type=jnp.float32)
    position = lax.broadcasted_iota(jnp.int32, (1, cache), 1)
    s = jnp.where(position < length_ref[0], s, jnp.float32(-1e30))
    s_new = lax.dot_general(q, nk_ref[...], dims, preferred_element_type=jnp.float32)
    row = lax.broadcasted_iota(jnp.int32, (rows, tokens), 0) % tokens
    column = lax.broadcasted_iota(jnp.int32, (rows, tokens), 1)
    s_new = jnp.where(column <= row, s_new, jnp.float32(-1e30))
    top = jnp.maximum(jnp.max(s, axis=1, keepdims=True), jnp.max(s_new, axis=1, keepdims=True))
    w = jnp.exp2((s - top) * EXP2_SCALE)
    w_new = jnp.exp2((s_new - top) * EXP2_SCALE)
    total = jnp.sum(w, axis=1, keepdims=True) + jnp.sum(w_new, axis=1, keepdims=True)
    out = jnp.dot(w.astype(jnp.bfloat16), v_ref[0], preferred_element_type=jnp.float32)
    out += jnp.dot(w_new.astype(jnp.bfloat16), nv_ref[...], preferred_element_type=jnp.float32)
    out = (out / total).astype(out_ref.dtype)
    for i in range(PACK):
        out_ref[:, i * HEAD : (i + 1) * HEAD] = out[i * tokens : (i + 1) * tokens]


def attention(length, queries, new_keys, new_values, cache_keys, cache_values):
    tokens, width = queries.shape
    cache = cache_keys.shape[1]
    per_group = HEADS // KV_HEADS // PACK
    return pl.pallas_call(
        attention_kernel,
        grid=(HEADS // PACK,),
        in_specs=[
            pl.BlockSpec(memory_space=pltpu.SMEM),
            pl.BlockSpec((tokens, PACK * HEAD), lambda i: (0, i)),
            pl.BlockSpec((tokens, HEAD), lambda i: (0, i // per_group)),
            pl.BlockSpec((tokens, HEAD), lambda i: (0, i // per_group)),
            pl.BlockSpec((1, cache, HEAD), lambda i: (0, 0, i // per_group)),
            pl.BlockSpec((1, cache, HEAD), lambda i: (0, 0, i // per_group)),
        ],
        out_specs=pl.BlockSpec((tokens, PACK * HEAD), lambda i: (0, i)),
        out_shape=jax.ShapeDtypeStruct((tokens, width), jnp.bfloat16),
        cost_estimate=pl.CostEstimate(
            flops=4 * tokens * width * (cache + tokens),
            bytes_accessed=4 * cache * KV_HEADS * HEAD + 4 * tokens * width,
            transcendentals=tokens * HEADS * (cache + tokens),
        ),
    )(length, queries, new_keys, new_values, cache_keys, cache_values)


def run_expert(rows_in, gate_w, up_w, down_w):
    gate_part = jnp.dot(rows_in, gate_w, preferred_element_type=jnp.float32)
    up_part = jnp.dot(rows_in, up_w, preferred_element_type=jnp.float32)
    activated = (jax.nn.silu(gate_part) * up_part).astype(jnp.bfloat16)
    return jnp.dot(activated, down_w, preferred_element_type=jnp.float32)


def sparse_experts(normed, expert_ids, shares, gate_w, up_w, down_w, devices):
    token_count = normed.shape[0]
    capacity = SPAN * TOPK // devices + max(2, SPAN * TOPK // (8 * devices))
    flat_ids = expert_ids.reshape(-1)
    named = expert_ids[:, :, None] == jnp.arange(devices, dtype=jnp.int32)[None, None, :]
    earlier = jnp.tril(jnp.ones((token_count, token_count), jnp.bfloat16), -1)
    before = jnp.dot(
        earlier, jnp.any(named, axis=1).astype(jnp.bfloat16), preferred_element_type=jnp.float32
    )
    ranks = jnp.sum(jnp.where(named, before[:, None, :], 0.0), axis=-1)
    ranks = ranks.astype(jnp.int32).reshape(-1)
    slot_index = flat_ids * capacity + ranks
    token_of = jnp.arange(flat_ids.shape[0], dtype=jnp.int32) // TOPK
    slot_token = (
        jnp.full((devices * capacity,), token_count, jnp.int32).at[slot_index].set(token_of)
    )
    padded = jnp.concatenate([normed, jnp.zeros((1, D), jnp.bfloat16)], axis=0)
    outgoing = padded[slot_token].reshape(devices, capacity, D)
    arrived = lax.all_to_all(outgoing, "wide", split_axis=0, concat_axis=0, tiled=True)
    served = run_expert(arrived.reshape(-1, D), gate_w, up_w, down_w).astype(jnp.bfloat16)
    served = served.reshape(devices, capacity, D)
    returned_rows = lax.all_to_all(served, "wide", split_axis=0, concat_axis=0, tiled=True)
    picked = returned_rows.reshape(devices * capacity, D)[slot_index].reshape(token_count, TOPK, D)
    return jnp.sum(picked.astype(jnp.float32) * shares[..., None], axis=1)


LINE = 4
PAIR = 2
EXTRA = 128
DOWN, UP, ACROSS, TWIN = range(4)


def attend(q, key, value, new_key, new_value, length, tokens):
    rows = q.shape[0]
    dims = (((1,), (1,)), ((), ()))
    s = lax.dot_general(q, key, dims, preferred_element_type=jnp.float32)
    position = lax.broadcasted_iota(jnp.int32, (1, key.shape[0]), 1)
    s = jnp.where(position < length, s, jnp.float32(-1e30))
    s_new = lax.dot_general(q, new_key, dims, preferred_element_type=jnp.float32)
    row = lax.broadcasted_iota(jnp.int32, (rows, tokens), 0) % tokens
    column = lax.broadcasted_iota(jnp.int32, (rows, tokens), 1)
    s_new = jnp.where(column <= row, s_new, jnp.float32(-1e30))
    top = jnp.maximum(jnp.max(s, axis=1, keepdims=True), jnp.max(s_new, axis=1, keepdims=True))
    w = jnp.exp2((s - top) * EXP2_SCALE)
    w_new = jnp.exp2((s_new - top) * EXP2_SCALE)
    total = jnp.sum(w, axis=1, keepdims=True) + jnp.sum(w_new, axis=1, keepdims=True)
    out = jnp.dot(w.astype(jnp.bfloat16), value, preferred_element_type=jnp.float32)
    out += jnp.dot(w_new.astype(jnp.bfloat16), new_value, preferred_element_type=jnp.float32)
    return (out / total).astype(jnp.bfloat16)


class Place:
    def __init__(self):
        self.me = lax.axis_index("wide")
        self.core = self.me % 2
        self.y = (self.me // 2) % PAIR
        self.z = self.me // (2 * PAIR)

    def block(self, z, y, core):
        return (z * PAIR + y) * 2 + core

    def towards(self, way):
        z, y, core = self.z, self.y, self.core
        if way == DOWN:
            return self.block(z - 1, y, core)
        if way == UP:
            return self.block(z + 1, y, core)
        if way == ACROSS:
            return self.block(z, 1 - y, core)
        return self.block(z, y, 1 - core)

    def line_at(self, i):
        low = self.z < LINE // 2
        inner = jnp.where(low, self.z, LINE - 1 - self.z)
        near = jnp.where((inner == 0) | (i >= 2), i, 1 - i)
        return jnp.where(low, near, LINE - 1 - near)

    def barrier(self, with_x=False):
        sem = pltpu.get_barrier_semaphore()

        def greet(way):
            pl.semaphore_signal(
                sem,
                inc=1,
                device_id={"wide": self.towards(way)},
                device_id_type=pl.DeviceIdType.MESH,
            )

        pl.when(self.z > 0)(lambda: greet(DOWN))
        pl.when(self.z < LINE - 1)(lambda: greet(UP))
        greet(ACROSS)
        greet(TWIN)
        if with_x:
            pl.semaphore_signal(
                sem, inc=1, device_id={"groups": 1 - lax.axis_index("groups")},
                device_id_type=pl.DeviceIdType.MESH,
            )
        ends = jnp.where((self.z == 0) | (self.z == LINE - 1), 1, 0)
        pl.semaphore_wait(sem, (5 if with_x else 4) - ends)


UPN, DOWNN = 0, 1
XWAY = 4
TILE = 16
P0, P1, PR, Q0, Q1, QS = range(6)
A_SLOTS = 6


def gather_events(*items):
    codes = [kind * 4 + nb for kind, nb in items]
    codes += [31] * (A_SLOTS - len(codes))
    return sum(c << (5 * j) for j, c in enumerate(codes))


A_END = (
    gather_events(), gather_events(), gather_events(),
    gather_events((Q0, 0), (P0, 1)),
    gather_events((Q1, 0)),
    gather_events((P1, 1)),
    gather_events((QS, 0), (Q0, 1)),
    gather_events((P0, 2), (PR, 1), (Q1, 1)),
    gather_events((P1, 2), (QS, 1)),
    gather_events((Q0, 2), (PR, 2), (P0, 3)),
    gather_events((Q1, 2), (QS, 2)),
    gather_events((P1, 3), (Q0, 3), (PR, 3), (Q1, 3), (QS, 3)),
)
A_INNER = (
    gather_events(), gather_events(), gather_events(),
    gather_events((Q0, 1), (P0, 0), (P0, 2)),
    gather_events((Q1, 1)),
    gather_events((P1, 0), (P1, 2)),
    gather_events((QS, 1), (Q0, 0)),
    gather_events((P0, 3), (PR, 0), (PR, 2)),
    gather_events((Q0, 2), (P1, 3)),
    gather_events((Q1, 0), (QS, 0)),
    gather_events((Q1, 2), (QS, 2)),
    gather_events((Q0, 3), (PR, 3), (Q1, 3), (QS, 3)),
)


def pick(index, inner, ends, inners):
    at_end, at_inner = jnp.int32(ends[0]), jnp.int32(inners[0])
    for k in range(1, len(ends)):
        at_end = jnp.where(index == k, jnp.int32(ends[k]), at_end)
        at_inner = jnp.where(index == k, jnp.int32(inners[k]), at_inner)
    return jnp.where(inner == 1, at_inner, at_end)


def attention_block_kernel(
    length_ref, q_ref, nk_ref, nv_ref, k_ref, v_ref, res_ref, gain_ref, extra_ref, ow_ref,
    mixed_ref, rows_ref, held, attn, own_sem, send_sem, recv_sem,
):
    place = Place()
    z, y, core = place.z, place.y, place.core
    group = lax.axis_index("groups")
    tokens = q_ref.shape[0]
    depth = ow_ref.shape[0]
    low = z < LINE // 2
    inner = jnp.where(low, z, LINE - 1 - z)
    step_up = jnp.where(low, 1, -1)
    own = pltpu.make_async_copy(ow_ref, held.at[place.me], own_sem)
    own.start()
    place.barrier(True)
    own.wait()

    third = depth // 8 * 2
    half = depth // 8 * 3
    last = depth - half
    span = {
        P0: (jnp.where(group == 0, 0, last), half),
        P1: (jnp.where(group == 0, half, third), half),
        PR: (jnp.where(group == 0, depth - third, 0), third),
        Q0: (jnp.where(group == 0, 0, last), half),
        Q1: (half, depth - 2 * half),
        QS: (jnp.where(group == 0, last, 0), half),
    }
    given = {PR: (jnp.where(group == 0, 0, depth - third), third), QS: span[Q0]}

    def real(nb):
        return jnp.where(low, nb, LINE - 1 - nb)

    def device(way):
        if way == XWAY:
            return {"groups": 1 - group}
        if way == UPN:
            return {"wide": place.block(z + step_up, y, core)}
        if way == DOWNN:
            return {"wide": place.block(z - step_up, y, core)}
        return {"wide": place.towards(way)}

    def copy(b, what, way):
        start, size = given[what] if way == XWAY else span[what]
        if not isinstance(start, int):
            start = pl.multiple_of(start, TILE)
        ref = held.at[b, pl.ds(start, size)]
        i = what % 3
        return pltpu.make_async_remote_copy(
            src_ref=ref, dst_ref=ref, send_sem=send_sem.at[b, i, way], recv_sem=recv_sem.at[b, i],
            device_id=device(way), device_id_type=pl.DeviceIdType.MESH,
        )

    def whole(b):
        return pltpu.make_async_remote_copy(
            src_ref=held.at[b], dst_ref=held.at[b], send_sem=send_sem.at[b, 2, TWIN],
            recv_sem=recv_sem.at[b, 0], device_id=device(TWIN),
            device_id_type=pl.DeviceIdType.MESH,
        )

    def block_at(nb, yb, c):
        return place.block(real(nb), yb, c)

    me = place.me
    copy(me, P0, UPN).start()
    pl.when(inner == 1)(copy(me, P0, DOWNN).start)
    copy(me, Q0, ACROSS).start()
    copy(me, P1, UPN).start()
    pl.when(inner == 1)(copy(me, P1, DOWNN).start)
    copy(me, Q1, ACROSS).start()
    whole(me).start()

    def happen(code):
        nb = lax.rem(code, 4)
        kind = code // 4
        own_b = block_at(nb, y, core)
        other_b = block_at(nb, 1 - y, core)

        def line(what):
            pl.when(nb < inner)(copy(own_b, what, UPN).start)
            pl.when((nb > inner) & (inner == 1))(copy(own_b, what, DOWNN).start)

        @pl.when(kind == P0)
        def _():
            copy(own_b, P0, TWIN).wait_recv()
            line(P0)
            copy(own_b, Q0, ACROSS).start()
            copy(own_b, PR, XWAY).start()
            copy(own_b, P0, TWIN).start()

        @pl.when(kind == P1)
        def _():
            copy(own_b, P1, TWIN).wait_recv()
            line(P1)
            copy(own_b, Q1, ACROSS).start()
            copy(own_b, P1, TWIN).start()

        @pl.when(kind == PR)
        def _():
            copy(own_b, PR, TWIN).wait_recv()
            copy(own_b, PR, TWIN).start()

        @pl.when(kind == Q0)
        def _():
            copy(other_b, Q0, TWIN).wait_recv()
            copy(other_b, QS, XWAY).start()
            copy(other_b, Q0, TWIN).start()

        @pl.when(kind == Q1)
        def _():
            copy(other_b, Q1, TWIN).wait_recv()
            copy(other_b, Q1, TWIN).start()

        @pl.when(kind == QS)
        def _():
            copy(other_b, QS, TWIN).wait_recv()
            copy(other_b, QS, TWIN).start()

    length = length_ref[place.me]
    attends = HEADS // PACK
    per_group = HEADS // KV_HEADS // PACK

    def attend_step(i):
        q = jnp.concatenate(
            [
                q_ref[:, pl.ds(pl.multiple_of((i * PACK + j) * HEAD, HEAD), HEAD)]
                for j in range(PACK)
            ],
            axis=0,
        )
        columns = pl.ds(pl.multiple_of(i // per_group * HEAD, HEAD), HEAD)
        out = attend(
            q, k_ref[0, :, columns], v_ref[0, :, columns], nk_ref[:, columns],
            nv_ref[:, columns], length, tokens,
        )
        for j in range(PACK):
            attn[:, pl.ds(pl.multiple_of((i * PACK + j) * HEAD, HEAD), HEAD)] = out[
                j * tokens : (j + 1) * tokens
            ]

    mixed_ref[...] = res_ref[...].astype(jnp.float32)

    def project(nb, is_own):
        yb = jnp.where(is_own, y, 1 - y)
        b = block_at(nb, yb, 1 - core)

        @pl.when(is_own & (nb == inner))
        def _():
            whole(b).wait_recv()

        @pl.when(is_own & (nb != inner))
        def _():
            for what in (P0, P1, PR):
                copy(b, what, TWIN).wait_recv()

        @pl.when(jnp.logical_not(is_own))
        def _():
            for what in (Q0, Q1, QS):
                copy(b, what, TWIN).wait_recv()

        first = block_at(nb, yb, 0)
        part = attn[:, pl.ds(pl.multiple_of(first * depth, 2 * depth), 2 * depth)]
        weight = held[pl.ds(first, 2)].reshape(2 * depth, D)
        mixed_ref[...] += jnp.dot(part, weight, preferred_element_type=jnp.float32)

    def step(s, carry):
        def one(j, word):
            code = lax.rem(word, 32)
            pl.when(code < 31)(lambda: happen(code))
            return word // 32

        lax.fori_loop(0, A_SLOTS, one, pick(s, inner, A_END, A_INNER))
        pl.when(s < attends)(lambda: attend_step(s))

        @pl.when(s >= attends)
        def _():
            nb = pick(s - attends, inner, (0, 1, 2, 3), (1, 0, 2, 3))

            def both(k, inside):
                project(nb, k == 0)
                return inside

            lax.fori_loop(0, 2, both, 0)

        return carry

    lax.fori_loop(0, len(A_END), step, 0)
    mixed = mixed_ref[...]
    scale = lax.rsqrt(jnp.mean(mixed * mixed, axis=-1, keepdims=True) + 1e-06)
    rows_ref[:, :D] = (mixed * scale * gain_ref[...]).astype(jnp.bfloat16)
    rows_ref[:, D:] = extra_ref[...]

    def settle(nb, carry):
        own_b = block_at(nb, y, core)
        other_b = block_at(nb, 1 - y, core)
        for what in (P0, P1):
            pl.when(nb <= inner)(copy(own_b, what, UPN).wait_send)
            pl.when((nb >= inner) & (inner == 1))(copy(own_b, what, DOWNN).wait_send)
        copy(own_b, Q0, ACROSS).wait_send()
        copy(own_b, Q1, ACROSS).wait_send()

        @pl.when(nb == inner)
        def _():
            whole(own_b).wait_send()

        @pl.when(nb != inner)
        def _():
            copy(own_b, PR, XWAY).wait_send()
            for what in (P0, P1, PR):
                copy(own_b, what, TWIN).wait_send()

        copy(other_b, QS, XWAY).wait_send()
        for what in (Q0, Q1, QS):
            copy(other_b, what, TWIN).wait_send()
        return carry

    lax.fori_loop(0, LINE, settle, 0)


def attention_block(
    cache_len, queries, new_keys, new_values, cache_keys, cache_values, residual, gain, extra,
    o_weight, devices,
):
    tokens, width = queries.shape
    cache = cache_keys.shape[1]
    vmem = pl.BlockSpec(memory_space=pltpu.VMEM)
    return pl.pallas_call(
        attention_block_kernel,
        in_specs=[pl.BlockSpec(memory_space=pltpu.SMEM)] + [vmem] * 8
        + [pl.BlockSpec(memory_space=pl.ANY)],
        out_specs=[vmem, vmem],
        out_shape=[
            jax.ShapeDtypeStruct((tokens, D), jnp.float32),
            jax.ShapeDtypeStruct((tokens, D + EXTRA), jnp.bfloat16),
        ],
        scratch_shapes=[
            pltpu.VMEM((devices,) + o_weight.shape, jnp.bfloat16),
            pltpu.VMEM((tokens, width), jnp.bfloat16),
            pltpu.SemaphoreType.DMA,
            pltpu.SemaphoreType.DMA((devices, 3, 5)),
            pltpu.SemaphoreType.DMA((devices, 3)),
        ],
        compiler_params=pltpu.CompilerParams(
            collective_id=0, has_side_effects=True, vmem_limit_bytes=60 << 20
        ),
    )(
        cache_len, queries, new_keys, new_values, cache_keys, cache_values, residual, gain, extra,
        o_weight,
    )


SUBS = 2
PA, PB, PC, PD = range(4)
ARRIVE, OWN_UP, OWN_DOWN, NOTHING = range(4)
WORDS = 3


def event(kind, nb, piece, h):
    return ((kind * 4 + nb) * 4 + piece) * 2 + h


def events(text):
    kinds = {"u": OWN_UP, "d": OWN_DOWN}
    codes = []
    for item in (text[k : k + 3] for k in range(0, len(text), 3)):
        if item[0] in kinds:
            codes.append(event(kinds[item[0]], 0, "abcd".index(item[1]), int(item[2])))
        else:
            codes.append(event(ARRIVE, int(item[0]), "abcd".index(item[1]), int(item[2])))
    assert len(codes) <= 4 * WORDS
    codes += [127] * (4 * WORDS - len(codes))
    return [sum(c << (7 * j) for j, c in enumerate(codes[4 * w : 4 * w + 4])) for w in range(WORDS)]


def folds(text):
    codes = [int(item[0]) * 4 + int(item[1]) for item in (text[k : k + 2] for k in range(0, len(text), 2))]
    codes += [15] * (7 - len(codes))
    return sum(c << (4 * j) for j, c in enumerate(codes))


END_STEPS = (
    ("0b0ub00b1ub1uc0uc11a0", "01", ""),
    ("0d00d12a0", "00", ""),
    ("3a03a13b03b1", "31", "3132"),
    ("3c03c13d03d1", "30", ""),
    ("2a12b02b1", "21", "302122"),
    ("2c02c12d02d1", "20", ""),
    ("1a11b01b1", "11", "201112"),
    ("1c01c11d01d1", "10", "10"),
)
INNER_STEPS = (
    ("0a02a01b00a13a01b1", "11", ""),
    ("0b03a11d00b13b01d1", "10", ""),
    ("0c03b10c13c0ua1ub0ub1uc0uc1", "01", ""),
    ("3c10d00d1", "00", ""),
    ("2a1da1db0", "31", ""),
    ("2b03d03d12b1db1", "30", ""),
    ("2c02c1dc0dc1", "21", "3132"),
    ("2d02d1", "20", "30010221002220"),
)


def experts_kernel(
    x_ref, wg_ref, wu_ref, wd_ref, mixed_ref, out_ref,
    rows, part, from_twin, from_pair, from_line, acc, wg, wu, wd,
    own_sem, send_sem, recv_sem, back_send, twin_sem, pair_sem, line_sem,
):
    place = Place()
    me, z, y, core = place.me, place.z, place.y, place.core
    half = x_ref.shape[0] // 2
    sub = half // SUBS
    devices = rows.shape[0] // (2 * SUBS)
    low = z < LINE // 2
    inner = jnp.where(low, z, LINE - 1 - z)
    step_up = jnp.where(low, 1, -1)
    side_up = jnp.where(low, 0, 1)

    def real(nb):
        return jnp.where(low, nb, LINE - 1 - nb)

    def target(way):
        if way == UPN:
            return place.block(z + step_up, y, core)
        if way == DOWNN:
            return place.block(z - step_up, y, core)
        return place.towards(way)

    def send(source, dest, send_one, recv_one, way):
        return pltpu.make_async_remote_copy(
            src_ref=source, dst_ref=dest, send_sem=send_one, recv_sem=recv_one,
            device_id={"wide": target(way)}, device_id_type=pl.DeviceIdType.MESH,
        )

    def slot(zb, p, yb, c):
        return ((zb * 2 + p) * PAIR + yb) * 2 + c

    def copy(b, h, way):
        t = b * SUBS + h
        return send(rows.at[t], rows.at[t], send_sem.at[t, way], recv_sem.at[t], way)

    loads = [
        pltpu.make_async_copy(
            x_ref.at[pl.ds(p * half + h * sub, sub)],
            rows.at[slot(z, p, y, core) * SUBS + h],
            own_sem.at[p * SUBS + h],
        )
        for p in range(2)
        for h in range(SUBS)
    ]
    loads += [
        pltpu.make_async_copy(source, dest, own_sem.at[2 * SUBS + k])
        for k, (source, dest) in enumerate(((wg_ref, wg), (wu_ref, wu), (wd_ref, wd)))
    ]
    for load in loads:
        load.start()
    place.barrier()
    own_a = slot(z, 1, y, core)
    own_c = slot(z, 0, y, core)
    for h in range(SUBS):
        loads[SUBS + h].wait()
        copy(own_a, h, ACROSS).start()
        if h == 0:
            copy(own_a, h, UPN).start()
            pl.when(inner == 1)(copy(own_a, h, DOWNN).start)
        else:
            pl.when(inner == 0)(copy(own_a, h, UPN).start)
        copy(own_a, h, TWIN).start()
    for h in range(SUBS):
        loads[h].wait()
        copy(own_c, h, ACROSS).start()
        copy(own_c, h, TWIN).start()

    lane = lax.broadcasted_iota(jnp.int32, (1, EXTRA), 1)
    chosen = (lane == me) | (lane == me + devices)

    def to_twin(zb, p, yb):
        b = slot(zb, p, yb, 1 - core)
        t = (zb * 2 + p) * PAIR + yb
        return send(part.at[b], from_twin.at[t], back_send.at[b], twin_sem.at[t], TWIN)

    def to_pair(zb, p):
        b = slot(zb, p, 1 - y, core)
        t = LINE if p else zb
        return send(part.at[b], from_pair.at[t], back_send.at[b], pair_sem.at[t], ACROSS)

    def kind_slot(zb, kind):
        p = jnp.minimum(kind, 1)
        yb = jnp.where(kind == 2, 1 - y, y)
        return p, yb, slot(zb, p, yb, core)

    def to_line(zb, kind, way):
        b = kind_slot(zb, kind)[2]
        side = side_up if way == UPN else 1 - side_up
        return send(
            part.at[b], from_line.at[side, zb, kind], back_send.at[b],
            line_sem.at[side, zb, kind], way,
        )

    def wait_rows(b):
        for h in range(SUBS):
            copy(b, h, TWIN).wait_recv()

    def serve(zb, p):
        wait_rows(slot(zb, p, 0, 1 - core))
        wait_rows(slot(zb, p, 1, 1 - core))
        first = slot(zb, p, 0, 0)
        four = rows[pl.ds(first * SUBS, 4 * SUBS)].reshape(4 * half, D + EXTRA)
        x = four[:, :D]
        share = jnp.sum(
            jnp.where(chosen, four[:, D:].astype(jnp.float32), 0.0), axis=1, keepdims=True
        )
        gate = jnp.dot(x, wg[...], preferred_element_type=jnp.float32)
        up = jnp.dot(x, wu[...], preferred_element_type=jnp.float32)
        act = (gate / (1.0 + jnp.exp(-gate)) * up).astype(jnp.bfloat16)
        out = jnp.dot(act, wd[...], preferred_element_type=jnp.float32) * share
        part[pl.ds(first, 4)] = out.astype(jnp.bfloat16).reshape(4, half, D)
        to_twin(zb, p, 0).start()
        to_twin(zb, p, 1).start()

    def with_twin(zb, p, yb):
        to_twin(zb, p, yb).wait_recv()
        b = slot(zb, p, yb, core)
        t = (zb * 2 + p) * PAIR + yb
        return part[b].astype(jnp.float32) + from_twin[t].astype(jnp.float32)

    def add_line(zb, kind, way):
        to_line(zb, kind, way).wait_recv()
        side = side_up if way == UPN else 1 - side_up
        acc[...] += from_line[side, zb, kind].astype(jnp.float32)

    def fold(nb, kind):
        zb = real(nb)
        p, yb, b = kind_slot(zb, kind)
        acc[...] = with_twin(zb, p, yb)

        @pl.when(kind == 0)
        def _():
            to_pair(zb, 0).wait_recv()
            acc[...] += from_pair[zb].astype(jnp.float32)

        pl.when((nb > inner) & (inner == 1))(lambda: add_line(zb, kind, UPN))
        pl.when(nb < inner)(lambda: add_line(zb, kind, DOWNN))
        part[b] = acc[...].astype(jnp.bfloat16)
        pl.when(nb > inner)(to_line(zb, kind, UPN).start)
        pl.when(nb < inner)(to_line(zb, kind, DOWNN).start)

    def happen(code):
        h = lax.rem(code, 2)
        piece = lax.rem(code // 2, 4)
        nb = lax.rem(code // 8, 4)
        kind = code // 32
        p = jnp.where(piece <= PB, 1, 0)
        yb = jnp.where((piece == PA) | (piece == PC), y, 1 - y)

        @pl.when(kind == ARRIVE)
        def _():
            b = slot(real(nb), p, yb, core)
            copy(b, h, TWIN).wait_recv()
            onward = piece != PD
            pl.when(onward & (nb < inner))(copy(b, h, UPN).start)
            pl.when(onward & (nb > inner) & (inner == 1))(copy(b, h, DOWNN).start)
            pl.when((piece == PC) & (nb != inner))(copy(b, h, ACROSS).start)
            copy(b, h, TWIN).start()

        mine = slot(z, p, yb, core)
        pl.when(kind == OWN_UP)(copy(mine, h, UPN).start)
        pl.when(kind == OWN_DOWN)(copy(mine, h, DOWNN).start)

    end_words = [events(e[0]) for e in END_STEPS]
    inner_words = [events(e[0]) for e in INNER_STEPS]

    def step(s, carry):
        for w in range(WORDS):
            def one(j, word):
                happen(lax.rem(word, 128))
                return word // 128

            lax.fori_loop(0, 4, one, pick(s, inner, [e[w] for e in end_words], [e[w] for e in inner_words]))

        @pl.when(s == 0)
        def _():
            for load in loads[2 * SUBS :]:
                load.wait()

        nb = pick(
            s, inner, [int(e[1][0]) for e in END_STEPS], [int(e[1][0]) for e in INNER_STEPS]
        )
        zb = real(nb)
        p = 1 - lax.rem(s, 2)
        serve(zb, p)

        @pl.when(p == 0)
        def _():
            part[slot(zb, 0, 1 - y, core)] = with_twin(zb, 0, 1 - y).astype(jnp.bfloat16)
            to_pair(zb, 0).start()

        def one_fold(j, word):
            code = lax.rem(word, 16)
            pl.when(code < 15)(lambda: fold(code // 4, lax.rem(code, 4)))
            return word // 16

        lax.fori_loop(0, 7, one_fold, pick(
            s, inner, [folds(e[2]) for e in END_STEPS], [folds(e[2]) for e in INNER_STEPS]
        ))
        return carry

    lax.fori_loop(0, len(END_STEPS), step, 0)

    def both_sides(kind):
        pl.when(inner == 1)(lambda: add_line(z, kind, UPN))
        add_line(z, kind, DOWNN)

    acc[...] = with_twin(z, 1, 1 - y)
    both_sides(2)
    part[slot(z, 1, 1 - y, core)] = acc[...].astype(jnp.bfloat16)
    to_pair(z, 1).start()
    for p in range(2):
        here = pl.ds(p * half, half)
        acc[...] = with_twin(z, p, y) + mixed_ref[here]
        both_sides(p)
        to_pair(z, p).wait_recv()
        acc[...] += from_pair[LINE if p else z].astype(jnp.float32)
        out_ref[here] = acc[...].astype(jnp.bfloat16)
    for h in range(SUBS):
        copy(own_a, h, ACROSS).wait_send()
    to_pair(z, 1).wait_send()

    def settle(nb, carry):
        zb = real(nb)
        for h in range(SUBS):
            for p, yb in ((0, y), (1, y), (1, 1 - y)):
                b = slot(zb, p, yb, core)
                pl.when(nb <= inner)(copy(b, h, UPN).wait_send)
                pl.when((nb >= inner) & (inner == 1))(copy(b, h, DOWNN).wait_send)
            copy(slot(zb, 0, y, core), h, ACROSS).wait_send()
            for p in range(2):
                for yb in (y, 1 - y):
                    copy(slot(zb, p, yb, core), h, TWIN).wait_send()
        for p in range(2):
            for yb in (y, 1 - y):
                to_twin(zb, p, yb).wait_send()
        to_pair(zb, 0).wait_send()

        @pl.when(nb != inner)
        def _():
            for kind in range(3):
                to_line(zb, kind, UPN).wait_send()

        return carry

    lax.fori_loop(0, LINE, settle, 0)


def experts_block(x, gate_w, up_w, down_w, mixed, devices):
    tokens = x.shape[0]
    half = tokens // 2
    vmem = pl.BlockSpec(memory_space=pltpu.VMEM)
    whole = pl.BlockSpec(memory_space=pl.ANY)

    def held(*lead):
        return pltpu.VMEM(lead + (half, D), jnp.bfloat16)

    dma = pltpu.SemaphoreType.DMA
    return pl.pallas_call(
        experts_kernel,
        in_specs=[whole] * 4 + [vmem],
        out_specs=vmem,
        out_shape=jax.ShapeDtypeStruct((tokens, D), jnp.bfloat16),
        scratch_shapes=[
            pltpu.VMEM((2 * devices * SUBS, half // SUBS, x.shape[1]), jnp.bfloat16),
            held(2 * devices),
            held(devices),
            held(LINE + 1),
            held(2, LINE, 3),
            pltpu.VMEM((half, D), jnp.float32),
            pltpu.VMEM(gate_w.shape, jnp.bfloat16),
            pltpu.VMEM(up_w.shape, jnp.bfloat16),
            pltpu.VMEM(down_w.shape, jnp.bfloat16),
            dma((2 * SUBS + 3,)),
            dma((2 * devices * SUBS, 4)),
            dma((2 * devices * SUBS,)),
            dma((2 * devices,)),
            dma((devices,)),
            dma((LINE + 1,)),
            dma((2, LINE, 3)),
        ],
        compiler_params=pltpu.CompilerParams(
            collective_id=1, has_side_effects=True, vmem_limit_bytes=60 << 20
        ),
    )(x, gate_w, up_w, down_w, mixed)


def grid_device(
    residual, queries, new_keys, new_values, cache_keys, cache_values, cache_len, o_weight,
    norm_gain, expert_ids, gate_raw, w_gate, w_up, w_down,
):
    devices = lax.axis_size("wide")
    shares = gate_raw / jnp.sum(gate_raw, axis=-1, keepdims=True)
    hits = expert_ids[:, :, None] == jnp.arange(devices, dtype=jnp.int32)[None, None, :]
    share_of = jnp.sum(jnp.where(hits, shares[..., None], 0.0), axis=1)
    coarse = share_of.astype(jnp.bfloat16)
    fine = (share_of - coarse.astype(jnp.float32)).astype(jnp.bfloat16)
    extra = jnp.pad(jnp.concatenate([coarse, fine], axis=1), ((0, 0), (0, EXTRA - 2 * devices)))
    mixed, rows = attention_block(
        cache_len, queries, new_keys, new_values, cache_keys, cache_values, residual,
        norm_gain.reshape(1, D), extra, o_weight, devices,
    )
    return experts_block(rows, w_gate[0], w_up[0], w_down[0], mixed, devices)


def per_device(
    residual,
    queries,
    new_keys,
    new_values,
    cache_keys,
    cache_values,
    cache_len,
    o_weight,
    norm_gain,
    expert_ids,
    gate_raw,
    w_gate,
    w_up,
    w_down,
):
    devices = lax.axis_size("wide")
    me = lax.axis_index("wide")
    length = lax.dynamic_slice_in_dim(cache_len, me, 1, 0)
    attn = attention(length, queries, new_keys, new_values, cache_keys, cache_values)
    projected = jnp.dot(
        attn,
        lax.all_gather(o_weight, "wide", axis=0, tiled=True),
        preferred_element_type=jnp.float32,
    )
    mixed = residual.astype(jnp.float32) + projected
    normed = (
        mixed * lax.rsqrt(jnp.mean(mixed * mixed, axis=-1, keepdims=True) + 1e-06) * norm_gain
    ).astype(jnp.bfloat16)
    shares = gate_raw / jnp.sum(gate_raw, axis=-1, keepdims=True)
    routed = sparse_experts(normed, expert_ids, shares, w_gate[0], w_up[0], w_down[0], devices)
    return (mixed + routed).astype(jnp.bfloat16)


def solution(mesh):
    rows = P(("groups", "wide"), None)
    blocks = P(("groups", "wide"), None, None)
    weights = P("wide", None, None)
    placed = (rows, rows, rows, rows, blocks, blocks, P("groups"), P("wide", None), P())
    placed += (rows, rows, weights, weights, weights)
    grid = mesh.shape["wide"] == LINE * PAIR * 2 and mesh.shape["groups"] == 2
    return jax.shard_map(
        grid_device if grid else per_device,
        mesh=mesh,
        in_specs=placed,
        out_specs=rows,
        check_vma=False,
    )
```

```python
import functools
import jax
import jax.numpy as jnp
from jax import lax
from jax.experimental import pallas as pl
from jax.experimental.pallas import tpu as pltpu
from jax.sharding import PartitionSpec as P

D = 2048
HEADS = 16
KV_HEADS = 2
HEAD = 128
TOPK = 8
SPAN = 128
PACK = 2
EXP2_SCALE = HEAD ** (-0.5) * 1.4426950408889634


def attention_kernel(length_ref, q_ref, nk_ref, nv_ref, k_ref, v_ref, out_ref):
    tokens = q_ref.shape[0]
    rows = PACK * tokens
    cache = k_ref.shape[1]
    q = jnp.concatenate([q_ref[:, i * HEAD : (i + 1) * HEAD] for i in range(PACK)], axis=0)
    dims = (((1,), (1,)), ((), ()))
    s = lax.dot_general(q, k_ref[0], dims, preferred_element_type=jnp.float32)
    position = lax.broadcasted_iota(jnp.int32, (1, cache), 1)
    s = jnp.where(position < length_ref[0], s, jnp.float32(-1e30))
    s_new = lax.dot_general(q, nk_ref[...], dims, preferred_element_type=jnp.float32)
    row = lax.broadcasted_iota(jnp.int32, (rows, tokens), 0) % tokens
    column = lax.broadcasted_iota(jnp.int32, (rows, tokens), 1)
    s_new = jnp.where(column <= row, s_new, jnp.float32(-1e30))
    top = jnp.maximum(jnp.max(s, axis=1, keepdims=True), jnp.max(s_new, axis=1, keepdims=True))
    w = jnp.exp2((s - top) * EXP2_SCALE)
    w_new = jnp.exp2((s_new - top) * EXP2_SCALE)
    total = jnp.sum(w, axis=1, keepdims=True) + jnp.sum(w_new, axis=1, keepdims=True)
    out = jnp.dot(w.astype(jnp.bfloat16), v_ref[0], preferred_element_type=jnp.float32)
    out += jnp.dot(w_new.astype(jnp.bfloat16), nv_ref[...], preferred_element_type=jnp.float32)
    out = (out / total).astype(out_ref.dtype)
    for i in range(PACK):
        out_ref[:, i * HEAD : (i + 1) * HEAD] = out[i * tokens : (i + 1) * tokens]


def attention(length, queries, new_keys, new_values, cache_keys, cache_values):
    tokens, width = queries.shape
    cache = cache_keys.shape[1]
    per_group = HEADS // KV_HEADS // PACK
    return pl.pallas_call(
        attention_kernel,
        grid=(HEADS // PACK,),
        in_specs=[
            pl.BlockSpec(memory_space=pltpu.SMEM),
            pl.BlockSpec((tokens, PACK * HEAD), lambda i: (0, i)),
            pl.BlockSpec((tokens, HEAD), lambda i: (0, i // per_group)),
            pl.BlockSpec((tokens, HEAD), lambda i: (0, i // per_group)),
            pl.BlockSpec((1, cache, HEAD), lambda i: (0, 0, i // per_group)),
            pl.BlockSpec((1, cache, HEAD), lambda i: (0, 0, i // per_group)),
        ],
        out_specs=pl.BlockSpec((tokens, PACK * HEAD), lambda i: (0, i)),
        out_shape=jax.ShapeDtypeStruct((tokens, width), jnp.bfloat16),
        cost_estimate=pl.CostEstimate(
            flops=4 * tokens * width * (cache + tokens),
            bytes_accessed=4 * cache * KV_HEADS * HEAD + 4 * tokens * width,
            transcendentals=tokens * HEADS * (cache + tokens),
        ),
    )(length, queries, new_keys, new_values, cache_keys, cache_values)


def run_expert(rows_in, gate_w, up_w, down_w):
    gate_part = jnp.dot(rows_in, gate_w, preferred_element_type=jnp.float32)
    up_part = jnp.dot(rows_in, up_w, preferred_element_type=jnp.float32)
    activated = (jax.nn.silu(gate_part) * up_part).astype(jnp.bfloat16)
    return jnp.dot(activated, down_w, preferred_element_type=jnp.float32)


def sparse_experts(normed, expert_ids, shares, gate_w, up_w, down_w, devices):
    token_count = normed.shape[0]
    capacity = SPAN * TOPK // devices + max(2, SPAN * TOPK // (8 * devices))
    flat_ids = expert_ids.reshape(-1)
    named = expert_ids[:, :, None] == jnp.arange(devices, dtype=jnp.int32)[None, None, :]
    earlier = jnp.tril(jnp.ones((token_count, token_count), jnp.bfloat16), -1)
    before = jnp.dot(
        earlier, jnp.any(named, axis=1).astype(jnp.bfloat16), preferred_element_type=jnp.float32
    )
    ranks = jnp.sum(jnp.where(named, before[:, None, :], 0.0), axis=-1)
    ranks = ranks.astype(jnp.int32).reshape(-1)
    slot_index = flat_ids * capacity + ranks
    token_of = jnp.arange(flat_ids.shape[0], dtype=jnp.int32) // TOPK
    slot_token = (
        jnp.full((devices * capacity,), token_count, jnp.int32).at[slot_index].set(token_of)
    )
    padded = jnp.concatenate([normed, jnp.zeros((1, D), jnp.bfloat16)], axis=0)
    outgoing = padded[slot_token].reshape(devices, capacity, D)
    arrived = lax.all_to_all(outgoing, "wide", split_axis=0, concat_axis=0, tiled=True)
    served = run_expert(arrived.reshape(-1, D), gate_w, up_w, down_w).astype(jnp.bfloat16)
    served = served.reshape(devices, capacity, D)
    returned_rows = lax.all_to_all(served, "wide", split_axis=0, concat_axis=0, tiled=True)
    picked = returned_rows.reshape(devices * capacity, D)[slot_index].reshape(token_count, TOPK, D)
    return jnp.sum(picked.astype(jnp.float32) * shares[..., None], axis=1)


LINE = 4
PAIR = 2
DOWN, UP, ACROSS, TWIN = range(4)


def attend(q, key, value, new_key, new_value, length, tokens):
    rows = q.shape[0]
    dims = (((1,), (1,)), ((), ()))
    s = lax.dot_general(q, key, dims, preferred_element_type=jnp.float32)
    position = lax.broadcasted_iota(jnp.int32, (1, key.shape[0]), 1)
    s = jnp.where(position < length, s, jnp.float32(-1e30))
    s_new = lax.dot_general(q, new_key, dims, preferred_element_type=jnp.float32)
    row = lax.broadcasted_iota(jnp.int32, (rows, tokens), 0) % tokens
    column = lax.broadcasted_iota(jnp.int32, (rows, tokens), 1)
    s_new = jnp.where(column <= row, s_new, jnp.float32(-1e30))
    top = jnp.maximum(jnp.max(s, axis=1, keepdims=True), jnp.max(s_new, axis=1, keepdims=True))
    w = jnp.exp2((s - top) * EXP2_SCALE)
    w_new = jnp.exp2((s_new - top) * EXP2_SCALE)
    total = jnp.sum(w, axis=1, keepdims=True) + jnp.sum(w_new, axis=1, keepdims=True)
    out = jnp.dot(w.astype(jnp.bfloat16), value, preferred_element_type=jnp.float32)
    out += jnp.dot(w_new.astype(jnp.bfloat16), new_value, preferred_element_type=jnp.float32)
    return (out / total).astype(jnp.bfloat16)


class Place:
    def __init__(self):
        self.me = lax.axis_index("wide")
        self.core = self.me % 2
        self.y = (self.me // 2) % PAIR
        self.z = self.me // (2 * PAIR)

    def block(self, z, y, core):
        return (z * PAIR + y) * 2 + core

    def towards(self, way):
        z, y, core = self.z, self.y, self.core
        if way == DOWN:
            return self.block(z - 1, y, core)
        if way == UP:
            return self.block(z + 1, y, core)
        if way == ACROSS:
            return self.block(z, 1 - y, core)
        return self.block(z, y, 1 - core)

    def line_at(self, i):
        low = self.z < LINE // 2
        inner = jnp.where(low, self.z, LINE - 1 - self.z)
        near = jnp.where((inner == 0) | (i >= 2), i, 1 - i)
        return jnp.where(low, near, LINE - 1 - near)

    def barrier(self, with_x=False):
        sem = pltpu.get_barrier_semaphore()

        def greet(way):
            pl.semaphore_signal(
                sem,
                inc=1,
                device_id={"wide": self.towards(way)},
                device_id_type=pl.DeviceIdType.MESH,
            )

        pl.when(self.z > 0)(lambda: greet(DOWN))
        pl.when(self.z < LINE - 1)(lambda: greet(UP))
        greet(ACROSS)
        greet(TWIN)
        if with_x:
            pl.semaphore_signal(
                sem, inc=1, device_id={"groups": 1 - lax.axis_index("groups")},
                device_id_type=pl.DeviceIdType.MESH,
            )
        ends = jnp.where((self.z == 0) | (self.z == LINE - 1), 1, 0)
        pl.semaphore_wait(sem, (5 if with_x else 4) - ends)


UPN, DOWNN = 0, 1
XWAY = 4
TILE = 16
P0, P1, PR, Q0, Q1, QS = range(6)
A_SLOTS = 6
SHARE_ROWS = 32


def gather_events(*items):
    codes = [kind * 4 + nb for kind, nb in items]
    codes += [31] * (A_SLOTS - len(codes))
    return sum(c << (5 * j) for j, c in enumerate(codes))


A_END = (
    gather_events(), gather_events(), gather_events(),
    gather_events((Q0, 0), (P0, 1)),
    gather_events((Q1, 0)),
    gather_events((P1, 1)),
    gather_events((QS, 0), (Q0, 1)),
    gather_events((P0, 2), (PR, 1), (Q1, 1)),
    gather_events((P1, 2), (QS, 1)),
    gather_events((Q0, 2), (PR, 2), (P0, 3)),
    gather_events((Q1, 2), (QS, 2)),
    gather_events((P1, 3), (Q0, 3), (PR, 3), (Q1, 3), (QS, 3)),
)
A_INNER = (
    gather_events(), gather_events(), gather_events(),
    gather_events((Q0, 1), (P0, 0), (P0, 2)),
    gather_events((Q1, 1)),
    gather_events((P1, 0), (P1, 2)),
    gather_events((QS, 1), (Q0, 0)),
    gather_events((P0, 3), (PR, 0), (PR, 2)),
    gather_events((Q0, 2), (P1, 3)),
    gather_events((Q1, 0), (QS, 0)),
    gather_events((Q1, 2), (QS, 2)),
    gather_events((Q0, 3), (PR, 3), (Q1, 3), (QS, 3)),
)


def pick(index, inner, ends, inners):
    at_end, at_inner = jnp.int32(ends[0]), jnp.int32(inners[0])
    for k in range(1, len(ends)):
        at_end = jnp.where(index == k, jnp.int32(ends[k]), at_end)
        at_inner = jnp.where(index == k, jnp.int32(inners[k]), at_inner)
    return jnp.where(inner == 1, at_inner, at_end)


PIECES = "abcd"
GET, UP_OWN, DOWN_OWN, PASS_OWN, SERVE, PAIR_UP, FOLD, FINISH = range(8)
KINDS = {"g": GET, "u": UP_OWN, "d": DOWN_OWN, "y": PASS_OWN}
KINDS.update({"s": SERVE, "p": PAIR_UP, "f": FOLD, "z": FINISH})
PA, PB, PC, PD = range(4)
B_END = (
    "uc", "ua", "ya", "yc", "g0b", "ub", "g1b", "g1a", "s11", "g3c", "g0d", "s00",
    "g3d", "g3a", "f11", "s30", "f12", "g3b", "p0", "p3", "s31", "f32", "f31", "s01",
    "g2c", "g2a", "f30", "g2b", "s21", "g2d", "g1c", "f22", "s20", "f21", "g1d", "p2",
    "s10", "p1", "f20", "z2", "f10", "z0", "z1",
)
B_INNER = (
    "ya", "uc", "da", "g0c", "g1b", "db", "g0a", "yc", "g3c", "g0b", "g3a", "s11",
    "ua", "g0d", "g3b", "g2c", "g1d", "s31", "ub", "g2a", "g3d", "s30", "s00", "g2b",
    "p3", "dc", "s10", "p0", "f32", "s21", "f31", "p1", "s01", "g2d", "f30", "f02",
    "s20", "f22", "p2", "f01", "f21", "f00", "z2", "f20", "z1", "z0",
)


def code_of(text):
    kind = KINDS[text[0]]
    if kind == GET:
        return kind * 16 + int(text[1]) * 4 + PIECES.index(text[2])
    if kind in (UP_OWN, DOWN_OWN, PASS_OWN):
        return kind * 16 + PIECES.index(text[1])
    if kind == PAIR_UP:
        return kind * 16 + int(text[1]) * 4
    if kind == FINISH:
        return kind * 16 + int(text[1])
    return kind * 16 + int(text[1]) * 4 + int(text[2])


def packed(program, words):
    codes = [code_of(text) for text in program]
    codes += [127] * (4 * words - len(codes))
    return [sum(c << (7 * j) for j, c in enumerate(codes[4 * w : 4 * w + 4])) for w in range(words)]


def first_serve(program):
    return [text[0] for text in program].index("s")


def layer_kernel(
    length_ref, q_ref, nk_ref, nv_ref, k_ref, v_ref, res_ref, gain_ref, share_ref, ow_ref,
    wg_ref, wu_ref, wd_ref, out_ref,
    held, attn, mixed_ref, share_tab, share_col, rows, part, from_twin, from_pair, from_line, acc,
    wg, wu, wd, own_sem, load_sem, send_sem, recv_sem, share_send, share_recv,
    row_send, row_recv, back_send, twin_sem, pair_sem, line_sem,
):
    place = Place()
    z, y, core = place.z, place.y, place.core
    group = lax.axis_index("groups")
    tokens = q_ref.shape[0]
    depth = ow_ref.shape[0]
    low = z < LINE // 2
    inner = jnp.where(low, z, LINE - 1 - z)
    step_up = jnp.where(low, 1, -1)
    own = pltpu.make_async_copy(ow_ref, held.at[place.me], own_sem)
    own.start()
    loads = [
        pltpu.make_async_copy(source, dest, load_sem.at[k])
        for k, (source, dest) in enumerate(((wg_ref, wg), (wu_ref, wu), (wd_ref, wd)))
    ]
    for load in loads:
        load.start()
    share_tab[place.me] = share_ref[...]
    place.barrier(True)
    own.wait()

    third = depth // 8 * 2
    half = depth // 8 * 3
    last = depth - half
    span = {
        P0: (jnp.where(group == 0, 0, last), half),
        P1: (jnp.where(group == 0, half, third), half),
        PR: (jnp.where(group == 0, depth - third, 0), third),
        Q0: (jnp.where(group == 0, 0, last), half),
        Q1: (half, depth - 2 * half),
        QS: (jnp.where(group == 0, last, 0), half),
    }
    given = {PR: (jnp.where(group == 0, 0, depth - third), third), QS: span[Q0]}

    def real(nb):
        return jnp.where(low, nb, LINE - 1 - nb)

    def device(way):
        if way == XWAY:
            return {"groups": 1 - group}
        if way == UPN:
            return {"wide": place.block(z + step_up, y, core)}
        if way == DOWNN:
            return {"wide": place.block(z - step_up, y, core)}
        return {"wide": place.towards(way)}

    def copy(b, what, way):
        start, size = given[what] if way == XWAY else span[what]
        if not isinstance(start, int):
            start = pl.multiple_of(start, TILE)
        ref = held.at[b, pl.ds(start, size)]
        i = what % 3
        return pltpu.make_async_remote_copy(
            src_ref=ref, dst_ref=ref, send_sem=send_sem.at[b, i, way], recv_sem=recv_sem.at[b, i],
            device_id=device(way), device_id_type=pl.DeviceIdType.MESH,
        )

    def whole(b):
        return pltpu.make_async_remote_copy(
            src_ref=held.at[b], dst_ref=held.at[b], send_sem=send_sem.at[b, 2, TWIN],
            recv_sem=recv_sem.at[b, 0], device_id=device(TWIN),
            device_id_type=pl.DeviceIdType.MESH,
        )

    def share_copy(b, way):
        return pltpu.make_async_remote_copy(
            src_ref=share_tab.at[b], dst_ref=share_tab.at[b], send_sem=share_send.at[b, way],
            recv_sem=share_recv.at[b], device_id=device(way),
            device_id_type=pl.DeviceIdType.MESH,
        )

    def block_at(nb, yb, c):
        return place.block(real(nb), yb, c)

    me = place.me
    copy(me, P0, UPN).start()
    pl.when(inner == 1)(copy(me, P0, DOWNN).start)
    copy(me, Q0, ACROSS).start()
    copy(me, P1, UPN).start()
    pl.when(inner == 1)(copy(me, P1, DOWNN).start)
    copy(me, Q1, ACROSS).start()
    whole(me).start()
    share_copy(me, UPN).start()
    pl.when(inner == 1)(share_copy(me, DOWNN).start)
    share_copy(me, ACROSS).start()
    share_copy(me, TWIN).start()

    def happen(code):
        nb = lax.rem(code, 4)
        kind = code // 4
        own_b = block_at(nb, y, core)
        other_b = block_at(nb, 1 - y, core)

        def line(what):
            pl.when(nb < inner)(copy(own_b, what, UPN).start)
            pl.when((nb > inner) & (inner == 1))(copy(own_b, what, DOWNN).start)

        @pl.when(kind == P0)
        def _():
            copy(own_b, P0, TWIN).wait_recv()
            line(P0)
            copy(own_b, Q0, ACROSS).start()
            copy(own_b, PR, XWAY).start()
            copy(own_b, P0, TWIN).start()
            share_copy(own_b, TWIN).wait_recv()
            pl.when(nb < inner)(share_copy(own_b, UPN).start)
            pl.when((nb > inner) & (inner == 1))(share_copy(own_b, DOWNN).start)
            share_copy(own_b, ACROSS).start()
            share_copy(own_b, TWIN).start()

        @pl.when(kind == P1)
        def _():
            copy(own_b, P1, TWIN).wait_recv()
            line(P1)
            copy(own_b, Q1, ACROSS).start()
            copy(own_b, P1, TWIN).start()

        @pl.when(kind == PR)
        def _():
            copy(own_b, PR, TWIN).wait_recv()
            copy(own_b, PR, TWIN).start()

        @pl.when(kind == Q0)
        def _():
            copy(other_b, Q0, TWIN).wait_recv()
            copy(other_b, QS, XWAY).start()
            copy(other_b, Q0, TWIN).start()
            share_copy(other_b, TWIN).wait_recv()
            share_copy(other_b, TWIN).start()

        @pl.when(kind == Q1)
        def _():
            copy(other_b, Q1, TWIN).wait_recv()
            copy(other_b, Q1, TWIN).start()

        @pl.when(kind == QS)
        def _():
            copy(other_b, QS, TWIN).wait_recv()
            copy(other_b, QS, TWIN).start()

    length = length_ref[place.me]
    attends = HEADS // PACK
    per_group = HEADS // KV_HEADS // PACK

    def attend_step(i):
        q = jnp.concatenate(
            [
                q_ref[:, pl.ds(pl.multiple_of((i * PACK + j) * HEAD, HEAD), HEAD)]
                for j in range(PACK)
            ],
            axis=0,
        )
        columns = pl.ds(pl.multiple_of(i // per_group * HEAD, HEAD), HEAD)
        out = attend(
            q, k_ref[0, :, columns], v_ref[0, :, columns], nk_ref[:, columns],
            nv_ref[:, columns], length, tokens,
        )
        for j in range(PACK):
            attn[:, pl.ds(pl.multiple_of((i * PACK + j) * HEAD, HEAD), HEAD)] = out[
                j * tokens : (j + 1) * tokens
            ]

    mixed_ref[...] = res_ref[...].astype(jnp.float32)
    lane = lax.broadcasted_iota(jnp.int32, (1, SHARE_ROWS), 1)
    chosen = (lane == me) | (lane == me + SHARE_ROWS // 2)

    def project(nb, is_own):
        yb = jnp.where(is_own, y, 1 - y)
        b = block_at(nb, yb, 1 - core)

        @pl.when(is_own & (nb == inner))
        def _():
            whole(b).wait_recv()

        @pl.when(is_own & (nb != inner))
        def _():
            for what in (P0, P1, PR):
                copy(b, what, TWIN).wait_recv()

        @pl.when(jnp.logical_not(is_own))
        def _():
            for what in (Q0, Q1, QS):
                copy(b, what, TWIN).wait_recv()

        share_copy(b, TWIN).wait_recv()
        first = block_at(nb, yb, 0)
        for c in range(2):
            turned = share_tab[first + c].astype(jnp.float32).T
            column = jnp.sum(jnp.where(chosen, turned, 0.0), axis=1, keepdims=True)
            share_col[first + c] = jnp.broadcast_to(column, share_col.shape[1:])
        mine = attn[:, pl.ds(pl.multiple_of(first * depth, 2 * depth), 2 * depth)]
        weight = held[pl.ds(first, 2)].reshape(2 * depth, D)
        mixed_ref[...] += jnp.dot(mine, weight, preferred_element_type=jnp.float32)

    def step(s, carry):
        def one(j, word):
            code = lax.rem(word, 32)
            pl.when(code < 31)(lambda: happen(code))
            return word // 32

        lax.fori_loop(0, A_SLOTS, one, pick(s, inner, A_END, A_INNER))
        pl.when(s < attends)(lambda: attend_step(s))

        @pl.when(s >= attends)
        def _():
            nb = pick(s - attends, inner, (0, 1, 2, 3), (1, 0, 2, 3))

            def both(k, inside):
                project(nb, k == 0)
                return inside

            lax.fori_loop(0, 2, both, 0)

        return carry

    lax.fori_loop(0, len(A_END), step, 0)
    half_rows = tokens // 2
    mixed = mixed_ref[...]
    scale = lax.rsqrt(jnp.mean(mixed * mixed, axis=-1, keepdims=True) + 1e-06)
    normed = (mixed * scale * gain_ref[...]).astype(jnp.bfloat16)

    def slot(zb, p, yb, c):
        return ((zb * 2 + p) * PAIR + yb) * 2 + c

    for p in range(2):
        rows[slot(z, p, y, core)] = normed[p * half_rows : (p + 1) * half_rows]

    def send(source, dest, send_one, recv_one, way):
        return pltpu.make_async_remote_copy(
            src_ref=source, dst_ref=dest, send_sem=send_one, recv_sem=recv_one,
            device_id=device(way), device_id_type=pl.DeviceIdType.MESH,
        )

    def row_copy(b, way):
        return send(rows.at[b], rows.at[b], row_send.at[b, way], row_recv.at[b], way)

    def to_twin(zb, p, yb):
        b = slot(zb, p, yb, 1 - core)
        t = (zb * 2 + p) * PAIR + yb
        return send(part.at[b], from_twin.at[t], back_send.at[b], twin_sem.at[t], TWIN)

    def to_pair(zb, p):
        b = slot(zb, p, 1 - y, core)
        t = LINE if p else zb
        return send(part.at[b], from_pair.at[t], back_send.at[b], pair_sem.at[t], ACROSS)

    def kind_slot(zb, kind):
        p = jnp.minimum(kind, 1)
        yb = jnp.where(kind == 2, 1 - y, y)
        return p, yb, slot(zb, p, yb, core)

    side_up = jnp.where(low, 0, 1)

    def to_line(zb, kind, way):
        b = kind_slot(zb, kind)[2]
        side = side_up if way == UPN else 1 - side_up
        return send(
            part.at[b], from_line.at[side, zb, kind], back_send.at[b],
            line_sem.at[side, zb, kind], way,
        )

    def serve(zb, p):
        for yb in range(2):
            row_copy(slot(zb, p, yb, 1 - core), TWIN).wait_recv()
        first = slot(zb, p, 0, 0)
        x = rows[pl.ds(first, 4)].reshape(4 * half_rows, D)
        here = pl.ds(pl.multiple_of(p * half_rows, half_rows), half_rows)
        share = share_col[pl.ds(place.block(zb, 0, 0), 4), here].reshape(4 * half_rows, HEAD)
        gate = jnp.dot(x, wg[...], preferred_element_type=jnp.float32)
        up = jnp.dot(x, wu[...], preferred_element_type=jnp.float32)
        act = (gate / (1.0 + jnp.exp(-gate)) * up).astype(jnp.bfloat16)
        out = jnp.dot(act, wd[...], preferred_element_type=jnp.float32) * share[:, :1]
        part[pl.ds(first, 4)] = out.astype(jnp.bfloat16).reshape(4, half_rows, D)
        to_twin(zb, p, 0).start()
        to_twin(zb, p, 1).start()

    def with_twin(zb, p, yb):
        to_twin(zb, p, yb).wait_recv()
        b = slot(zb, p, yb, core)
        t = (zb * 2 + p) * PAIR + yb
        return part[b].astype(jnp.float32) + from_twin[t].astype(jnp.float32)

    def add_line(zb, kind, way):
        to_line(zb, kind, way).wait_recv()
        side = side_up if way == UPN else 1 - side_up
        acc[...] += from_line[side, zb, kind].astype(jnp.float32)

    def fold(nb, kind):
        zb = real(nb)
        p, yb, b = kind_slot(zb, kind)
        acc[...] = with_twin(zb, p, yb)

        @pl.when(kind == 0)
        def _():
            to_pair(zb, 0).wait_recv()
            acc[...] += from_pair[zb].astype(jnp.float32)

        pl.when((nb > inner) & (inner == 1))(lambda: add_line(zb, kind, UPN))
        pl.when(nb < inner)(lambda: add_line(zb, kind, DOWNN))
        part[b] = acc[...].astype(jnp.bfloat16)
        pl.when(nb > inner)(to_line(zb, kind, UPN).start)
        pl.when(nb < inner)(to_line(zb, kind, DOWNN).start)

    def finish(kind):
        p, yb, b = kind_slot(z, kind)
        acc[...] = with_twin(z, p, yb)
        pl.when(inner == 1)(lambda: add_line(z, kind, UPN))
        add_line(z, kind, DOWNN)

        @pl.when(kind == 2)
        def _():
            part[b] = acc[...].astype(jnp.bfloat16)
            to_pair(z, 1).start()

        def close(p, t):
            here = pl.ds(p * half_rows, half_rows)
            to_pair(z, p).wait_recv()
            out_ref[here] = (
                acc[...] + mixed_ref[here] + from_pair[t].astype(jnp.float32)
            ).astype(jnp.bfloat16)

        pl.when(kind == 0)(lambda: close(0, z))
        pl.when(kind == 1)(lambda: close(1, LINE))

    def act_on(code, first):
        kind = code // 16
        nb = lax.rem(code // 4, 4)
        piece = lax.rem(code, 4)
        zb = real(nb)
        p = jnp.where(piece <= PB, 1, 0)
        yb = jnp.where((piece == PA) | (piece == PC), y, 1 - y)
        own_piece = slot(z, p, yb, core)

        @pl.when(kind == GET)
        def _():
            b = slot(zb, p, yb, core)
            row_copy(b, TWIN).wait_recv()
            onward = piece != PD
            pl.when(onward & (nb < inner))(row_copy(b, UPN).start)
            pl.when(onward & (nb > inner) & (inner == 1))(row_copy(b, DOWNN).start)
            pl.when((piece == PC) & (nb != inner))(row_copy(b, ACROSS).start)
            row_copy(b, TWIN).start()

        pl.when(kind == UP_OWN)(row_copy(own_piece, UPN).start)
        pl.when(kind == DOWN_OWN)(row_copy(own_piece, DOWNN).start)

        @pl.when(kind == PASS_OWN)
        def _():
            row_copy(own_piece, ACROSS).start()
            row_copy(own_piece, TWIN).start()

        @pl.when(kind == SERVE)
        def _():
            @pl.when(first)
            def _():
                for load in loads:
                    load.wait()

            serve(zb, piece)

        @pl.when(kind == PAIR_UP)
        def _():
            part[slot(zb, 0, 1 - y, core)] = with_twin(zb, 0, 1 - y).astype(jnp.bfloat16)
            to_pair(zb, 0).start()

        pl.when(kind == FOLD)(lambda: fold(nb, piece))
        pl.when((kind == FINISH) & (piece < 3))(lambda: finish(piece))

    words = -(-max(len(B_END), len(B_INNER)) // 4)
    end_words, inner_words = packed(B_END, words), packed(B_INNER, words)
    serve_at = jnp.where(inner == 1, first_serve(B_INNER), first_serve(B_END))

    def route(w, carry):
        def one(j, word):
            act_on(lax.rem(word, 128), w * 4 + j == serve_at)
            return word // 128

        lax.fori_loop(0, 4, one, pick(w, inner, end_words, inner_words))
        return carry

    lax.fori_loop(0, words, route, 0)

    def settle_rows(nb, carry):
        zb = real(nb)
        for p, yb in ((0, y), (1, y), (1, 1 - y)):
            b = slot(zb, p, yb, core)
            pl.when(nb <= inner)(row_copy(b, UPN).wait_send)
            pl.when((nb >= inner) & (inner == 1))(row_copy(b, DOWNN).wait_send)
        row_copy(slot(zb, 0, y, core), ACROSS).wait_send()
        pl.when(nb == inner)(row_copy(slot(zb, 1, y, core), ACROSS).wait_send)
        for p in range(2):
            for yb in (y, 1 - y):
                row_copy(slot(zb, p, yb, core), TWIN).wait_send()
                to_twin(zb, p, yb).wait_send()
        to_pair(zb, 0).wait_send()
        pl.when(nb == inner)(to_pair(zb, 1).wait_send)

        @pl.when(nb != inner)
        def _():
            for kind in range(3):
                to_line(zb, kind, UPN).wait_send()

        return carry

    lax.fori_loop(0, LINE, settle_rows, 0)

    def settle_weights(nb, carry):
        own_b = block_at(nb, y, core)
        other_b = block_at(nb, 1 - y, core)
        for what in (P0, P1):
            pl.when(nb <= inner)(copy(own_b, what, UPN).wait_send)
            pl.when((nb >= inner) & (inner == 1))(copy(own_b, what, DOWNN).wait_send)
        pl.when(nb <= inner)(share_copy(own_b, UPN).wait_send)
        pl.when((nb >= inner) & (inner == 1))(share_copy(own_b, DOWNN).wait_send)
        share_copy(own_b, ACROSS).wait_send()
        share_copy(own_b, TWIN).wait_send()
        share_copy(other_b, TWIN).wait_send()
        copy(own_b, Q0, ACROSS).wait_send()
        copy(own_b, Q1, ACROSS).wait_send()

        @pl.when(nb == inner)
        def _():
            whole(own_b).wait_send()

        @pl.when(nb != inner)
        def _():
            copy(own_b, PR, XWAY).wait_send()
            for what in (P0, P1, PR):
                copy(own_b, what, TWIN).wait_send()

        copy(other_b, QS, XWAY).wait_send()
        for what in (Q0, Q1, QS):
            copy(other_b, what, TWIN).wait_send()
        return carry

    lax.fori_loop(0, LINE, settle_weights, 0)


def layer(
    cache_len, queries, new_keys, new_values, cache_keys, cache_values, residual, gain, shares,
    o_weight, gate_w, up_w, down_w, devices,
):
    tokens, width = queries.shape
    half = tokens // 2
    vmem = pl.BlockSpec(memory_space=pltpu.VMEM)
    whole = pl.BlockSpec(memory_space=pl.ANY)
    dma = pltpu.SemaphoreType.DMA

    def held(*lead):
        return pltpu.VMEM(lead + (half, D), jnp.bfloat16)

    return pl.pallas_call(
        layer_kernel,
        in_specs=[pl.BlockSpec(memory_space=pltpu.SMEM)] + [vmem] * 8 + [whole] * 4,
        out_specs=vmem,
        out_shape=jax.ShapeDtypeStruct((tokens, D), jnp.bfloat16),
        scratch_shapes=[
            pltpu.VMEM((devices,) + o_weight.shape, jnp.bfloat16),
            pltpu.VMEM((tokens, width), jnp.bfloat16),
            pltpu.VMEM((tokens, D), jnp.float32),
            pltpu.VMEM((devices,) + shares.shape, jnp.bfloat16),
            pltpu.VMEM((devices, tokens, HEAD), jnp.float32),
            held(2 * devices),
            held(2 * devices),
            held(devices),
            held(LINE + 1),
            held(2, LINE, 3),
            pltpu.VMEM((half, D), jnp.float32),
            pltpu.VMEM(gate_w.shape, jnp.bfloat16),
            pltpu.VMEM(up_w.shape, jnp.bfloat16),
            pltpu.VMEM(down_w.shape, jnp.bfloat16),
            dma,
            dma((3,)),
            dma((devices, 3, 5)),
            dma((devices, 3)),
            dma((devices, 4)),
            dma((devices,)),
            dma((2 * devices, 4)),
            dma((2 * devices,)),
            dma((2 * devices,)),
            dma((devices,)),
            dma((LINE + 1,)),
            dma((2, LINE, 3)),
        ],
        compiler_params=pltpu.CompilerParams(
            collective_id=0, has_side_effects=True, vmem_limit_bytes=63 << 20
        ),
    )(
        cache_len, queries, new_keys, new_values, cache_keys, cache_values, residual, gain, shares,
        o_weight, gate_w, up_w, down_w,
    )


def grid_device(
    residual, queries, new_keys, new_values, cache_keys, cache_values, cache_len, o_weight,
    norm_gain, expert_ids, gate_raw, w_gate, w_up, w_down,
):
    devices = lax.axis_size("wide")
    parts = gate_raw / jnp.sum(gate_raw, axis=-1, keepdims=True)
    hits = expert_ids[:, :, None] == jnp.arange(devices, dtype=jnp.int32)[None, None, :]
    share_of = jnp.sum(jnp.where(hits, parts[..., None], 0.0), axis=1)
    coarse = share_of.astype(jnp.bfloat16)
    fine = (share_of - coarse.astype(jnp.float32)).astype(jnp.bfloat16)
    shares = jnp.concatenate([coarse, fine], axis=1).T
    return layer(
        cache_len, queries, new_keys, new_values, cache_keys, cache_values, residual,
        norm_gain.reshape(1, D), shares, o_weight, w_gate[0], w_up[0], w_down[0], devices,
    )


def per_device(
    residual,
    queries,
    new_keys,
    new_values,
    cache_keys,
    cache_values,
    cache_len,
    o_weight,
    norm_gain,
    expert_ids,
    gate_raw,
    w_gate,
    w_up,
    w_down,
):
    devices = lax.axis_size("wide")
    me = lax.axis_index("wide")
    length = lax.dynamic_slice_in_dim(cache_len, me, 1, 0)
    attn = attention(length, queries, new_keys, new_values, cache_keys, cache_values)
    projected = jnp.dot(
        attn,
        lax.all_gather(o_weight, "wide", axis=0, tiled=True),
        preferred_element_type=jnp.float32,
    )
    mixed = residual.astype(jnp.float32) + projected
    normed = (
        mixed * lax.rsqrt(jnp.mean(mixed * mixed, axis=-1, keepdims=True) + 1e-06) * norm_gain
    ).astype(jnp.bfloat16)
    shares = gate_raw / jnp.sum(gate_raw, axis=-1, keepdims=True)
    routed = sparse_experts(normed, expert_ids, shares, w_gate[0], w_up[0], w_down[0], devices)
    return (mixed + routed).astype(jnp.bfloat16)


def solution(mesh):
    rows = P(("groups", "wide"), None)
    blocks = P(("groups", "wide"), None, None)
    weights = P("wide", None, None)
    placed = (rows, rows, rows, rows, blocks, blocks, P("groups"), P("wide", None), P())
    placed += (rows, rows, weights, weights, weights)
    grid = mesh.shape["wide"] == LINE * PAIR * 2 and mesh.shape["groups"] == 2
    return jax.shard_map(
        grid_device if grid else per_device,
        mesh=mesh,
        in_specs=placed,
        out_specs=rows,
        check_vma=False,
    )
```

```python
import functools
import jax
import jax.numpy as jnp
from jax import lax
from jax.experimental import pallas as pl
from jax.experimental.pallas import tpu as pltpu
from jax.sharding import PartitionSpec as P

D = 2048
HEADS = 16
KV_HEADS = 2
HEAD = 128
TOPK = 8
SPAN = 128
PACK = 2
EXP2_SCALE = HEAD ** (-0.5) * 1.4426950408889634


def attention_kernel(length_ref, q_ref, nk_ref, nv_ref, k_ref, v_ref, out_ref):
    tokens = q_ref.shape[0]
    rows = PACK * tokens
    cache = k_ref.shape[1]
    q = jnp.concatenate([q_ref[:, i * HEAD : (i + 1) * HEAD] for i in range(PACK)], axis=0)
    dims = (((1,), (1,)), ((), ()))
    s = lax.dot_general(q, k_ref[0], dims, preferred_element_type=jnp.float32)
    position = lax.broadcasted_iota(jnp.int32, (1, cache), 1)
    s = jnp.where(position < length_ref[0], s, jnp.float32(-1e30))
    s_new = lax.dot_general(q, nk_ref[...], dims, preferred_element_type=jnp.float32)
    row = lax.broadcasted_iota(jnp.int32, (rows, tokens), 0) % tokens
    column = lax.broadcasted_iota(jnp.int32, (rows, tokens), 1)
    s_new = jnp.where(column <= row, s_new, jnp.float32(-1e30))
    top = jnp.maximum(jnp.max(s, axis=1, keepdims=True), jnp.max(s_new, axis=1, keepdims=True))
    w = jnp.exp2((s - top) * EXP2_SCALE)
    w_new = jnp.exp2((s_new - top) * EXP2_SCALE)
    total = jnp.sum(w, axis=1, keepdims=True) + jnp.sum(w_new, axis=1, keepdims=True)
    out = jnp.dot(w.astype(jnp.bfloat16), v_ref[0], preferred_element_type=jnp.float32)
    out += jnp.dot(w_new.astype(jnp.bfloat16), nv_ref[...], preferred_element_type=jnp.float32)
    out = (out / total).astype(out_ref.dtype)
    for i in range(PACK):
        out_ref[:, i * HEAD : (i + 1) * HEAD] = out[i * tokens : (i + 1) * tokens]


def attention(length, queries, new_keys, new_values, cache_keys, cache_values):
    tokens, width = queries.shape
    cache = cache_keys.shape[1]
    per_group = HEADS // KV_HEADS // PACK
    return pl.pallas_call(
        attention_kernel,
        grid=(HEADS // PACK,),
        in_specs=[
            pl.BlockSpec(memory_space=pltpu.SMEM),
            pl.BlockSpec((tokens, PACK * HEAD), lambda i: (0, i)),
            pl.BlockSpec((tokens, HEAD), lambda i: (0, i // per_group)),
            pl.BlockSpec((tokens, HEAD), lambda i: (0, i // per_group)),
            pl.BlockSpec((1, cache, HEAD), lambda i: (0, 0, i // per_group)),
            pl.BlockSpec((1, cache, HEAD), lambda i: (0, 0, i // per_group)),
        ],
        out_specs=pl.BlockSpec((tokens, PACK * HEAD), lambda i: (0, i)),
        out_shape=jax.ShapeDtypeStruct((tokens, width), jnp.bfloat16),
        cost_estimate=pl.CostEstimate(
            flops=4 * tokens * width * (cache + tokens),
            bytes_accessed=4 * cache * KV_HEADS * HEAD + 4 * tokens * width,
            transcendentals=tokens * HEADS * (cache + tokens),
        ),
    )(length, queries, new_keys, new_values, cache_keys, cache_values)


def run_expert(rows_in, gate_w, up_w, down_w):
    gate_part = jnp.dot(rows_in, gate_w, preferred_element_type=jnp.float32)
    up_part = jnp.dot(rows_in, up_w, preferred_element_type=jnp.float32)
    activated = (jax.nn.silu(gate_part) * up_part).astype(jnp.bfloat16)
    return jnp.dot(activated, down_w, preferred_element_type=jnp.float32)


def sparse_experts(normed, expert_ids, shares, gate_w, up_w, down_w, devices):
    token_count = normed.shape[0]
    capacity = SPAN * TOPK // devices + max(2, SPAN * TOPK // (8 * devices))
    flat_ids = expert_ids.reshape(-1)
    named = expert_ids[:, :, None] == jnp.arange(devices, dtype=jnp.int32)[None, None, :]
    earlier = jnp.tril(jnp.ones((token_count, token_count), jnp.bfloat16), -1)
    before = jnp.dot(
        earlier, jnp.any(named, axis=1).astype(jnp.bfloat16), preferred_element_type=jnp.float32
    )
    ranks = jnp.sum(jnp.where(named, before[:, None, :], 0.0), axis=-1)
    ranks = ranks.astype(jnp.int32).reshape(-1)
    slot_index = flat_ids * capacity + ranks
    token_of = jnp.arange(flat_ids.shape[0], dtype=jnp.int32) // TOPK
    slot_token = (
        jnp.full((devices * capacity,), token_count, jnp.int32).at[slot_index].set(token_of)
    )
    padded = jnp.concatenate([normed, jnp.zeros((1, D), jnp.bfloat16)], axis=0)
    outgoing = padded[slot_token].reshape(devices, capacity, D)
    arrived = lax.all_to_all(outgoing, "wide", split_axis=0, concat_axis=0, tiled=True)
    served = run_expert(arrived.reshape(-1, D), gate_w, up_w, down_w).astype(jnp.bfloat16)
    served = served.reshape(devices, capacity, D)
    returned_rows = lax.all_to_all(served, "wide", split_axis=0, concat_axis=0, tiled=True)
    picked = returned_rows.reshape(devices * capacity, D)[slot_index].reshape(token_count, TOPK, D)
    return jnp.sum(picked.astype(jnp.float32) * shares[..., None], axis=1)


LINE = 4
PAIR = 2
DOWN, UP, ACROSS, TWIN = range(4)


def attend(q, key, value, new_key, new_value, length, tokens):
    rows = q.shape[0]
    dims = (((1,), (1,)), ((), ()))
    s = lax.dot_general(q, key, dims, preferred_element_type=jnp.float32)
    position = lax.broadcasted_iota(jnp.int32, (1, key.shape[0]), 1)
    s = jnp.where(position < length, s, jnp.float32(-1e30))
    s_new = lax.dot_general(q, new_key, dims, preferred_element_type=jnp.float32)
    row = lax.broadcasted_iota(jnp.int32, (rows, tokens), 0) % tokens
    column = lax.broadcasted_iota(jnp.int32, (rows, tokens), 1)
    s_new = jnp.where(column <= row, s_new, jnp.float32(-1e30))
    top = jnp.maximum(jnp.max(s, axis=1, keepdims=True), jnp.max(s_new, axis=1, keepdims=True))
    w = jnp.exp2((s - top) * EXP2_SCALE)
    w_new = jnp.exp2((s_new - top) * EXP2_SCALE)
    total = jnp.sum(w, axis=1, keepdims=True) + jnp.sum(w_new, axis=1, keepdims=True)
    out = jnp.dot(w.astype(jnp.bfloat16), value, preferred_element_type=jnp.float32)
    out += jnp.dot(w_new.astype(jnp.bfloat16), new_value, preferred_element_type=jnp.float32)
    return (out / total).astype(jnp.bfloat16)


class Place:
    def __init__(self):
        self.me = lax.axis_index("wide")
        self.core = self.me % 2
        self.y = (self.me // 2) % PAIR
        self.z = self.me // (2 * PAIR)

    def block(self, z, y, core):
        return (z * PAIR + y) * 2 + core

    def towards(self, way):
        z, y, core = self.z, self.y, self.core
        if way == DOWN:
            return self.block(z - 1, y, core)
        if way == UP:
            return self.block(z + 1, y, core)
        if way == ACROSS:
            return self.block(z, 1 - y, core)
        return self.block(z, y, 1 - core)

    def line_at(self, i):
        low = self.z < LINE // 2
        inner = jnp.where(low, self.z, LINE - 1 - self.z)
        near = jnp.where((inner == 0) | (i >= 2), i, 1 - i)
        return jnp.where(low, near, LINE - 1 - near)

    def barrier(self, with_x=False):
        sem = pltpu.get_barrier_semaphore()

        def greet(way):
            pl.semaphore_signal(
                sem,
                inc=1,
                device_id={"wide": self.towards(way)},
                device_id_type=pl.DeviceIdType.MESH,
            )

        pl.when(self.z > 0)(lambda: greet(DOWN))
        pl.when(self.z < LINE - 1)(lambda: greet(UP))
        greet(ACROSS)
        greet(TWIN)
        if with_x:
            pl.semaphore_signal(
                sem, inc=1, device_id={"groups": 1 - lax.axis_index("groups")},
                device_id_type=pl.DeviceIdType.MESH,
            )
        ends = jnp.where((self.z == 0) | (self.z == LINE - 1), 1, 0)
        pl.semaphore_wait(sem, (5 if with_x else 4) - ends)


UPN, DOWNN = 0, 1
XWAY = 4
TILE = 16
P0, P1, PR, Q0, Q1, QS = range(6)
A_UP, A_DOWN, A_PASS, ATTEND, PROJECT = range(6, 11)
A_KINDS = {"P0": P0, "P1": P1, "PR": PR, "Q0": Q0, "Q1": Q1, "QS": QS}
A_OWN = {"u": A_UP, "d": A_DOWN, "y": A_PASS}
A_END = (
    "yQ0", "uP0", "a", "uP1", "a", "0Q0", "1P0", "a", "yQ1", "a", "a", "1Q0",
    "1P1", "a", "a", "2P0", "a", "1QS", "0Q1", "3P0", "0QS", "j01", "1Q1", "j10",
    "2Q0", "1PR", "3PR", "3P1", "2PR", "j00", "3Q0", "2P1", "2QS", "j21", "j31", "j11",
    "2Q1", "3Q1", "3QS", "j20", "j30",
)
A_INNER = (
    "yQ0", "yQ1", "dP0", "uP0", "dP1", "a", "a", "1Q0", "0P0", "a", "2P0", "0P1",
    "3P0", "a", "1QS", "uP1", "a", "3P1", "0Q0", "a", "a", "2P1", "a", "2Q0",
    "2PR", "j21", "0PR", "3PR", "j11", "3Q0", "0Q1", "1Q1", "j01", "0QS", "j10", "j00",
    "j31", "2Q1", "3Q1", "2QS", "3QS", "j20", "j30",
)


def gather_code(text):
    if text == "a":
        return ATTEND * 8
    if text[0] in A_OWN:
        return A_OWN[text[0]] * 8 + int(text[2])
    if text[0] == "j":
        return PROJECT * 8 + int(text[1]) * 2 + int(text[2])
    return A_KINDS[text[1:]] * 8 + int(text[0]) * 2


def packed(codes, words, bits):
    codes = codes + [(1 << bits) - 1] * (words * (28 // bits) - len(codes))
    per = 28 // bits
    return [
        sum(c << (bits * j) for j, c in enumerate(codes[per * w : per * w + per]))
        for w in range(words)
    ]


def pick(index, inner, ends, inners):
    at_end, at_inner = jnp.int32(ends[0]), jnp.int32(inners[0])
    for k in range(1, len(ends)):
        at_end = jnp.where(index == k, jnp.int32(ends[k]), at_end)
        at_inner = jnp.where(index == k, jnp.int32(inners[k]), at_inner)
    return jnp.where(inner == 1, at_inner, at_end)


PIECES = "abcd"
GET, UP_OWN, DOWN_OWN, PASS_OWN, SERVE, PAIR_UP, FOLD, FINISH = range(8)
KINDS = {"g": GET, "u": UP_OWN, "d": DOWN_OWN, "y": PASS_OWN}
KINDS.update({"s": SERVE, "p": PAIR_UP, "f": FOLD, "z": FINISH})
PA, PB, PC, PD = range(4)
SUBS = 2
B_END = (
    "ya1", "uc0", "uc1", "ya0", "g0b1", "yc1", "ua1", "g0b0", "ub1", "ua0", "s01", "g1b0",
    "yc0", "g0d1", "g1b1", "g1a0", "g1a1", "ub0", "g3c0", "g3c1", "s11", "g3d1", "g3d0", "f12",
    "s30", "g3a1", "g0d0", "p3", "f11", "s00", "g3a0", "g3b1", "g3b0", "g2c1", "p0", "f30",
    "s31", "g2b1", "f32", "g2a1", "g2b0", "g2a0", "g2d1", "f31", "g2c0", "s21", "g1c1", "g2d0",
    "f22", "g1c0", "s20", "g1d1", "f21", "g1d0", "p2", "s10", "p1", "f20", "z2", "z0",
    "f10", "z1",
)
B_INNER = (
    "da1", "ya1", "uc1", "ya0", "da0", "ua0", "g0c0", "g1b1", "db1", "g1b0", "db0", "yc1",
    "g0c1", "g0a1", "yc0", "g3c0", "g3c1", "g2a0", "g0b1", "g0d0", "s11", "g2c1", "g0a0", "g0b0",
    "g0d1", "ub1", "g3a1", "ua1", "s00", "uc0", "g3d0", "g3d1", "g3a0", "g1d0", "g3b1", "s30",
    "g3b0", "p3", "g2d1", "g2b1", "g2a1", "ub0", "g1d1", "s31", "g2b0", "p0", "s01", "g2c0",
    "dc1", "f30", "s21", "g2d0", "dc0", "f32", "s20", "f00", "f31", "s10", "p2", "f22",
    "p1", "f02", "f21", "f01", "z2", "f20", "z1", "z0",
)


def code_of(text):
    kind = KINDS[text[0]] * 32
    if kind == GET * 32:
        return kind + int(text[1]) * 8 + PIECES.index(text[2]) * 2 + int(text[3])
    if kind in (UP_OWN * 32, DOWN_OWN * 32, PASS_OWN * 32):
        return kind + PIECES.index(text[1]) * 2 + int(text[2])
    if kind == PAIR_UP * 32:
        return kind + int(text[1]) * 8
    if kind == FINISH * 32:
        return kind + int(text[1]) * 2
    return kind + int(text[1]) * 8 + int(text[2]) * 2


def first_serve(program):
    return [text[0] for text in program].index("s")


def layer_kernel(
    length_ref, nk_ref, nv_ref, res_ref, gain_ref, ids_ref, raw_ref, q_hbm, k_hbm, v_hbm, ow_ref,
    wg_ref, wu_ref, wd_ref, out_ref, q_ref, k_ref, v_ref,
    held, attn, mixed_ref, share_tab, share_col, rows, part, from_twin, from_pair, from_line, acc,
    wg, wu, wd, own_sem, load_sem, send_sem, recv_sem, share_send, share_recv,
    row_send, row_recv, back_send, twin_sem, pair_sem, line_sem,
):
    place = Place()
    z, y, core = place.z, place.y, place.core
    group = lax.axis_index("groups")
    tokens = q_ref.shape[0]
    depth = ow_ref.shape[0]
    low = z < LINE // 2
    inner = jnp.where(low, z, LINE - 1 - z)
    step_up = jnp.where(low, 1, -1)
    own = pltpu.make_async_copy(ow_ref, held.at[place.me], own_sem)
    own.start()
    pairs = ((q_hbm, q_ref), (k_hbm, k_ref), (v_hbm, v_ref), (wg_ref, wg), (wu_ref, wu), (wd_ref, wd))
    fetches = [
        pltpu.make_async_copy(source, dest, load_sem.at[k])
        for k, (source, dest) in enumerate(pairs)
    ]
    fetches, loads = fetches[:3], fetches[3:]
    for fetch in fetches:
        fetch.start()
    place.barrier(True)
    own.wait()

    third = depth // 8 * 2
    half = depth // 8 * 3
    last = depth - half
    span = {
        P0: (jnp.where(group == 0, 0, last), half),
        P1: (jnp.where(group == 0, half, third), half),
        PR: (jnp.where(group == 0, depth - third, 0), third),
        Q0: (jnp.where(group == 0, 0, last), half),
        Q1: (half, depth - 2 * half),
        QS: (jnp.where(group == 0, last, 0), half),
    }
    given = {PR: (jnp.where(group == 0, 0, depth - third), third), QS: span[Q0]}

    def real(nb):
        return jnp.where(low, nb, LINE - 1 - nb)

    def device(way):
        if way == XWAY:
            return {"groups": 1 - group}
        if way == UPN:
            return {"wide": place.block(z + step_up, y, core)}
        if way == DOWNN:
            return {"wide": place.block(z - step_up, y, core)}
        return {"wide": place.towards(way)}

    def copy(b, what, way):
        start, size = given[what] if way == XWAY else span[what]
        if not isinstance(start, int):
            start = pl.multiple_of(start, TILE)
        ref = held.at[b, pl.ds(start, size)]
        i = what % 3
        return pltpu.make_async_remote_copy(
            src_ref=ref, dst_ref=ref, send_sem=send_sem.at[b, i, way], recv_sem=recv_sem.at[b, i],
            device_id=device(way), device_id_type=pl.DeviceIdType.MESH,
        )

    def whole(b):
        return pltpu.make_async_remote_copy(
            src_ref=held.at[b], dst_ref=held.at[b], send_sem=send_sem.at[b, 2, TWIN],
            recv_sem=recv_sem.at[b, 0], device_id=device(TWIN),
            device_id_type=pl.DeviceIdType.MESH,
        )

    def share_copy(b, way):
        return pltpu.make_async_remote_copy(
            src_ref=share_tab.at[b], dst_ref=share_tab.at[b], send_sem=share_send.at[b, way],
            recv_sem=share_recv.at[b], device_id=device(way),
            device_id_type=pl.DeviceIdType.MESH,
        )

    def block_at(nb, yb, c):
        return place.block(real(nb), yb, c)

    me = place.me
    whole(me).start()

    def share_out():
        raw = raw_ref[...]
        given_share = raw / jnp.sum(raw, axis=0, keepdims=True)
        expert = lax.broadcasted_iota(jnp.int32, (share_tab.shape[1], 1), 0)
        table = jnp.zeros(share_tab.shape[1:], jnp.float32)
        for k in range(TOPK):
            hit = ids_ref[k : k + 1] == expert
            table = table + jnp.where(hit, given_share[k : k + 1], 0.0)
        share_tab[me] = table
        share_copy(me, UPN).start()
        pl.when(inner == 1)(share_copy(me, DOWNN).start)
        share_copy(me, ACROSS).start()
        share_copy(me, TWIN).start()

    def happen(code, turn):
        nb = lax.rem(code // 2, 4)
        flag = lax.rem(code, 2)
        kind = code // 8

        def own_line(way):
            pl.when(flag == 0)(copy(me, P0, way).start)
            pl.when(flag == 1)(copy(me, P1, way).start)

        pl.when(kind == A_UP)(lambda: own_line(UPN))
        pl.when(kind == A_DOWN)(lambda: own_line(DOWNN))

        @pl.when(kind == A_PASS)
        def _():
            pl.when(flag == 0)(copy(me, Q0, ACROSS).start)
            pl.when(flag == 1)(copy(me, Q1, ACROSS).start)

        @pl.when(kind == ATTEND)
        def _():
            @pl.when(turn == 0)
            def _():
                share_out()
                for load in loads:
                    load.start()
                for fetch in fetches:
                    fetch.wait()

            attend_step(turn)

        pl.when(kind == PROJECT)(lambda: project(nb, flag == 1))
        own_b = block_at(nb, y, core)
        other_b = block_at(nb, 1 - y, core)

        def line(what):
            pl.when(nb < inner)(copy(own_b, what, UPN).start)
            pl.when((nb > inner) & (inner == 1))(copy(own_b, what, DOWNN).start)

        @pl.when(kind == P0)
        def _():
            copy(own_b, P0, TWIN).wait_recv()
            line(P0)
            copy(own_b, Q0, ACROSS).start()
            copy(own_b, PR, XWAY).start()
            copy(own_b, P0, TWIN).start()
            share_copy(own_b, TWIN).wait_recv()
            pl.when(nb < inner)(share_copy(own_b, UPN).start)
            pl.when((nb > inner) & (inner == 1))(share_copy(own_b, DOWNN).start)
            share_copy(own_b, ACROSS).start()
            share_copy(own_b, TWIN).start()

        @pl.when(kind == P1)
        def _():
            copy(own_b, P1, TWIN).wait_recv()
            line(P1)
            copy(own_b, Q1, ACROSS).start()
            copy(own_b, P1, TWIN).start()

        @pl.when(kind == PR)
        def _():
            copy(own_b, PR, TWIN).wait_recv()
            copy(own_b, PR, TWIN).start()

        @pl.when(kind == Q0)
        def _():
            copy(other_b, Q0, TWIN).wait_recv()
            copy(other_b, QS, XWAY).start()
            copy(other_b, Q0, TWIN).start()
            share_copy(other_b, TWIN).wait_recv()
            share_copy(other_b, TWIN).start()

        @pl.when(kind == Q1)
        def _():
            copy(other_b, Q1, TWIN).wait_recv()
            copy(other_b, Q1, TWIN).start()

        @pl.when(kind == QS)
        def _():
            copy(other_b, QS, TWIN).wait_recv()
            copy(other_b, QS, TWIN).start()

    length = length_ref[place.me]
    per_group = HEADS // KV_HEADS // PACK

    def attend_step(i):
        q = jnp.concatenate(
            [
                q_ref[:, pl.ds(pl.multiple_of((i * PACK + j) * HEAD, HEAD), HEAD)]
                for j in range(PACK)
            ],
            axis=0,
        )
        columns = pl.ds(pl.multiple_of(i // per_group * HEAD, HEAD), HEAD)
        out = attend(
            q, k_ref[0, :, columns], v_ref[0, :, columns], nk_ref[:, columns],
            nv_ref[:, columns], length, tokens,
        )
        for j in range(PACK):
            attn[:, pl.ds(pl.multiple_of((i * PACK + j) * HEAD, HEAD), HEAD)] = out[
                j * tokens : (j + 1) * tokens
            ]

    mixed_ref[...] = res_ref[...].astype(jnp.float32)
    chosen = lax.broadcasted_iota(jnp.int32, (1, share_tab.shape[1]), 1) == me

    def project(nb, is_own):
        yb = jnp.where(is_own, y, 1 - y)
        b = block_at(nb, yb, 1 - core)

        @pl.when(is_own & (nb == inner))
        def _():
            whole(b).wait_recv()

        @pl.when(is_own & (nb != inner))
        def _():
            for what in (P0, P1, PR):
                copy(b, what, TWIN).wait_recv()

        @pl.when(jnp.logical_not(is_own))
        def _():
            for what in (Q0, Q1, QS):
                copy(b, what, TWIN).wait_recv()

        share_copy(b, TWIN).wait_recv()
        first = block_at(nb, yb, 0)
        for c in range(2):
            turned = share_tab[first + c].T
            column = jnp.sum(jnp.where(chosen, turned, 0.0), axis=1, keepdims=True)
            share_col[first + c] = jnp.broadcast_to(column, share_col.shape[1:])
        mine = attn[:, pl.ds(pl.multiple_of(first * depth, 2 * depth), 2 * depth)]
        weight = held[pl.ds(first, 2)].reshape(2 * depth, D)
        mixed_ref[...] += jnp.dot(mine, weight, preferred_element_type=jnp.float32)

    a_words = -(-max(len(A_END), len(A_INNER)) // 4)
    a_end = packed([gather_code(text) for text in A_END], a_words, 7)
    a_inner = packed([gather_code(text) for text in A_INNER], a_words, 7)

    def gather_route(w, turn):
        def one(j, state):
            word, at = state
            code = lax.rem(word, 128)
            happen(code, at)
            return word // 128, at + jnp.where(code // 8 == ATTEND, 1, 0)

        return lax.fori_loop(0, 4, one, (pick(w, inner, a_end, a_inner), turn))[1]

    lax.fori_loop(0, a_words, gather_route, jnp.int32(0))
    half_rows = tokens // 2
    mixed = mixed_ref[...]
    scale = lax.rsqrt(jnp.mean(mixed * mixed, axis=-1, keepdims=True) + 1e-06)
    normed = (mixed * scale * gain_ref[...]).astype(jnp.bfloat16)

    def slot(zb, p, yb, c):
        return ((zb * 2 + p) * PAIR + yb) * 2 + c

    sub = half_rows // SUBS
    for p in range(2):
        for h in range(SUBS):
            first_row = p * half_rows + h * sub
            rows[slot(z, p, y, core) * SUBS + h] = normed[first_row : first_row + sub]

    def send(source, dest, send_one, recv_one, way):
        return pltpu.make_async_remote_copy(
            src_ref=source, dst_ref=dest, send_sem=send_one, recv_sem=recv_one,
            device_id=device(way), device_id_type=pl.DeviceIdType.MESH,
        )

    def row_copy(b, h, way):
        t = b * SUBS + h
        return send(rows.at[t], rows.at[t], row_send.at[t, way], row_recv.at[t], way)

    def to_twin(zb, p, yb):
        b = slot(zb, p, yb, 1 - core)
        t = (zb * 2 + p) * PAIR + yb
        return send(part.at[b], from_twin.at[t], back_send.at[b], twin_sem.at[t], TWIN)

    def to_pair(zb, p):
        b = slot(zb, p, 1 - y, core)
        t = LINE if p else zb
        return send(part.at[b], from_pair.at[t], back_send.at[b], pair_sem.at[t], ACROSS)

    def kind_slot(zb, kind):
        p = jnp.minimum(kind, 1)
        yb = jnp.where(kind == 2, 1 - y, y)
        return p, yb, slot(zb, p, yb, core)

    side_up = jnp.where(low, 0, 1)

    def to_line(zb, kind, way):
        b = kind_slot(zb, kind)[2]
        side = side_up if way == UPN else 1 - side_up
        return send(
            part.at[b], from_line.at[side, zb, kind], back_send.at[b],
            line_sem.at[side, zb, kind], way,
        )

    def serve(zb, p):
        for yb in range(2):
            for h in range(SUBS):
                row_copy(slot(zb, p, yb, 1 - core), h, TWIN).wait_recv()
        first = slot(zb, p, 0, 0)
        x = rows[pl.ds(first * SUBS, 4 * SUBS)].reshape(4 * half_rows, D)
        here = pl.ds(pl.multiple_of(p * half_rows, half_rows), half_rows)
        share = share_col[pl.ds(place.block(zb, 0, 0), 4), here].reshape(4 * half_rows, HEAD)
        gate = jnp.dot(x, wg[...], preferred_element_type=jnp.float32)
        up = jnp.dot(x, wu[...], preferred_element_type=jnp.float32)
        act = (gate / (1.0 + jnp.exp(-gate)) * up).astype(jnp.bfloat16)
        out = jnp.dot(act, wd[...], preferred_element_type=jnp.float32) * share[:, :1]
        part[pl.ds(first, 4)] = out.astype(jnp.bfloat16).reshape(4, half_rows, D)
        to_twin(zb, p, 0).start()
        to_twin(zb, p, 1).start()

    def with_twin(zb, p, yb):
        to_twin(zb, p, yb).wait_recv()
        b = slot(zb, p, yb, core)
        t = (zb * 2 + p) * PAIR + yb
        return part[b].astype(jnp.float32) + from_twin[t].astype(jnp.float32)

    def add_line(zb, kind, way):
        to_line(zb, kind, way).wait_recv()
        side = side_up if way == UPN else 1 - side_up
        acc[...] += from_line[side, zb, kind].astype(jnp.float32)

    def fold(nb, kind):
        zb = real(nb)
        p, yb, b = kind_slot(zb, kind)
        acc[...] = with_twin(zb, p, yb)

        @pl.when(kind == 0)
        def _():
            to_pair(zb, 0).wait_recv()
            acc[...] += from_pair[zb].astype(jnp.float32)

        pl.when((nb > inner) & (inner == 1))(lambda: add_line(zb, kind, UPN))
        pl.when(nb < inner)(lambda: add_line(zb, kind, DOWNN))
        part[b] = acc[...].astype(jnp.bfloat16)
        pl.when(nb > inner)(to_line(zb, kind, UPN).start)
        pl.when(nb < inner)(to_line(zb, kind, DOWNN).start)

    def finish(kind):
        p, yb, b = kind_slot(z, kind)
        acc[...] = with_twin(z, p, yb)
        pl.when(inner == 1)(lambda: add_line(z, kind, UPN))
        add_line(z, kind, DOWNN)

        @pl.when(kind == 2)
        def _():
            part[b] = acc[...].astype(jnp.bfloat16)
            to_pair(z, 1).start()

        def close(p, t):
            here = pl.ds(p * half_rows, half_rows)
            to_pair(z, p).wait_recv()
            out_ref[here] = (
                acc[...] + mixed_ref[here] + from_pair[t].astype(jnp.float32)
            ).astype(jnp.bfloat16)

        pl.when(kind == 0)(lambda: close(0, z))
        pl.when(kind == 1)(lambda: close(1, LINE))

    def act_on(code, first):
        kind = code // 32
        nb = lax.rem(code // 8, 4)
        piece = lax.rem(code // 2, 4)
        h = lax.rem(code, 2)
        zb = real(nb)
        p = jnp.where(piece <= PB, 1, 0)
        yb = jnp.where((piece == PA) | (piece == PC), y, 1 - y)
        own_piece = slot(z, p, yb, core)

        @pl.when(kind == GET)
        def _():
            b = slot(zb, p, yb, core)
            row_copy(b, h, TWIN).wait_recv()
            onward = piece != PD
            pl.when(onward & (nb < inner))(row_copy(b, h, UPN).start)
            pl.when(onward & (nb > inner) & (inner == 1))(row_copy(b, h, DOWNN).start)
            pl.when((piece == PC) & (nb != inner))(row_copy(b, h, ACROSS).start)
            row_copy(b, h, TWIN).start()

        pl.when(kind == UP_OWN)(row_copy(own_piece, h, UPN).start)
        pl.when(kind == DOWN_OWN)(row_copy(own_piece, h, DOWNN).start)

        @pl.when(kind == PASS_OWN)
        def _():
            row_copy(own_piece, h, ACROSS).start()
            row_copy(own_piece, h, TWIN).start()

        @pl.when(kind == SERVE)
        def _():
            @pl.when(first)
            def _():
                for load in loads:
                    load.wait()

            serve(zb, piece)

        @pl.when(kind == PAIR_UP)
        def _():
            part[slot(zb, 0, 1 - y, core)] = with_twin(zb, 0, 1 - y).astype(jnp.bfloat16)
            to_pair(zb, 0).start()

        pl.when(kind == FOLD)(lambda: fold(nb, piece))
        pl.when((kind == FINISH) & (piece < 3))(lambda: finish(piece))

    words = -(-max(len(B_END), len(B_INNER)) // 3)
    end_words = packed([code_of(text) for text in B_END], words, 9)
    inner_words = packed([code_of(text) for text in B_INNER], words, 9)
    serve_at = jnp.where(inner == 1, first_serve(B_INNER), first_serve(B_END))

    def route(w, carry):
        def one(j, word):
            act_on(lax.rem(word, 512), w * 3 + j == serve_at)
            return word // 512

        lax.fori_loop(0, 3, one, pick(w, inner, end_words, inner_words))
        return carry

    lax.fori_loop(0, words, route, 0)

    def settle_rows(nb, carry):
        zb = real(nb)
        for h in range(SUBS):
            for p, yb in ((0, y), (1, y), (1, 1 - y)):
                b = slot(zb, p, yb, core)
                pl.when(nb <= inner)(row_copy(b, h, UPN).wait_send)
                pl.when((nb >= inner) & (inner == 1))(row_copy(b, h, DOWNN).wait_send)
            row_copy(slot(zb, 0, y, core), h, ACROSS).wait_send()
            pl.when(nb == inner)(row_copy(slot(zb, 1, y, core), h, ACROSS).wait_send)
            for p in range(2):
                for yb in (y, 1 - y):
                    row_copy(slot(zb, p, yb, core), h, TWIN).wait_send()
        for p in range(2):
            for yb in (y, 1 - y):
                to_twin(zb, p, yb).wait_send()
        to_pair(zb, 0).wait_send()
        pl.when(nb == inner)(to_pair(zb, 1).wait_send)

        @pl.when(nb != inner)
        def _():
            for kind in range(3):
                to_line(zb, kind, UPN).wait_send()

        return carry

    lax.fori_loop(0, LINE, settle_rows, 0)

    def settle_weights(nb, carry):
        own_b = block_at(nb, y, core)
        other_b = block_at(nb, 1 - y, core)
        for what in (P0, P1):
            pl.when(nb <= inner)(copy(own_b, what, UPN).wait_send)
            pl.when((nb >= inner) & (inner == 1))(copy(own_b, what, DOWNN).wait_send)
        pl.when(nb <= inner)(share_copy(own_b, UPN).wait_send)
        pl.when((nb >= inner) & (inner == 1))(share_copy(own_b, DOWNN).wait_send)
        share_copy(own_b, ACROSS).wait_send()
        share_copy(own_b, TWIN).wait_send()
        share_copy(other_b, TWIN).wait_send()
        copy(own_b, Q0, ACROSS).wait_send()
        copy(own_b, Q1, ACROSS).wait_send()

        @pl.when(nb == inner)
        def _():
            whole(own_b).wait_send()

        @pl.when(nb != inner)
        def _():
            copy(own_b, PR, XWAY).wait_send()
            for what in (P0, P1, PR):
                copy(own_b, what, TWIN).wait_send()

        copy(other_b, QS, XWAY).wait_send()
        for what in (Q0, Q1, QS):
            copy(other_b, what, TWIN).wait_send()
        return carry

    lax.fori_loop(0, LINE, settle_weights, 0)


def layer(
    cache_len, queries, new_keys, new_values, cache_keys, cache_values, residual, gain, ids, raw,
    o_weight, gate_w, up_w, down_w, devices,
):
    tokens, width = queries.shape
    half = tokens // 2
    vmem = pl.BlockSpec(memory_space=pltpu.VMEM)
    whole = pl.BlockSpec(memory_space=pl.ANY)
    dma = pltpu.SemaphoreType.DMA

    def held(*lead):
        return pltpu.VMEM(lead + (half, D), jnp.bfloat16)

    return pl.pallas_call(
        layer_kernel,
        in_specs=[pl.BlockSpec(memory_space=pltpu.SMEM)] + [vmem] * 6 + [whole] * 7,
        out_specs=vmem,
        out_shape=jax.ShapeDtypeStruct((tokens, D), jnp.bfloat16),
        scratch_shapes=[
            pltpu.VMEM(queries.shape, jnp.bfloat16),
            pltpu.VMEM(cache_keys.shape, jnp.bfloat16),
            pltpu.VMEM(cache_values.shape, jnp.bfloat16),
            pltpu.VMEM((devices,) + o_weight.shape, jnp.bfloat16),
            pltpu.VMEM((tokens, width), jnp.bfloat16),
            pltpu.VMEM((tokens, D), jnp.float32),
            pltpu.VMEM((devices, devices, tokens), jnp.float32),
            pltpu.VMEM((devices, tokens, HEAD), jnp.float32),
            pltpu.VMEM((2 * devices * SUBS, half // SUBS, D), jnp.bfloat16),
            held(2 * devices),
            held(devices),
            held(LINE + 1),
            held(2, LINE, 3),
            pltpu.VMEM((half, D), jnp.float32),
            pltpu.VMEM(gate_w.shape, jnp.bfloat16),
            pltpu.VMEM(up_w.shape, jnp.bfloat16),
            pltpu.VMEM(down_w.shape, jnp.bfloat16),
            dma,
            dma((6,)),
            dma((devices, 3, 5)),
            dma((devices, 3)),
            dma((devices, 4)),
            dma((devices,)),
            dma((2 * devices * SUBS, 4)),
            dma((2 * devices * SUBS,)),
            dma((2 * devices,)),
            dma((devices,)),
            dma((LINE + 1,)),
            dma((2, LINE, 3)),
        ],
        compiler_params=pltpu.CompilerParams(
            collective_id=0, has_side_effects=True, vmem_limit_bytes=63 << 20
        ),
    )(
        cache_len, new_keys, new_values, residual, gain, ids, raw, queries, cache_keys, cache_values,
        o_weight, gate_w, up_w, down_w,
    )


def grid_device(
    residual, queries, new_keys, new_values, cache_keys, cache_values, cache_len, o_weight,
    norm_gain, expert_ids, gate_raw, w_gate, w_up, w_down,
):
    devices = lax.axis_size("wide")
    return layer(
        cache_len, queries, new_keys, new_values, cache_keys, cache_values, residual,
        norm_gain.reshape(1, D), expert_ids.T, gate_raw.T, o_weight, w_gate[0], w_up[0], w_down[0], devices,
    )


def per_device(
    residual,
    queries,
    new_keys,
    new_values,
    cache_keys,
    cache_values,
    cache_len,
    o_weight,
    norm_gain,
    expert_ids,
    gate_raw,
    w_gate,
    w_up,
    w_down,
):
    devices = lax.axis_size("wide")
    me = lax.axis_index("wide")
    length = lax.dynamic_slice_in_dim(cache_len, me, 1, 0)
    attn = attention(length, queries, new_keys, new_values, cache_keys, cache_values)
    projected = jnp.dot(
        attn,
        lax.all_gather(o_weight, "wide", axis=0, tiled=True),
        preferred_element_type=jnp.float32,
    )
    mixed = residual.astype(jnp.float32) + projected
    normed = (
        mixed * lax.rsqrt(jnp.mean(mixed * mixed, axis=-1, keepdims=True) + 1e-06) * norm_gain
    ).astype(jnp.bfloat16)
    shares = gate_raw / jnp.sum(gate_raw, axis=-1, keepdims=True)
    routed = sparse_experts(normed, expert_ids, shares, w_gate[0], w_up[0], w_down[0], devices)
    return (mixed + routed).astype(jnp.bfloat16)


def solution(mesh):
    rows = P(("groups", "wide"), None)
    blocks = P(("groups", "wide"), None, None)
    weights = P("wide", None, None)
    placed = (rows, rows, rows, rows, blocks, blocks, P("groups"), P("wide", None), P())
    placed += (rows, rows, weights, weights, weights)
    grid = mesh.shape["wide"] == LINE * PAIR * 2 and mesh.shape["groups"] == 2
    return jax.shard_map(
        grid_device if grid else per_device,
        mesh=mesh,
        in_specs=placed,
        out_specs=rows,
        check_vma=False,
    )
```

```python
import functools
import jax
import jax.numpy as jnp
from jax import lax
from jax.experimental import pallas as pl
from jax.experimental.pallas import tpu as pltpu
from jax.sharding import PartitionSpec as P

D = 2048
HEADS = 16
KV_HEADS = 2
HEAD = 128
TOPK = 8
SPAN = 128
PACK = 2
EXP2_SCALE = HEAD ** (-0.5) * 1.4426950408889634


def attention_kernel(length_ref, q_ref, nk_ref, nv_ref, k_ref, v_ref, out_ref):
    tokens = q_ref.shape[0]
    rows = PACK * tokens
    cache = k_ref.shape[1]
    q = jnp.concatenate([q_ref[:, i * HEAD : (i + 1) * HEAD] for i in range(PACK)], axis=0)
    dims = (((1,), (1,)), ((), ()))
    s = lax.dot_general(q, k_ref[0], dims, preferred_element_type=jnp.float32)
    position = lax.broadcasted_iota(jnp.int32, (1, cache), 1)
    s = jnp.where(position < length_ref[0], s, jnp.float32(-1e30))
    s_new = lax.dot_general(q, nk_ref[...], dims, preferred_element_type=jnp.float32)
    row = lax.broadcasted_iota(jnp.int32, (rows, tokens), 0) % tokens
    column = lax.broadcasted_iota(jnp.int32, (rows, tokens), 1)
    s_new = jnp.where(column <= row, s_new, jnp.float32(-1e30))
    top = jnp.maximum(jnp.max(s, axis=1, keepdims=True), jnp.max(s_new, axis=1, keepdims=True))
    w = jnp.exp2((s - top) * EXP2_SCALE)
    w_new = jnp.exp2((s_new - top) * EXP2_SCALE)
    total = jnp.sum(w, axis=1, keepdims=True) + jnp.sum(w_new, axis=1, keepdims=True)
    out = jnp.dot(w.astype(jnp.bfloat16), v_ref[0], preferred_element_type=jnp.float32)
    out += jnp.dot(w_new.astype(jnp.bfloat16), nv_ref[...], preferred_element_type=jnp.float32)
    out = (out / total).astype(out_ref.dtype)
    for i in range(PACK):
        out_ref[:, i * HEAD : (i + 1) * HEAD] = out[i * tokens : (i + 1) * tokens]


def attention(length, queries, new_keys, new_values, cache_keys, cache_values):
    tokens, width = queries.shape
    cache = cache_keys.shape[1]
    per_group = HEADS // KV_HEADS // PACK
    return pl.pallas_call(
        attention_kernel,
        grid=(HEADS // PACK,),
        in_specs=[
            pl.BlockSpec(memory_space=pltpu.SMEM),
            pl.BlockSpec((tokens, PACK * HEAD), lambda i: (0, i)),
            pl.BlockSpec((tokens, HEAD), lambda i: (0, i // per_group)),
            pl.BlockSpec((tokens, HEAD), lambda i: (0, i // per_group)),
            pl.BlockSpec((1, cache, HEAD), lambda i: (0, 0, i // per_group)),
            pl.BlockSpec((1, cache, HEAD), lambda i: (0, 0, i // per_group)),
        ],
        out_specs=pl.BlockSpec((tokens, PACK * HEAD), lambda i: (0, i)),
        out_shape=jax.ShapeDtypeStruct((tokens, width), jnp.bfloat16),
        cost_estimate=pl.CostEstimate(
            flops=4 * tokens * width * (cache + tokens),
            bytes_accessed=4 * cache * KV_HEADS * HEAD + 4 * tokens * width,
            transcendentals=tokens * HEADS * (cache + tokens),
        ),
    )(length, queries, new_keys, new_values, cache_keys, cache_values)


def run_expert(rows_in, gate_w, up_w, down_w):
    gate_part = jnp.dot(rows_in, gate_w, preferred_element_type=jnp.float32)
    up_part = jnp.dot(rows_in, up_w, preferred_element_type=jnp.float32)
    activated = (jax.nn.silu(gate_part) * up_part).astype(jnp.bfloat16)
    return jnp.dot(activated, down_w, preferred_element_type=jnp.float32)


def sparse_experts(normed, expert_ids, shares, gate_w, up_w, down_w, devices):
    token_count = normed.shape[0]
    capacity = SPAN * TOPK // devices + max(2, SPAN * TOPK // (8 * devices))
    flat_ids = expert_ids.reshape(-1)
    named = expert_ids[:, :, None] == jnp.arange(devices, dtype=jnp.int32)[None, None, :]
    earlier = jnp.tril(jnp.ones((token_count, token_count), jnp.bfloat16), -1)
    before = jnp.dot(
        earlier, jnp.any(named, axis=1).astype(jnp.bfloat16), preferred_element_type=jnp.float32
    )
    ranks = jnp.sum(jnp.where(named, before[:, None, :], 0.0), axis=-1)
    ranks = ranks.astype(jnp.int32).reshape(-1)
    slot_index = flat_ids * capacity + ranks
    token_of = jnp.arange(flat_ids.shape[0], dtype=jnp.int32) // TOPK
    slot_token = (
        jnp.full((devices * capacity,), token_count, jnp.int32).at[slot_index].set(token_of)
    )
    padded = jnp.concatenate([normed, jnp.zeros((1, D), jnp.bfloat16)], axis=0)
    outgoing = padded[slot_token].reshape(devices, capacity, D)
    arrived = lax.all_to_all(outgoing, "wide", split_axis=0, concat_axis=0, tiled=True)
    served = run_expert(arrived.reshape(-1, D), gate_w, up_w, down_w).astype(jnp.bfloat16)
    served = served.reshape(devices, capacity, D)
    returned_rows = lax.all_to_all(served, "wide", split_axis=0, concat_axis=0, tiled=True)
    picked = returned_rows.reshape(devices * capacity, D)[slot_index].reshape(token_count, TOPK, D)
    return jnp.sum(picked.astype(jnp.float32) * shares[..., None], axis=1)


LINE = 4
PAIR = 2
DOWN, UP, ACROSS, TWIN = range(4)


def attend(q, key, value, new_key, new_value, length, tokens):
    rows = q.shape[0]
    dims = (((1,), (1,)), ((), ()))
    s = lax.dot_general(q, key, dims, preferred_element_type=jnp.float32)
    position = lax.broadcasted_iota(jnp.int32, (1, key.shape[0]), 1)
    s = jnp.where(position < length, s, jnp.float32(-1e30))
    s_new = lax.dot_general(q, new_key, dims, preferred_element_type=jnp.float32)
    row = lax.broadcasted_iota(jnp.int32, (rows, tokens), 0) % tokens
    column = lax.broadcasted_iota(jnp.int32, (rows, tokens), 1)
    s_new = jnp.where(column <= row, s_new, jnp.float32(-1e30))
    top = jnp.maximum(jnp.max(s, axis=1, keepdims=True), jnp.max(s_new, axis=1, keepdims=True))
    w = jnp.exp2((s - top) * EXP2_SCALE)
    w_new = jnp.exp2((s_new - top) * EXP2_SCALE)
    total = jnp.sum(w, axis=1, keepdims=True) + jnp.sum(w_new, axis=1, keepdims=True)
    out = jnp.dot(w.astype(jnp.bfloat16), value, preferred_element_type=jnp.float32)
    out += jnp.dot(w_new.astype(jnp.bfloat16), new_value, preferred_element_type=jnp.float32)
    return (out / total).astype(jnp.bfloat16)


class Place:
    def __init__(self):
        self.me = lax.axis_index("wide")
        self.core = self.me % 2
        self.y = (self.me // 2) % PAIR
        self.z = self.me // (2 * PAIR)

    def block(self, z, y, core):
        return (z * PAIR + y) * 2 + core

    def towards(self, way):
        z, y, core = self.z, self.y, self.core
        if way == DOWN:
            return self.block(z - 1, y, core)
        if way == UP:
            return self.block(z + 1, y, core)
        if way == ACROSS:
            return self.block(z, 1 - y, core)
        return self.block(z, y, 1 - core)

    def line_at(self, i):
        low = self.z < LINE // 2
        inner = jnp.where(low, self.z, LINE - 1 - self.z)
        near = jnp.where((inner == 0) | (i >= 2), i, 1 - i)
        return jnp.where(low, near, LINE - 1 - near)

    def barrier(self, with_x=False):
        sem = pltpu.get_barrier_semaphore()

        def greet(way):
            pl.semaphore_signal(
                sem,
                inc=1,
                device_id={"wide": self.towards(way)},
                device_id_type=pl.DeviceIdType.MESH,
            )

        pl.when(self.z > 0)(lambda: greet(DOWN))
        pl.when(self.z < LINE - 1)(lambda: greet(UP))
        greet(ACROSS)
        greet(TWIN)
        if with_x:
            pl.semaphore_signal(
                sem, inc=1, device_id={"groups": 1 - lax.axis_index("groups")},
                device_id_type=pl.DeviceIdType.MESH,
            )
        ends = jnp.where((self.z == 0) | (self.z == LINE - 1), 1, 0)
        pl.semaphore_wait(sem, (5 if with_x else 4) - ends)


UPN, DOWNN = 0, 1
XWAY = 4
TILE = 16
P0, P1, PR, Q0, Q1, QS = range(6)
A_UP, A_DOWN, A_PASS, ATTEND, PROJECT = range(6, 11)
A_KINDS = {"P0": P0, "P1": P1, "PR": PR, "Q0": Q0, "Q1": Q1, "QS": QS}
A_OWN = {"u": A_UP, "d": A_DOWN, "y": A_PASS}
A_END = (
    "yQ0", "uP0", "a", "uP1", "a", "0Q0", "1P0", "a", "yQ1", "a", "a", "1Q0",
    "1P1", "a", "a", "2P0", "a", "1QS", "0Q1", "3P0", "0QS", "j01", "1Q1", "j10",
    "2Q0", "1PR", "3PR", "3P1", "2PR", "j00", "3Q0", "2P1", "2QS", "j21", "j31", "j11",
    "2Q1", "3Q1", "3QS", "j20", "j30",
)
A_INNER = (
    "yQ0", "yQ1", "dP0", "uP0", "dP1", "a", "a", "1Q0", "0P0", "a", "2P0", "0P1",
    "3P0", "a", "1QS", "uP1", "a", "3P1", "0Q0", "a", "a", "2P1", "a", "2Q0",
    "2PR", "j21", "0PR", "3PR", "j11", "3Q0", "0Q1", "1Q1", "j01", "0QS", "j10", "j00",
    "j31", "2Q1", "3Q1", "2QS", "3QS", "j20", "j30",
)


def gather_code(text):
    if text == "a":
        return ATTEND * 8
    if text[0] in A_OWN:
        return A_OWN[text[0]] * 8 + int(text[2])
    if text[0] == "j":
        return PROJECT * 8 + int(text[1]) * 2 + int(text[2])
    return A_KINDS[text[1:]] * 8 + int(text[0]) * 2


def packed(codes, words, bits):
    codes = codes + [(1 << bits) - 1] * (words * (28 // bits) - len(codes))
    per = 28 // bits
    return [
        sum(c << (bits * j) for j, c in enumerate(codes[per * w : per * w + per]))
        for w in range(words)
    ]


def pick(index, inner, ends, inners):
    at_end, at_inner = jnp.int32(ends[0]), jnp.int32(inners[0])
    for k in range(1, len(ends)):
        at_end = jnp.where(index == k, jnp.int32(ends[k]), at_end)
        at_inner = jnp.where(index == k, jnp.int32(inners[k]), at_inner)
    return jnp.where(inner == 1, at_inner, at_end)


PIECES = "abcd"
GET, UP_OWN, DOWN_OWN, PASS_OWN, SERVE, PAIR_UP, FOLD, FINISH = range(8)
KINDS = {"g": GET, "u": UP_OWN, "d": DOWN_OWN, "y": PASS_OWN}
KINDS.update({"s": SERVE, "p": PAIR_UP, "f": FOLD, "z": FINISH})
PA, PB, PC, PD = range(4)
SUBS = 2
B_END = (
    "ya1", "uc0", "uc1", "ya0", "g0b1", "yc1", "ua1", "g0b0", "ub1", "ua0", "s01", "g1b0",
    "yc0", "g0d1", "g1b1", "g1a0", "g1a1", "ub0", "g3c0", "g3c1", "s11", "g3d1", "g3d0", "f12",
    "s30", "g3a1", "g0d0", "p3", "f11", "s00", "g3a0", "g3b1", "g3b0", "g2c1", "p0", "f30",
    "s31", "g2b1", "f32", "g2a1", "g2b0", "g2a0", "g2d1", "f31", "g2c0", "s21", "g1c1", "g2d0",
    "f22", "g1c0", "s20", "g1d1", "f21", "g1d0", "p2", "s10", "p1", "f20", "z2", "z0",
    "f10", "z1",
)
B_INNER = (
    "da1", "ya1", "uc1", "ya0", "da0", "ua0", "g0c0", "g1b1", "db1", "g1b0", "db0", "yc1",
    "g0c1", "g0a1", "yc0", "g3c0", "g3c1", "g2a0", "g0b1", "g0d0", "s11", "g2c1", "g0a0", "g0b0",
    "g0d1", "ub1", "g3a1", "ua1", "s00", "uc0", "g3d0", "g3d1", "g3a0", "g1d0", "g3b1", "s30",
    "g3b0", "p3", "g2d1", "g2b1", "g2a1", "ub0", "g1d1", "s31", "g2b0", "p0", "s01", "g2c0",
    "dc1", "f30", "s21", "g2d0", "dc0", "f32", "s20", "f00", "f31", "s10", "p2", "f22",
    "p1", "f02", "f21", "f01", "z2", "f20", "z1", "z0",
)


def code_of(text):
    kind = KINDS[text[0]] * 32
    if kind == GET * 32:
        return kind + int(text[1]) * 8 + PIECES.index(text[2]) * 2 + int(text[3])
    if kind in (UP_OWN * 32, DOWN_OWN * 32, PASS_OWN * 32):
        return kind + PIECES.index(text[1]) * 2 + int(text[2])
    if kind == PAIR_UP * 32:
        return kind + int(text[1]) * 8
    if kind == FINISH * 32:
        return kind + int(text[1]) * 2
    return kind + int(text[1]) * 8 + int(text[2]) * 2


def first_serve(program):
    return [text[0] for text in program].index("s")


def layer_kernel(
    length_ref, nk_ref, nv_ref, res_ref, gain_ref, ids_ref, raw_ref, q_hbm, k_hbm, v_hbm, ow_ref,
    wg_ref, wu_ref, wd_ref, out_ref, q_ref, k_ref, v_ref,
    held, attn, mixed_ref, share_tab, share_col, rows, part, from_twin, from_pair, from_line, acc,
    wg, wu, wd, own_sem, load_sem, send_sem, recv_sem, recv_twin, share_send,
    share_recv, row_send, row_recv, twin_rows, back_send, twin_sem, pair_sem, line_sem,
):
    place = Place()
    z, y, core = place.z, place.y, place.core
    group = lax.axis_index("groups")
    tokens = q_ref.shape[0]
    depth = ow_ref.shape[0]
    low = z < LINE // 2
    inner = jnp.where(low, z, LINE - 1 - z)
    step_up = jnp.where(low, 1, -1)
    own = pltpu.make_async_copy(ow_ref, held.at[place.me], own_sem)
    own.start()
    pairs = ((q_hbm, q_ref), (k_hbm, k_ref), (v_hbm, v_ref), (wg_ref, wg), (wu_ref, wu), (wd_ref, wd))
    fetches = [
        pltpu.make_async_copy(source, dest, load_sem.at[k])
        for k, (source, dest) in enumerate(pairs)
    ]
    fetches, loads = fetches[:3], fetches[3:]
    for fetch in fetches:
        fetch.start()
    place.barrier(True)
    own.wait()

    third = depth // 8 * 2
    half = depth // 8 * 3
    last = depth - half
    span = {
        P0: (jnp.where(group == 0, 0, last), half),
        P1: (jnp.where(group == 0, half, third), half),
        PR: (jnp.where(group == 0, depth - third, 0), third),
        Q0: (jnp.where(group == 0, 0, last), half),
        Q1: (half, depth - 2 * half),
        QS: (jnp.where(group == 0, last, 0), half),
    }
    given = {PR: (jnp.where(group == 0, 0, depth - third), third), QS: span[Q0]}

    def real(nb):
        return jnp.where(low, nb, LINE - 1 - nb)

    def device(way):
        if way == XWAY:
            return {"groups": 1 - group}
        if way == UPN:
            return {"wide": place.block(z + step_up, y, core)}
        if way == DOWNN:
            return {"wide": place.block(z - step_up, y, core)}
        return {"wide": place.towards(way)}

    def copy(b, what, way):
        start, size = given[what] if way == XWAY else span[what]
        if not isinstance(start, int):
            start = pl.multiple_of(start, TILE)
        ref = held.at[b, pl.ds(start, size)]
        return pltpu.make_async_remote_copy(
            src_ref=ref, dst_ref=ref, send_sem=send_sem.at[way],
            recv_sem=recv_twin.at[b // 2] if way == TWIN else recv_sem.at[b // 2, what % 3],
            device_id=device(way), device_id_type=pl.DeviceIdType.MESH,
        )

    def arrived(b, what):
        copy(b, what, ACROSS).wait_recv()

    def whole(b):
        return pltpu.make_async_remote_copy(
            src_ref=held.at[b], dst_ref=held.at[b], send_sem=send_sem.at[TWIN],
            recv_sem=recv_twin.at[b // 2], device_id=device(TWIN),
            device_id_type=pl.DeviceIdType.MESH,
        )

    def share_copy(b, way):
        return pltpu.make_async_remote_copy(
            src_ref=share_tab.at[b], dst_ref=share_tab.at[b], send_sem=share_send.at[way],
            recv_sem=share_recv.at[b], device_id=device(way),
            device_id_type=pl.DeviceIdType.MESH,
        )

    def block_at(nb, yb, c):
        return place.block(real(nb), yb, c)

    me = place.me
    whole(me).start()

    def share_out():
        raw = raw_ref[...]
        given_share = raw / jnp.sum(raw, axis=0, keepdims=True)
        expert = lax.broadcasted_iota(jnp.int32, (share_tab.shape[1], 1), 0)
        table = jnp.zeros(share_tab.shape[1:], jnp.float32)
        for k in range(TOPK):
            hit = ids_ref[k : k + 1] == expert
            table = table + jnp.where(hit, given_share[k : k + 1], 0.0)
        share_tab[me] = table
        share_copy(me, UPN).start()
        pl.when(inner == 1)(share_copy(me, DOWNN).start)
        share_copy(me, ACROSS).start()
        share_copy(me, TWIN).start()

    def happen(code, turn):
        nb = lax.rem(code // 2, 4)
        flag = lax.rem(code, 2)
        kind = code // 8

        def own_line(way):
            pl.when(flag == 0)(copy(me, P0, way).start)
            pl.when(flag == 1)(copy(me, P1, way).start)

        pl.when(kind == A_UP)(lambda: own_line(UPN))
        pl.when(kind == A_DOWN)(lambda: own_line(DOWNN))

        @pl.when(kind == A_PASS)
        def _():
            pl.when(flag == 0)(copy(me, Q0, ACROSS).start)
            pl.when(flag == 1)(copy(me, Q1, ACROSS).start)

        @pl.when(kind == ATTEND)
        def _():
            @pl.when(turn == 0)
            def _():
                share_out()
                for load in loads:
                    load.start()
                for fetch in fetches:
                    fetch.wait()

            attend_step(turn)

        pl.when(kind == PROJECT)(lambda: project(nb, flag == 1))
        own_b = block_at(nb, y, core)
        other_b = block_at(nb, 1 - y, core)

        def line(what):
            pl.when(nb < inner)(copy(own_b, what, UPN).start)
            pl.when((nb > inner) & (inner == 1))(copy(own_b, what, DOWNN).start)

        @pl.when(kind == P0)
        def _():
            arrived(own_b, P0)
            line(P0)
            copy(own_b, Q0, ACROSS).start()
            copy(own_b, PR, XWAY).start()
            copy(own_b, P0, TWIN).start()
            share_copy(own_b, TWIN).wait_recv()
            pl.when(nb < inner)(share_copy(own_b, UPN).start)
            pl.when((nb > inner) & (inner == 1))(share_copy(own_b, DOWNN).start)
            share_copy(own_b, ACROSS).start()
            share_copy(own_b, TWIN).start()

        @pl.when(kind == P1)
        def _():
            arrived(own_b, P1)
            line(P1)
            copy(own_b, Q1, ACROSS).start()
            copy(own_b, P1, TWIN).start()

        @pl.when(kind == PR)
        def _():
            arrived(own_b, PR)
            copy(own_b, PR, TWIN).start()

        @pl.when(kind == Q0)
        def _():
            arrived(other_b, Q0)
            copy(other_b, QS, XWAY).start()
            copy(other_b, Q0, TWIN).start()
            share_copy(other_b, TWIN).wait_recv()
            share_copy(other_b, TWIN).start()

        @pl.when(kind == Q1)
        def _():
            arrived(other_b, Q1)
            copy(other_b, Q1, TWIN).start()

        @pl.when(kind == QS)
        def _():
            arrived(other_b, QS)
            copy(other_b, QS, TWIN).start()

    length = length_ref[place.me]
    per_group = HEADS // KV_HEADS // PACK

    def attend_step(i):
        q = jnp.concatenate(
            [
                q_ref[:, pl.ds(pl.multiple_of((i * PACK + j) * HEAD, HEAD), HEAD)]
                for j in range(PACK)
            ],
            axis=0,
        )
        columns = pl.ds(pl.multiple_of(i // per_group * HEAD, HEAD), HEAD)
        out = attend(
            q, k_ref[0, :, columns], v_ref[0, :, columns], nk_ref[:, columns],
            nv_ref[:, columns], length, tokens,
        )
        for j in range(PACK):
            attn[:, pl.ds(pl.multiple_of((i * PACK + j) * HEAD, HEAD), HEAD)] = out[
                j * tokens : (j + 1) * tokens
            ]

    mixed_ref[...] = res_ref[...].astype(jnp.float32)
    chosen = lax.broadcasted_iota(jnp.int32, (1, share_tab.shape[1]), 1) == me

    def project(nb, is_own):
        yb = jnp.where(is_own, y, 1 - y)
        b = block_at(nb, yb, 1 - core)

        whole(b).wait_recv()
        share_copy(b, TWIN).wait_recv()
        first = block_at(nb, yb, 0)
        for c in range(2):
            turned = share_tab[first + c].T
            column = jnp.sum(jnp.where(chosen, turned, 0.0), axis=1, keepdims=True)
            share_col[first + c] = jnp.broadcast_to(column, share_col.shape[1:])
        mine = attn[:, pl.ds(pl.multiple_of(first * depth, 2 * depth), 2 * depth)]
        weight = held[pl.ds(first, 2)].reshape(2 * depth, D)
        mixed_ref[...] += jnp.dot(mine, weight, preferred_element_type=jnp.float32)

    a_words = -(-max(len(A_END), len(A_INNER)) // 4)
    a_end = packed([gather_code(text) for text in A_END], a_words, 7)
    a_inner = packed([gather_code(text) for text in A_INNER], a_words, 7)

    def gather_route(w, turn):
        def one(j, state):
            word, at = state
            code = lax.rem(word, 128)
            happen(code, at)
            return word // 128, at + jnp.where(code // 8 == ATTEND, 1, 0)

        return lax.fori_loop(0, 4, one, (pick(w, inner, a_end, a_inner), turn))[1]

    lax.fori_loop(0, a_words, gather_route, jnp.int32(0))
    half_rows = tokens // 2
    mixed = mixed_ref[...]
    scale = lax.rsqrt(jnp.mean(mixed * mixed, axis=-1, keepdims=True) + 1e-06)
    normed = (mixed * scale * gain_ref[...]).astype(jnp.bfloat16)

    def slot(zb, p, yb, c):
        return ((zb * 2 + p) * PAIR + yb) * 2 + c

    sub = half_rows // SUBS
    for p in range(2):
        for h in range(SUBS):
            first_row = p * half_rows + h * sub
            rows[slot(z, p, y, core) * SUBS + h] = normed[first_row : first_row + sub]

    def send(source, dest, send_one, recv_one, way):
        return pltpu.make_async_remote_copy(
            src_ref=source, dst_ref=dest, send_sem=send_one, recv_sem=recv_one,
            device_id=device(way), device_id_type=pl.DeviceIdType.MESH,
        )

    def row_copy(b, h, way):
        t = b * SUBS + h
        landed = twin_rows.at[b // 4] if way == TWIN else row_recv.at[b // 2 * SUBS + h]
        return send(rows.at[t], rows.at[t], row_send.at[way], landed, way)

    def to_twin(zb, p, yb):
        b = slot(zb, p, yb, 1 - core)
        t = (zb * 2 + p) * PAIR + yb
        return send(part.at[b], from_twin.at[t], back_send.at[0], twin_sem.at[t], TWIN)

    def to_pair(zb, p):
        b = slot(zb, p, 1 - y, core)
        t = LINE if p else zb
        return send(part.at[b], from_pair.at[t], back_send.at[0], pair_sem.at[t], ACROSS)

    def kind_slot(zb, kind):
        p = jnp.minimum(kind, 1)
        yb = jnp.where(kind == 2, 1 - y, y)
        return p, yb, slot(zb, p, yb, core)

    side_up = jnp.where(low, 0, 1)

    def to_line(zb, kind, way):
        b = kind_slot(zb, kind)[2]
        side = side_up if way == UPN else 1 - side_up
        return send(
            part.at[b], from_line.at[side, zb, kind], back_send.at[0],
            line_sem.at[side, zb, kind], way,
        )

    def serve(zb, p):
        first = slot(zb, p, 0, 0)
        bulk = rows.at[pl.ds(0, 2 * SUBS)]
        send(bulk, bulk, row_send.at[TWIN], twin_rows.at[first // 4], TWIN).wait_recv()
        x = rows[pl.ds(first * SUBS, 4 * SUBS)].reshape(4 * half_rows, D)
        here = pl.ds(pl.multiple_of(p * half_rows, half_rows), half_rows)
        share = share_col[pl.ds(place.block(zb, 0, 0), 4), here].reshape(4 * half_rows, HEAD)
        gate = jnp.dot(x, wg[...], preferred_element_type=jnp.float32)
        up = jnp.dot(x, wu[...], preferred_element_type=jnp.float32)
        act = (gate / (1.0 + jnp.exp(-gate)) * up).astype(jnp.bfloat16)
        out = jnp.dot(act, wd[...], preferred_element_type=jnp.float32) * share[:, :1]
        part[pl.ds(first, 4)] = out.astype(jnp.bfloat16).reshape(4, half_rows, D)
        to_twin(zb, p, 0).start()
        to_twin(zb, p, 1).start()

    def with_twin(zb, p, yb):
        to_twin(zb, p, yb).wait_recv()
        b = slot(zb, p, yb, core)
        t = (zb * 2 + p) * PAIR + yb
        return part[b].astype(jnp.float32) + from_twin[t].astype(jnp.float32)

    def add_line(zb, kind, way):
        to_line(zb, kind, way).wait_recv()
        side = side_up if way == UPN else 1 - side_up
        acc[...] += from_line[side, zb, kind].astype(jnp.float32)

    def fold(nb, kind):
        zb = real(nb)
        p, yb, b = kind_slot(zb, kind)
        acc[...] = with_twin(zb, p, yb)

        @pl.when(kind == 0)
        def _():
            to_pair(zb, 0).wait_recv()
            acc[...] += from_pair[zb].astype(jnp.float32)

        pl.when((nb > inner) & (inner == 1))(lambda: add_line(zb, kind, UPN))
        pl.when(nb < inner)(lambda: add_line(zb, kind, DOWNN))
        part[b] = acc[...].astype(jnp.bfloat16)
        pl.when(nb > inner)(to_line(zb, kind, UPN).start)
        pl.when(nb < inner)(to_line(zb, kind, DOWNN).start)

    def finish(kind):
        p, yb, b = kind_slot(z, kind)
        acc[...] = with_twin(z, p, yb)
        pl.when(inner == 1)(lambda: add_line(z, kind, UPN))
        add_line(z, kind, DOWNN)

        @pl.when(kind == 2)
        def _():
            part[b] = acc[...].astype(jnp.bfloat16)
            to_pair(z, 1).start()

        def close(p, t):
            here = pl.ds(p * half_rows, half_rows)
            to_pair(z, p).wait_recv()
            out_ref[here] = (
                acc[...] + mixed_ref[here] + from_pair[t].astype(jnp.float32)
            ).astype(jnp.bfloat16)

        pl.when(kind == 0)(lambda: close(0, z))
        pl.when(kind == 1)(lambda: close(1, LINE))

    def act_on(code, first):
        kind = code // 32
        nb = lax.rem(code // 8, 4)
        piece = lax.rem(code // 2, 4)
        h = lax.rem(code, 2)
        zb = real(nb)
        p = jnp.where(piece <= PB, 1, 0)
        yb = jnp.where((piece == PA) | (piece == PC), y, 1 - y)
        own_piece = slot(z, p, yb, core)

        @pl.when(kind == GET)
        def _():
            b = slot(zb, p, yb, core)
            row_copy(b, h, ACROSS).wait_recv()
            onward = piece != PD
            pl.when(onward & (nb < inner))(row_copy(b, h, UPN).start)
            pl.when(onward & (nb > inner) & (inner == 1))(row_copy(b, h, DOWNN).start)
            pl.when((piece == PC) & (nb != inner))(row_copy(b, h, ACROSS).start)
            row_copy(b, h, TWIN).start()

        pl.when(kind == UP_OWN)(row_copy(own_piece, h, UPN).start)
        pl.when(kind == DOWN_OWN)(row_copy(own_piece, h, DOWNN).start)

        @pl.when(kind == PASS_OWN)
        def _():
            row_copy(own_piece, h, ACROSS).start()
            row_copy(own_piece, h, TWIN).start()

        @pl.when(kind == SERVE)
        def _():
            @pl.when(first)
            def _():
                for load in loads:
                    load.wait()

            serve(zb, piece)

        @pl.when(kind == PAIR_UP)
        def _():
            part[slot(zb, 0, 1 - y, core)] = with_twin(zb, 0, 1 - y).astype(jnp.bfloat16)
            to_pair(zb, 0).start()

        pl.when(kind == FOLD)(lambda: fold(nb, piece))
        pl.when((kind == FINISH) & (piece < 3))(lambda: finish(piece))

    words = -(-max(len(B_END), len(B_INNER)) // 3)
    end_words = packed([code_of(text) for text in B_END], words, 9)
    inner_words = packed([code_of(text) for text in B_INNER], words, 9)
    serve_at = jnp.where(inner == 1, first_serve(B_INNER), first_serve(B_END))

    def route(w, carry):
        def one(j, word):
            act_on(lax.rem(word, 512), w * 3 + j == serve_at)
            return word // 512

        lax.fori_loop(0, 3, one, pick(w, inner, end_words, inner_words))
        return carry

    lax.fori_loop(0, words, route, 0)

    def sent(ref, sem, way=TWIN):
        send(ref, ref, sem, share_recv.at[0], way).wait_send()

    def sent_by_place(at_end, at_inner):
        pl.when(inner == 0)(at_end)
        pl.when(inner == 1)(at_inner)

    lines = 2 * half
    sent_by_place(
        lambda: sent(held.at[0, pl.ds(0, lines)], send_sem.at[UPN]),
        lambda: sent(held.at[pl.ds(0, 2), pl.ds(0, lines)], send_sem.at[UPN]),
    )
    sent_by_place(
        lambda: sent(share_tab.at[pl.ds(0, 1)], share_send.at[UPN]),
        lambda: sent(share_tab.at[pl.ds(0, 2)], share_send.at[UPN]),
    )
    sent_by_place(
        lambda: sent(rows.at[pl.ds(0, 3 * SUBS)], row_send.at[UPN]),
        lambda: sent(rows.at[pl.ds(0, 6 * SUBS)], row_send.at[UPN]),
    )

    @pl.when(inner == 1)
    def _():
        sent(held.at[pl.ds(0, 3), pl.ds(0, lines)], send_sem.at[DOWNN])
        sent(share_tab.at[pl.ds(0, 3)], share_send.at[DOWNN])
        sent(rows.at[pl.ds(0, 9 * SUBS)], row_send.at[DOWNN])

    sent(held.at[pl.ds(0, LINE), pl.ds(0, depth - half)], send_sem.at[ACROSS])
    sent(held.at[pl.ds(0, LINE - 1), pl.ds(0, lines)], send_sem.at[XWAY])
    sent(held.at[pl.ds(0, 2 * LINE)], send_sem.at[TWIN])
    sent(share_tab.at[pl.ds(0, LINE)], share_send.at[ACROSS])
    sent(share_tab.at[pl.ds(0, 2 * LINE)], share_send.at[TWIN])
    sent(rows.at[pl.ds(0, 5 * SUBS)], row_send.at[ACROSS])
    sent(rows.at[pl.ds(0, 4 * LINE * SUBS)], row_send.at[TWIN])
    sent(part.at[pl.ds(0, 7 * LINE + 2)], back_send.at[0])


def layer(
    cache_len, queries, new_keys, new_values, cache_keys, cache_values, residual, gain, ids, raw,
    o_weight, gate_w, up_w, down_w, devices,
):
    tokens, width = queries.shape
    half = tokens // 2
    vmem = pl.BlockSpec(memory_space=pltpu.VMEM)
    whole = pl.BlockSpec(memory_space=pl.ANY)
    dma = pltpu.SemaphoreType.DMA

    def held(*lead):
        return pltpu.VMEM(lead + (half, D), jnp.bfloat16)

    return pl.pallas_call(
        layer_kernel,
        in_specs=[pl.BlockSpec(memory_space=pltpu.SMEM)] + [vmem] * 6 + [whole] * 7,
        out_specs=vmem,
        out_shape=jax.ShapeDtypeStruct((tokens, D), jnp.bfloat16),
        scratch_shapes=[
            pltpu.VMEM(queries.shape, jnp.bfloat16),
            pltpu.VMEM(cache_keys.shape, jnp.bfloat16),
            pltpu.VMEM(cache_values.shape, jnp.bfloat16),
            pltpu.VMEM((devices,) + o_weight.shape, jnp.bfloat16),
            pltpu.VMEM((tokens, width), jnp.bfloat16),
            pltpu.VMEM((tokens, D), jnp.float32),
            pltpu.VMEM((devices, devices, tokens), jnp.float32),
            pltpu.VMEM((devices, tokens, HEAD), jnp.float32),
            pltpu.VMEM((2 * devices * SUBS, half // SUBS, D), jnp.bfloat16),
            held(2 * devices),
            held(devices),
            held(LINE + 1),
            held(2, LINE, 3),
            pltpu.VMEM((half, D), jnp.float32),
            pltpu.VMEM(gate_w.shape, jnp.bfloat16),
            pltpu.VMEM(up_w.shape, jnp.bfloat16),
            pltpu.VMEM(down_w.shape, jnp.bfloat16),
            dma,
            dma((6,)),
            dma((5,)),
            dma((devices // 2, 3)),
            dma((devices // 2,)),
            dma((4,)),
            dma((devices,)),
            dma((4,)),
            dma((devices * SUBS,)),
            dma((devices // 2,)),
            dma((1,)),
            dma((devices,)),
            dma((LINE + 1,)),
            dma((2, LINE, 3)),
        ],
        compiler_params=pltpu.CompilerParams(
            collective_id=0, has_side_effects=True, vmem_limit_bytes=63 << 20
        ),
    )(
        cache_len, new_keys, new_values, residual, gain, ids, raw, queries, cache_keys, cache_values,
        o_weight, gate_w, up_w, down_w,
    )


def grid_device(
    residual, queries, new_keys, new_values, cache_keys, cache_values, cache_len, o_weight,
    norm_gain, expert_ids, gate_raw, w_gate, w_up, w_down,
):
    devices = lax.axis_size("wide")
    return layer(
        cache_len, queries, new_keys, new_values, cache_keys, cache_values, residual,
        norm_gain.reshape(1, D), expert_ids.T, gate_raw.T, o_weight, w_gate[0], w_up[0], w_down[0], devices,
    )


def per_device(
    residual,
    queries,
    new_keys,
    new_values,
    cache_keys,
    cache_values,
    cache_len,
    o_weight,
    norm_gain,
    expert_ids,
    gate_raw,
    w_gate,
    w_up,
    w_down,
):
    devices = lax.axis_size("wide")
    me = lax.axis_index("wide")
    length = lax.dynamic_slice_in_dim(cache_len, me, 1, 0)
    attn = attention(length, queries, new_keys, new_values, cache_keys, cache_values)
    projected = jnp.dot(
        attn,
        lax.all_gather(o_weight, "wide", axis=0, tiled=True),
        preferred_element_type=jnp.float32,
    )
    mixed = residual.astype(jnp.float32) + projected
    normed = (
        mixed * lax.rsqrt(jnp.mean(mixed * mixed, axis=-1, keepdims=True) + 1e-06) * norm_gain
    ).astype(jnp.bfloat16)
    shares = gate_raw / jnp.sum(gate_raw, axis=-1, keepdims=True)
    routed = sparse_experts(normed, expert_ids, shares, w_gate[0], w_up[0], w_down[0], devices)
    return (mixed + routed).astype(jnp.bfloat16)


def solution(mesh):
    rows = P(("groups", "wide"), None)
    blocks = P(("groups", "wide"), None, None)
    weights = P("wide", None, None)
    placed = (rows, rows, rows, rows, blocks, blocks, P("groups"), P("wide", None), P())
    placed += (rows, rows, weights, weights, weights)
    grid = mesh.shape["wide"] == LINE * PAIR * 2 and mesh.shape["groups"] == 2
    return jax.shard_map(
        grid_device if grid else per_device,
        mesh=mesh,
        in_specs=placed,
        out_specs=rows,
        check_vma=False,
    )
```

```python
import functools
import jax
import jax.numpy as jnp
from jax import lax
from jax.experimental import pallas as pl
from jax.experimental.pallas import tpu as pltpu
from jax.sharding import PartitionSpec as P

D = 2048
HEADS = 16
KV_HEADS = 2
HEAD = 128
TOPK = 8
SPAN = 128
PACK = 2
EXP2_SCALE = HEAD ** (-0.5) * 1.4426950408889634


def attention_kernel(length_ref, q_ref, nk_ref, nv_ref, k_ref, v_ref, out_ref):
    tokens = q_ref.shape[0]
    rows = PACK * tokens
    cache = k_ref.shape[1]
    q = jnp.concatenate([q_ref[:, i * HEAD : (i + 1) * HEAD] for i in range(PACK)], axis=0)
    dims = (((1,), (1,)), ((), ()))
    s = lax.dot_general(q, k_ref[0], dims, preferred_element_type=jnp.float32)
    position = lax.broadcasted_iota(jnp.int32, (1, cache), 1)
    s = jnp.where(position < length_ref[0], s, jnp.float32(-1e30))
    s_new = lax.dot_general(q, nk_ref[...], dims, preferred_element_type=jnp.float32)
    row = lax.broadcasted_iota(jnp.int32, (rows, tokens), 0) % tokens
    column = lax.broadcasted_iota(jnp.int32, (rows, tokens), 1)
    s_new = jnp.where(column <= row, s_new, jnp.float32(-1e30))
    top = jnp.maximum(jnp.max(s, axis=1, keepdims=True), jnp.max(s_new, axis=1, keepdims=True))
    w = jnp.exp2((s - top) * EXP2_SCALE)
    w_new = jnp.exp2((s_new - top) * EXP2_SCALE)
    total = jnp.sum(w, axis=1, keepdims=True) + jnp.sum(w_new, axis=1, keepdims=True)
    out = jnp.dot(w.astype(jnp.bfloat16), v_ref[0], preferred_element_type=jnp.float32)
    out += jnp.dot(w_new.astype(jnp.bfloat16), nv_ref[...], preferred_element_type=jnp.float32)
    out = (out / total).astype(out_ref.dtype)
    for i in range(PACK):
        out_ref[:, i * HEAD : (i + 1) * HEAD] = out[i * tokens : (i + 1) * tokens]


def attention(length, queries, new_keys, new_values, cache_keys, cache_values):
    tokens, width = queries.shape
    cache = cache_keys.shape[1]
    per_group = HEADS // KV_HEADS // PACK
    return pl.pallas_call(
        attention_kernel,
        grid=(HEADS // PACK,),
        in_specs=[
            pl.BlockSpec(memory_space=pltpu.SMEM),
            pl.BlockSpec((tokens, PACK * HEAD), lambda i: (0, i)),
            pl.BlockSpec((tokens, HEAD), lambda i: (0, i // per_group)),
            pl.BlockSpec((tokens, HEAD), lambda i: (0, i // per_group)),
            pl.BlockSpec((1, cache, HEAD), lambda i: (0, 0, i // per_group)),
            pl.BlockSpec((1, cache, HEAD), lambda i: (0, 0, i // per_group)),
        ],
        out_specs=pl.BlockSpec((tokens, PACK * HEAD), lambda i: (0, i)),
        out_shape=jax.ShapeDtypeStruct((tokens, width), jnp.bfloat16),
        cost_estimate=pl.CostEstimate(
            flops=4 * tokens * width * (cache + tokens),
            bytes_accessed=4 * cache * KV_HEADS * HEAD + 4 * tokens * width,
            transcendentals=tokens * HEADS * (cache + tokens),
        ),
    )(length, queries, new_keys, new_values, cache_keys, cache_values)


def run_expert(rows_in, gate_w, up_w, down_w):
    gate_part = jnp.dot(rows_in, gate_w, preferred_element_type=jnp.float32)
    up_part = jnp.dot(rows_in, up_w, preferred_element_type=jnp.float32)
    activated = (jax.nn.silu(gate_part) * up_part).astype(jnp.bfloat16)
    return jnp.dot(activated, down_w, preferred_element_type=jnp.float32)


def sparse_experts(normed, expert_ids, shares, gate_w, up_w, down_w, devices):
    token_count = normed.shape[0]
    capacity = SPAN * TOPK // devices + max(2, SPAN * TOPK // (8 * devices))
    flat_ids = expert_ids.reshape(-1)
    named = expert_ids[:, :, None] == jnp.arange(devices, dtype=jnp.int32)[None, None, :]
    earlier = jnp.tril(jnp.ones((token_count, token_count), jnp.bfloat16), -1)
    before = jnp.dot(
        earlier, jnp.any(named, axis=1).astype(jnp.bfloat16), preferred_element_type=jnp.float32
    )
    ranks = jnp.sum(jnp.where(named, before[:, None, :], 0.0), axis=-1)
    ranks = ranks.astype(jnp.int32).reshape(-1)
    slot_index = flat_ids * capacity + ranks
    token_of = jnp.arange(flat_ids.shape[0], dtype=jnp.int32) // TOPK
    slot_token = (
        jnp.full((devices * capacity,), token_count, jnp.int32).at[slot_index].set(token_of)
    )
    padded = jnp.concatenate([normed, jnp.zeros((1, D), jnp.bfloat16)], axis=0)
    outgoing = padded[slot_token].reshape(devices, capacity, D)
    arrived = lax.all_to_all(outgoing, "wide", split_axis=0, concat_axis=0, tiled=True)
    served = run_expert(arrived.reshape(-1, D), gate_w, up_w, down_w).astype(jnp.bfloat16)
    served = served.reshape(devices, capacity, D)
    returned_rows = lax.all_to_all(served, "wide", split_axis=0, concat_axis=0, tiled=True)
    picked = returned_rows.reshape(devices * capacity, D)[slot_index].reshape(token_count, TOPK, D)
    return jnp.sum(picked.astype(jnp.float32) * shares[..., None], axis=1)


LINE = 4
PAIR = 2
DOWN, UP, ACROSS, TWIN = range(4)


def attend(q, key, value, new_key, new_value, length, tokens):
    rows = q.shape[0]
    dims = (((1,), (1,)), ((), ()))
    s = lax.dot_general(q, key, dims, preferred_element_type=jnp.float32)
    position = lax.broadcasted_iota(jnp.int32, (1, key.shape[0]), 1)
    s = jnp.where(position < length, s, jnp.float32(-1e30))
    s_new = lax.dot_general(q, new_key, dims, preferred_element_type=jnp.float32)
    row = lax.broadcasted_iota(jnp.int32, (rows, tokens), 0) % tokens
    column = lax.broadcasted_iota(jnp.int32, (rows, tokens), 1)
    s_new = jnp.where(column <= row, s_new, jnp.float32(-1e30))
    top = jnp.maximum(jnp.max(s, axis=1, keepdims=True), jnp.max(s_new, axis=1, keepdims=True))
    w = jnp.exp2((s - top) * EXP2_SCALE)
    w_new = jnp.exp2((s_new - top) * EXP2_SCALE)
    total = jnp.sum(w, axis=1, keepdims=True) + jnp.sum(w_new, axis=1, keepdims=True)
    out = jnp.dot(w.astype(jnp.bfloat16), value, preferred_element_type=jnp.float32)
    out += jnp.dot(w_new.astype(jnp.bfloat16), new_value, preferred_element_type=jnp.float32)
    return (out / total).astype(jnp.bfloat16)


class Place:
    def __init__(self):
        self.me = lax.axis_index("wide")
        self.core = self.me % 2
        self.y = (self.me // 2) % PAIR
        self.z = self.me // (2 * PAIR)

    def block(self, z, y, core):
        return (z * PAIR + y) * 2 + core

    def towards(self, way):
        z, y, core = self.z, self.y, self.core
        if way == DOWN:
            return self.block(z - 1, y, core)
        if way == UP:
            return self.block(z + 1, y, core)
        if way == ACROSS:
            return self.block(z, 1 - y, core)
        return self.block(z, y, 1 - core)

    def line_at(self, i):
        low = self.z < LINE // 2
        inner = jnp.where(low, self.z, LINE - 1 - self.z)
        near = jnp.where((inner == 0) | (i >= 2), i, 1 - i)
        return jnp.where(low, near, LINE - 1 - near)

    def barrier(self, with_x=False):
        sem = pltpu.get_barrier_semaphore()

        def greet(way):
            pl.semaphore_signal(
                sem,
                inc=1,
                device_id={"wide": self.towards(way)},
                device_id_type=pl.DeviceIdType.MESH,
            )

        pl.when(self.z > 0)(lambda: greet(DOWN))
        pl.when(self.z < LINE - 1)(lambda: greet(UP))
        greet(ACROSS)
        greet(TWIN)
        if with_x:
            pl.semaphore_signal(
                sem, inc=1, device_id={"groups": 1 - lax.axis_index("groups")},
                device_id_type=pl.DeviceIdType.MESH,
            )
        ends = jnp.where((self.z == 0) | (self.z == LINE - 1), 1, 0)
        pl.semaphore_wait(sem, (5 if with_x else 4) - ends)


UPN, DOWNN = 0, 1
XWAY = 4
TILE = 16
LINE_A, LINE_B, CROSS_A, CROSS_B, A_UP, A_DOWN, ATTEND, READY, PROJECT = range(9)
A_KINDS = {"A": LINE_A, "B": LINE_B, "XA": CROSS_A, "XB": CROSS_B}
A_PLAIN = {"u": A_UP, "d": A_DOWN, "a": ATTEND, "r": READY}
A_END = (
    "a", "a", "a", "0B", "u", "a", "a", "a", "1A", "1B", "a", "2A",
    "a", "3A", "1XA", "2XA", "1XB", "0XB", "r", "2B", "j10", "j21", "j01", "3XA",
    "2XB", "3B", "j00", "j20", "j11", "3XB", "j31", "j30",
)
A_INNER = (
    "a", "a", "2A", "0A", "1B", "u", "d", "a", "a", "3A", "0B", "a",
    "a", "2B", "a", "3B", "a", "1XB", "0XB", "2XA", "3XA", "2XB", "0XA", "3XB",
    "r", "j11", "j21", "j20", "j30", "j01", "j31", "j10", "j00",
)


def gather_code(text):
    if text[0] in A_PLAIN:
        return A_PLAIN[text[0]] * 8
    if text[0] == "j":
        return PROJECT * 8 + int(text[1]) * 2 + int(text[2])
    return A_KINDS[text[1:]] * 8 + int(text[0]) * 2


def packed(codes, words, bits):
    codes = codes + [(1 << bits) - 1] * (words * (28 // bits) - len(codes))
    per = 28 // bits
    return [
        sum(c << (bits * j) for j, c in enumerate(codes[per * w : per * w + per]))
        for w in range(words)
    ]


def pick(index, inner, ends, inners):
    at_end, at_inner = jnp.int32(ends[0]), jnp.int32(inners[0])
    for k in range(1, len(ends)):
        at_end = jnp.where(index == k, jnp.int32(ends[k]), at_end)
        at_inner = jnp.where(index == k, jnp.int32(inners[k]), at_inner)
    return jnp.where(inner == 1, at_inner, at_end)


PIECES = "abcd"
GET, UP_OWN, DOWN_OWN, PASS_OWN, SERVE, PAIR_UP, FOLD, FINISH = range(8)
KINDS = {"g": GET, "u": UP_OWN, "d": DOWN_OWN, "y": PASS_OWN}
KINDS.update({"s": SERVE, "p": PAIR_UP, "f": FOLD, "z": FINISH})
PA, PB, PC, PD = range(4)
SUBS = 2
B_END = (
    "ya1", "uc0", "uc1", "ya0", "g0b1", "yc1", "ua1", "g0b0", "ub1", "ua0", "s01", "g1b0",
    "yc0", "g0d1", "g1b1", "g1a0", "g1a1", "ub0", "g3c0", "g3c1", "s11", "g3d1", "g3d0", "f12",
    "s30", "g3a1", "g0d0", "p3", "f11", "s00", "g3a0", "g3b1", "g3b0", "g2c1", "p0", "f30",
    "s31", "g2b1", "f32", "g2a1", "g2b0", "g2a0", "g2d1", "f31", "g2c0", "s21", "g1c1", "g2d0",
    "f22", "g1c0", "s20", "g1d1", "f21", "g1d0", "p2", "s10", "p1", "f20", "z2", "z0",
    "f10", "z1",
)
B_INNER = (
    "da1", "ya1", "uc1", "ya0", "da0", "ua0", "g0c0", "g1b1", "db1", "g1b0", "db0", "yc1",
    "g0c1", "g0a1", "yc0", "g3c0", "g3c1", "g2a0", "g0b1", "g0d0", "s11", "g2c1", "g0a0", "g0b0",
    "g0d1", "ub1", "g3a1", "ua1", "s00", "uc0", "g3d0", "g3d1", "g3a0", "g1d0", "g3b1", "s30",
    "g3b0", "p3", "g2d1", "g2b1", "g2a1", "ub0", "g1d1", "s31", "g2b0", "p0", "s01", "g2c0",
    "dc1", "f30", "s21", "g2d0", "dc0", "f32", "s20", "f00", "f31", "s10", "p2", "f22",
    "p1", "f02", "f21", "f01", "z2", "f20", "z1", "z0",
)


def code_of(text):
    kind = KINDS[text[0]] * 32
    if kind == GET * 32:
        return kind + int(text[1]) * 8 + PIECES.index(text[2]) * 2 + int(text[3])
    if kind in (UP_OWN * 32, DOWN_OWN * 32, PASS_OWN * 32):
        return kind + PIECES.index(text[1]) * 2 + int(text[2])
    if kind == PAIR_UP * 32:
        return kind + int(text[1]) * 8
    if kind == FINISH * 32:
        return kind + int(text[1]) * 2
    return kind + int(text[1]) * 8 + int(text[2]) * 2


def first_serve(program):
    return [text[0] for text in program].index("s")


def layer_kernel(
    length_ref, nk_ref, nv_ref, res_ref, gain_ref, ids_ref, raw_ref, q_hbm, k_hbm, v_hbm, ow_ref,
    wg_ref, wu_ref, wd_ref, out_ref, q_ref, k_ref, v_ref,
    held, attn, mixed_ref, res_pair, squares, share_tab, share_col, rows, part, from_twin,
    from_pair, from_line, acc, wg, wu, wd,
    own_sem, load_sem, send_sem, recv_sem, recv_twin, near_send, near_recv, share_send,
    share_recv, row_send, row_recv, twin_rows, back_send, twin_sem, pair_sem, line_sem,
):
    place = Place()
    z, y, core = place.z, place.y, place.core
    group = lax.axis_index("groups")
    tokens = res_ref.shape[0]
    depth, wide = ow_ref.shape[0], ow_ref.shape[1] // 2
    low = z < LINE // 2
    inner = jnp.where(low, z, LINE - 1 - z)
    step_up = jnp.where(low, 1, -1)
    me = place.me
    my_columns = pl.ds(pl.multiple_of(y * wide, wide), wide)
    pair_columns = pl.ds(pl.multiple_of((1 - y) * wide, wide), wide)
    own = pltpu.make_async_copy(ow_ref.at[:, my_columns], held.at[me], own_sem)
    own.start()
    pairs = ((q_hbm, q_ref), (k_hbm, k_ref), (v_hbm, v_ref), (wg_ref, wg), (wu_ref, wu), (wd_ref, wd))
    fetches = [
        pltpu.make_async_copy(source, dest, load_sem.at[k])
        for k, (source, dest) in enumerate(pairs)
    ]
    fetches, loads = fetches[:3], fetches[3:]
    for fetch in fetches:
        fetch.start()
    place.barrier(True)

    short = depth // 8 * 3
    long = depth - short
    line_rows = pl.ds(pl.multiple_of(jnp.where(group == 0, 0, short), TILE), long)
    give_rows = pl.ds(pl.multiple_of(jnp.where(group == 0, 0, long), TILE), short)
    take_rows = pl.ds(pl.multiple_of(jnp.where(group == 0, long, 0), TILE), short)

    def real(nb):
        return jnp.where(low, nb, LINE - 1 - nb)

    def device(way):
        if way == XWAY:
            return {"groups": 1 - group}
        if way == UPN:
            return {"wide": place.block(z + step_up, y, core)}
        if way == DOWNN:
            return {"wide": place.block(z - step_up, y, core)}
        return {"wide": place.towards(way)}

    def send(source, dest, send_one, recv_one, way):
        return pltpu.make_async_remote_copy(
            src_ref=source, dst_ref=dest, send_sem=send_one, recv_sem=recv_one,
            device_id=device(way), device_id_type=pl.DeviceIdType.MESH,
        )

    def copy(b, way):
        ref = held.at[b, give_rows if way == XWAY else line_rows]
        if way == TWIN:
            return send(ref, ref, send_sem.at[way], recv_twin.at[b // 2], way)
        kind = 1 if way == XWAY else 0
        return send(ref, ref, send_sem.at[way], recv_sem.at[b // 2, kind], way)

    def taken(b):
        ref = held.at[b, take_rows]
        return (
            send(ref, ref, send_sem.at[XWAY], recv_sem.at[b // 2, 1], XWAY),
            send(ref, ref, send_sem.at[TWIN], recv_twin.at[b // 2], TWIN),
        )

    def whole(b):
        return send(held.at[b], held.at[b], send_sem.at[TWIN], recv_twin.at[b // 2], TWIN)

    def share_copy(b, way):
        return send(share_tab.at[b], share_tab.at[b], share_send.at[way], share_recv.at[b], way)

    def block_at(nb, yb, c):
        return place.block(real(nb), yb, c)

    send(
        ow_ref.at[line_rows, pair_columns], held.at[me, line_rows], send_sem.at[ACROSS],
        recv_sem.at[me // 2, 0], ACROSS,
    ).start()
    own.wait()
    copy(me, UPN).start()
    pl.when(inner == 1)(copy(me, DOWNN).start)
    whole(me).start()
    raw = raw_ref[...]
    given_share = raw / jnp.sum(raw, axis=0, keepdims=True)
    expert = lax.broadcasted_iota(jnp.int32, (share_tab.shape[1], 1), 0)
    table = jnp.zeros(share_tab.shape[1:], jnp.float32)
    for k in range(TOPK):
        hit = ids_ref[k : k + 1] == expert
        table = table + jnp.where(hit, given_share[k : k + 1], 0.0)
    share_tab[me] = table
    share_copy(me, UPN).start()
    pl.when(inner == 1)(share_copy(me, DOWNN).start)
    share_copy(me, ACROSS).start()
    share_copy(me, TWIN).start()
    attn_all = attn.at[pl.ds(tokens, tokens)]
    residual_sent = send(
        res_ref.at[:, pair_columns], res_pair, near_send.at[1], near_recv.at[1], ACROSS
    )

    def onward(b, nb, copier):
        pl.when(nb < inner)(copier(b, UPN).start)
        pl.when((nb > inner) & (inner == 1))(copier(b, DOWNN).start)

    def happen(code, turn):
        nb = lax.rem(code // 2, 4)
        flag = lax.rem(code, 2)
        kind = code // 8
        own_b = block_at(nb, y, core)
        other_b = block_at(nb, 1 - y, core)

        @pl.when(kind == LINE_A)
        def _():
            copy(own_b, ACROSS).wait_recv()
            onward(own_b, nb, copy)
            copy(own_b, XWAY).start()
            copy(own_b, TWIN).start()
            share_copy(own_b, TWIN).wait_recv()
            onward(own_b, nb, share_copy)
            share_copy(own_b, ACROSS).start()
            share_copy(own_b, TWIN).start()

        @pl.when(kind == LINE_B)
        def _():
            copy(other_b, ACROSS).wait_recv()
            onward(other_b, nb, copy)
            copy(other_b, XWAY).start()
            copy(other_b, TWIN).start()
            share_copy(other_b, TWIN).wait_recv()
            share_copy(other_b, TWIN).start()

        @pl.when((kind == CROSS_A) | (kind == CROSS_B))
        def _():
            arrival, forward = taken(jnp.where(kind == CROSS_A, own_b, other_b))
            arrival.wait_recv()
            forward.start()

        fresh = block_at(inner, 1 - y, core)
        pl.when(kind == A_UP)(copy(fresh, UPN).start)
        pl.when(kind == A_DOWN)(copy(fresh, DOWNN).start)

        @pl.when(kind == ATTEND)
        def _():
            @pl.when(turn == 0)
            def _():
                for load in loads:
                    load.start()
                for fetch in fetches:
                    fetch.wait()

            attend_step(turn)
            columns = pl.ds(pl.multiple_of(turn * PACK * HEAD, HEAD), PACK * HEAD)
            send(
                attn.at[pl.ds(0, tokens), columns], attn.at[pl.ds(tokens, tokens), columns],
                near_send.at[0], near_recv.at[0], ACROSS,
            ).start()

        @pl.when(kind == READY)
        def _():
            residual_sent.start()
            send(attn_all, attn_all, near_send.at[0], near_recv.at[0], ACROSS).wait_recv()

        pl.when(kind == PROJECT)(lambda: project(nb, flag == 1))

    length = length_ref[place.me]
    per_group = HEADS // KV_HEADS // PACK

    def attend_step(i):
        q = jnp.concatenate(
            [
                q_ref[:, pl.ds(pl.multiple_of((i * PACK + j) * HEAD, HEAD), HEAD)]
                for j in range(PACK)
            ],
            axis=0,
        )
        columns = pl.ds(pl.multiple_of(i // per_group * HEAD, HEAD), HEAD)
        out = attend(
            q, k_ref[0, :, columns], v_ref[0, :, columns], nk_ref[:, columns],
            nv_ref[:, columns], length, tokens,
        )
        for j in range(PACK):
            attn[:tokens, pl.ds(pl.multiple_of((i * PACK + j) * HEAD, HEAD), HEAD)] = out[
                j * tokens : (j + 1) * tokens
            ]

    mixed_ref[...] = jnp.zeros(mixed_ref.shape, jnp.float32)
    chosen = lax.broadcasted_iota(jnp.int32, (1, share_tab.shape[1]), 1) == me

    def project(nb, is_own):
        yb = jnp.where(is_own, y, 1 - y)
        b = block_at(nb, yb, 1 - core)

        whole(b).wait_recv()
        share_copy(b, TWIN).wait_recv()
        first = block_at(nb, yb, 0)
        for c in range(2):
            turned = share_tab[first + c].T
            column = jnp.sum(jnp.where(chosen, turned, 0.0), axis=1, keepdims=True)
            share_col[first + c] = jnp.broadcast_to(column, share_col.shape[1:])
        mine = attn[:, pl.ds(pl.multiple_of(first * depth, 2 * depth), 2 * depth)]
        weight = held[pl.ds(first, 2)].reshape(2 * depth, wide)
        mixed_ref[...] += jnp.dot(mine, weight, preferred_element_type=jnp.float32)

    a_words = -(-max(len(A_END), len(A_INNER)) // 4)
    a_end = packed([gather_code(text) for text in A_END], a_words, 7)
    a_inner = packed([gather_code(text) for text in A_INNER], a_words, 7)

    def gather_route(w, turn):
        def one(j, state):
            word, at = state
            code = lax.rem(word, 128)
            happen(code, at)
            return word // 128, at + jnp.where(code // 8 == ATTEND, 1, 0)

        return lax.fori_loop(0, 4, one, (pick(w, inner, a_end, a_inner), turn))[1]

    lax.fori_loop(0, a_words, gather_route, jnp.int32(0))
    half_rows = tokens // 2
    residual_sent.wait_recv()
    mixed_ref[:tokens] += res_ref[:, my_columns].astype(jnp.float32)
    mixed_ref[tokens:] += res_pair[...].astype(jnp.float32)
    mixed = mixed_ref[...]
    square = jnp.sum(mixed * mixed, axis=1, keepdims=True)
    squares[0] = jnp.broadcast_to(square, (2 * tokens, HEAD)).T[: squares.shape[1]]
    square_sent = send(squares.at[0], squares.at[1], near_send.at[2], near_recv.at[2], ACROSS)
    square_sent.start()
    square_sent.wait_recv()
    theirs = squares[1].T[:, :1]
    theirs = jnp.concatenate([theirs[tokens:], theirs[:tokens]], axis=0)
    scale = lax.rsqrt((square + theirs) * (1.0 / D) + 1e-06)
    normed = (mixed * scale * gain_ref[:, my_columns]).astype(jnp.bfloat16)

    def slot(zb, p, yb, c):
        return ((zb * 2 + p) * PAIR + yb) * 2 + c

    for p in range(2):
        base = slot(z, p, y, core) * SUBS
        rows[base + y] = normed[p * half_rows : (p + 1) * half_rows]
        rows[base + 1 - y] = normed[tokens + p * half_rows : tokens + (p + 1) * half_rows]

    def row_copy(b, h, way):
        t = b * SUBS + h
        landed = twin_rows.at[b // 4] if way == TWIN else row_recv.at[b // 2 * SUBS + h]
        return send(rows.at[t], rows.at[t], row_send.at[way], landed, way)

    def to_twin(zb, p, yb):
        b = slot(zb, p, yb, 1 - core)
        t = (zb * 2 + p) * PAIR + yb
        return send(part.at[b], from_twin.at[t], back_send.at[0], twin_sem.at[t], TWIN)

    def to_pair(zb, p):
        b = slot(zb, p, 1 - y, core)
        t = LINE if p else zb
        return send(part.at[b], from_pair.at[t], back_send.at[0], pair_sem.at[t], ACROSS)

    def kind_slot(zb, kind):
        p = jnp.minimum(kind, 1)
        yb = jnp.where(kind == 2, 1 - y, y)
        return p, yb, slot(zb, p, yb, core)

    side_up = jnp.where(low, 0, 1)

    def to_line(zb, kind, way):
        b = kind_slot(zb, kind)[2]
        side = side_up if way == UPN else 1 - side_up
        return send(
            part.at[b], from_line.at[side, zb, kind], back_send.at[0],
            line_sem.at[side, zb, kind], way,
        )

    def serve(zb, p):
        first = slot(zb, p, 0, 0)
        bulk = rows.at[pl.ds(0, 2 * SUBS)]
        send(bulk, bulk, row_send.at[TWIN], twin_rows.at[first // 4], TWIN).wait_recv()
        here = pl.ds(pl.multiple_of(p * half_rows, half_rows), half_rows)
        block = place.block(zb, 0, 0)
        share = jnp.concatenate(
            [share_col[block + yb * 2 + c, here] for c in range(2) for yb in range(2)], axis=0
        )
        sides = [
            rows[pl.ds((first + 2 * k) * SUBS, 2 * SUBS)].reshape(4 * half_rows, wide)
            for k in range(2)
        ]

        def times(w):
            return jnp.dot(sides[0], w[:wide], preferred_element_type=jnp.float32) + jnp.dot(
                sides[1], w[wide:], preferred_element_type=jnp.float32
            )

        gate, up = times(wg), times(wu)
        act = (gate / (1.0 + jnp.exp(-gate)) * up).astype(jnp.bfloat16)
        out = jnp.dot(act, wd[...], preferred_element_type=jnp.float32) * share[:, :1]
        out = out.astype(jnp.bfloat16)
        for k in range(4):
            part[first + k % 2 * 2 + k // 2] = out[k * half_rows : (k + 1) * half_rows]
        to_twin(zb, p, 0).start()
        to_twin(zb, p, 1).start()

    def with_twin(zb, p, yb):
        to_twin(zb, p, yb).wait_recv()
        b = slot(zb, p, yb, core)
        t = (zb * 2 + p) * PAIR + yb
        return part[b].astype(jnp.float32) + from_twin[t].astype(jnp.float32)

    def add_line(zb, kind, way):
        to_line(zb, kind, way).wait_recv()
        side = side_up if way == UPN else 1 - side_up
        acc[...] += from_line[side, zb, kind].astype(jnp.float32)

    def fold(nb, kind):
        zb = real(nb)
        p, yb, b = kind_slot(zb, kind)
        acc[...] = with_twin(zb, p, yb)

        @pl.when(kind == 0)
        def _():
            to_pair(zb, 0).wait_recv()
            acc[...] += from_pair[zb].astype(jnp.float32)

        pl.when((nb > inner) & (inner == 1))(lambda: add_line(zb, kind, UPN))
        pl.when(nb < inner)(lambda: add_line(zb, kind, DOWNN))
        part[b] = acc[...].astype(jnp.bfloat16)
        pl.when(nb > inner)(to_line(zb, kind, UPN).start)
        pl.when(nb < inner)(to_line(zb, kind, DOWNN).start)

    def finish(kind):
        p, yb, b = kind_slot(z, kind)
        acc[...] = with_twin(z, p, yb)
        pl.when(inner == 1)(lambda: add_line(z, kind, UPN))
        add_line(z, kind, DOWNN)

        @pl.when(kind == 2)
        def _():
            acc[:, my_columns] += mixed_ref[pl.ds(tokens + half_rows, half_rows)]
            part[b] = acc[...].astype(jnp.bfloat16)
            to_pair(z, 1).start()

        def close(p, t):
            here = pl.ds(p * half_rows, half_rows)
            to_pair(z, p).wait_recv()
            acc[:, my_columns] += mixed_ref[here]
            out_ref[here] = (acc[...] + from_pair[t].astype(jnp.float32)).astype(jnp.bfloat16)

        pl.when(kind == 0)(lambda: close(0, z))
        pl.when(kind == 1)(lambda: close(1, LINE))

    def act_on(code, first):
        kind = code // 32
        nb = lax.rem(code // 8, 4)
        piece = lax.rem(code // 2, 4)
        h = lax.rem(code, 2)
        zb = real(nb)
        p = jnp.where(piece <= PB, 1, 0)
        yb = jnp.where((piece == PA) | (piece == PC), y, 1 - y)
        own_piece = slot(z, p, yb, core)

        @pl.when(kind == GET)
        def _():
            b = slot(zb, p, yb, core)
            row_copy(b, h, ACROSS).wait_recv()
            onward = piece != PD
            pl.when(onward & (nb < inner))(row_copy(b, h, UPN).start)
            pl.when(onward & (nb > inner) & (inner == 1))(row_copy(b, h, DOWNN).start)
            pl.when((piece == PC) & (nb != inner))(row_copy(b, h, ACROSS).start)
            row_copy(b, h, TWIN).start()

        pl.when(kind == UP_OWN)(row_copy(own_piece, h, UPN).start)
        pl.when(kind == DOWN_OWN)(row_copy(own_piece, h, DOWNN).start)

        @pl.when(kind == PASS_OWN)
        def _():
            row_copy(own_piece, h, ACROSS).start()
            row_copy(own_piece, h, TWIN).start()

        @pl.when(kind == SERVE)
        def _():
            @pl.when(first)
            def _():
                for load in loads:
                    load.wait()

            serve(zb, piece)

        @pl.when(kind == PAIR_UP)
        def _():
            acc[...] = with_twin(zb, 0, 1 - y)

            @pl.when(nb == inner)
            def _():
                acc[:, my_columns] += mixed_ref[pl.ds(tokens, half_rows)]

            part[slot(zb, 0, 1 - y, core)] = acc[...].astype(jnp.bfloat16)
            to_pair(zb, 0).start()

        pl.when(kind == FOLD)(lambda: fold(nb, piece))
        pl.when((kind == FINISH) & (piece < 3))(lambda: finish(piece))

    words = -(-max(len(B_END), len(B_INNER)) // 3)
    end_words = packed([code_of(text) for text in B_END], words, 9)
    inner_words = packed([code_of(text) for text in B_INNER], words, 9)
    serve_at = jnp.where(inner == 1, first_serve(B_INNER), first_serve(B_END))

    def route(w, carry):
        def one(j, word):
            act_on(lax.rem(word, 512), w * 3 + j == serve_at)
            return word // 512

        lax.fori_loop(0, 3, one, pick(w, inner, end_words, inner_words))
        return carry

    lax.fori_loop(0, words, route, 0)

    def sent(ref, sem, way=TWIN):
        send(ref, ref, sem, share_recv.at[0], way).wait_send()

    def sent_by_place(at_end, at_inner):
        pl.when(inner == 0)(at_end)
        pl.when(inner == 1)(at_inner)

    lines = pl.ds(0, long)
    sent_by_place(
        lambda: sent(held.at[pl.ds(0, 2), lines], send_sem.at[UPN]),
        lambda: sent(held.at[pl.ds(0, 4), lines], send_sem.at[UPN]),
    )
    sent_by_place(
        lambda: sent(share_tab.at[pl.ds(0, 1)], share_send.at[UPN]),
        lambda: sent(share_tab.at[pl.ds(0, 2)], share_send.at[UPN]),
    )
    sent_by_place(
        lambda: sent(rows.at[pl.ds(0, 3 * SUBS)], row_send.at[UPN]),
        lambda: sent(rows.at[pl.ds(0, 6 * SUBS)], row_send.at[UPN]),
    )

    @pl.when(inner == 1)
    def _():
        sent(held.at[pl.ds(0, 6), lines], send_sem.at[DOWNN])
        sent(share_tab.at[pl.ds(0, 3)], share_send.at[DOWNN])
        sent(rows.at[pl.ds(0, 9 * SUBS)], row_send.at[DOWNN])

    sent(held.at[0, lines], send_sem.at[ACROSS])
    sent(held.at[pl.ds(0, 2 * LINE - 1), pl.ds(0, short)], send_sem.at[XWAY])
    sent(attn_all, near_send.at[0])
    residual_sent.wait_send()
    square_sent.wait_send()
    sent(held.at[pl.ds(0, 2 * LINE)], send_sem.at[TWIN])
    sent(share_tab.at[pl.ds(0, LINE)], share_send.at[ACROSS])
    sent(share_tab.at[pl.ds(0, 2 * LINE)], share_send.at[TWIN])
    sent(rows.at[pl.ds(0, 5 * SUBS)], row_send.at[ACROSS])
    sent(rows.at[pl.ds(0, 4 * LINE * SUBS)], row_send.at[TWIN])
    sent(part.at[pl.ds(0, 7 * LINE + 2)], back_send.at[0])


def layer(
    cache_len, queries, new_keys, new_values, cache_keys, cache_values, residual, gain, ids, raw,
    o_weight, gate_w, up_w, down_w, devices,
):
    tokens, width = queries.shape
    half = tokens // 2
    vmem = pl.BlockSpec(memory_space=pltpu.VMEM)
    whole = pl.BlockSpec(memory_space=pl.ANY)
    dma = pltpu.SemaphoreType.DMA

    def held(*lead):
        return pltpu.VMEM(lead + (half, D), jnp.bfloat16)

    return pl.pallas_call(
        layer_kernel,
        in_specs=[pl.BlockSpec(memory_space=pltpu.SMEM)] + [vmem] * 6 + [whole] * 7,
        out_specs=vmem,
        out_shape=jax.ShapeDtypeStruct((tokens, D), jnp.bfloat16),
        scratch_shapes=[
            pltpu.VMEM(queries.shape, jnp.bfloat16),
            pltpu.VMEM(cache_keys.shape, jnp.bfloat16),
            pltpu.VMEM(cache_values.shape, jnp.bfloat16),
            pltpu.VMEM((devices, o_weight.shape[0], D // 2), jnp.bfloat16),
            pltpu.VMEM((2 * tokens, width), jnp.bfloat16),
            pltpu.VMEM((2 * tokens, D // 2), jnp.float32),
            pltpu.VMEM((tokens, D // 2), jnp.bfloat16),
            pltpu.VMEM((2, 8, 2 * tokens), jnp.float32),
            pltpu.VMEM((devices, devices, tokens), jnp.float32),
            pltpu.VMEM((devices, tokens, HEAD), jnp.float32),
            pltpu.VMEM((2 * devices * SUBS, half, D // 2), jnp.bfloat16),
            held(2 * devices),
            held(devices),
            held(LINE + 1),
            held(2, LINE, 3),
            pltpu.VMEM((half, D), jnp.float32),
            pltpu.VMEM(gate_w.shape, jnp.bfloat16),
            pltpu.VMEM(up_w.shape, jnp.bfloat16),
            pltpu.VMEM(down_w.shape, jnp.bfloat16),
            dma,
            dma((6,)),
            dma((5,)),
            dma((devices // 2, 2)),
            dma((devices // 2,)),
            dma((3,)),
            dma((3,)),
            dma((4,)),
            dma((devices,)),
            dma((4,)),
            dma((devices * SUBS,)),
            dma((devices // 2,)),
            dma((1,)),
            dma((devices,)),
            dma((LINE + 1,)),
            dma((2, LINE, 3)),
        ],
        compiler_params=pltpu.CompilerParams(
            collective_id=0, has_side_effects=True, vmem_limit_bytes=63 << 20
        ),
    )(
        cache_len, new_keys, new_values, residual, gain, ids, raw, queries, cache_keys, cache_values,
        o_weight, gate_w, up_w, down_w,
    )


def grid_device(
    residual, queries, new_keys, new_values, cache_keys, cache_values, cache_len, o_weight,
    norm_gain, expert_ids, gate_raw, w_gate, w_up, w_down,
):
    devices = lax.axis_size("wide")
    return layer(
        cache_len, queries, new_keys, new_values, cache_keys, cache_values, residual,
        norm_gain.reshape(1, D), expert_ids.T, gate_raw.T, o_weight, w_gate[0], w_up[0], w_down[0], devices,
    )


def per_device(
    residual,
    queries,
    new_keys,
    new_values,
    cache_keys,
    cache_values,
    cache_len,
    o_weight,
    norm_gain,
    expert_ids,
    gate_raw,
    w_gate,
    w_up,
    w_down,
):
    devices = lax.axis_size("wide")
    me = lax.axis_index("wide")
    length = lax.dynamic_slice_in_dim(cache_len, me, 1, 0)
    attn = attention(length, queries, new_keys, new_values, cache_keys, cache_values)
    projected = jnp.dot(
        attn,
        lax.all_gather(o_weight, "wide", axis=0, tiled=True),
        preferred_element_type=jnp.float32,
    )
    mixed = residual.astype(jnp.float32) + projected
    normed = (
        mixed * lax.rsqrt(jnp.mean(mixed * mixed, axis=-1, keepdims=True) + 1e-06) * norm_gain
    ).astype(jnp.bfloat16)
    shares = gate_raw / jnp.sum(gate_raw, axis=-1, keepdims=True)
    routed = sparse_experts(normed, expert_ids, shares, w_gate[0], w_up[0], w_down[0], devices)
    return (mixed + routed).astype(jnp.bfloat16)


def solution(mesh):
    rows = P(("groups", "wide"), None)
    blocks = P(("groups", "wide"), None, None)
    weights = P("wide", None, None)
    placed = (rows, rows, rows, rows, blocks, blocks, P("groups"), P("wide", None), P())
    placed += (rows, rows, weights, weights, weights)
    grid = mesh.shape["wide"] == LINE * PAIR * 2 and mesh.shape["groups"] == 2
    return jax.shard_map(
        grid_device if grid else per_device,
        mesh=mesh,
        in_specs=placed,
        out_specs=rows,
        check_vma=False,
    )
```

```python
import functools
import jax
import jax.numpy as jnp
from jax import lax
from jax.experimental import pallas as pl
from jax.experimental.pallas import tpu as pltpu
from jax.sharding import PartitionSpec as P

D = 2048
HEADS = 16
KV_HEADS = 2
HEAD = 128
TOPK = 8
SPAN = 128
PACK = 2
EXP2_SCALE = HEAD ** (-0.5) * 1.4426950408889634


def attention_kernel(length_ref, q_ref, nk_ref, nv_ref, k_ref, v_ref, out_ref):
    tokens = q_ref.shape[0]
    rows = PACK * tokens
    cache = k_ref.shape[1]
    q = jnp.concatenate([q_ref[:, i * HEAD : (i + 1) * HEAD] for i in range(PACK)], axis=0)
    dims = (((1,), (1,)), ((), ()))
    s = lax.dot_general(q, k_ref[0], dims, preferred_element_type=jnp.float32)
    position = lax.broadcasted_iota(jnp.int32, (1, cache), 1)
    s = jnp.where(position < length_ref[0], s, jnp.float32(-1e30))
    s_new = lax.dot_general(q, nk_ref[...], dims, preferred_element_type=jnp.float32)
    row = lax.broadcasted_iota(jnp.int32, (rows, tokens), 0) % tokens
    column = lax.broadcasted_iota(jnp.int32, (rows, tokens), 1)
    s_new = jnp.where(column <= row, s_new, jnp.float32(-1e30))
    top = jnp.maximum(jnp.max(s, axis=1, keepdims=True), jnp.max(s_new, axis=1, keepdims=True))
    w = jnp.exp2((s - top) * EXP2_SCALE)
    w_new = jnp.exp2((s_new - top) * EXP2_SCALE)
    total = jnp.sum(w, axis=1, keepdims=True) + jnp.sum(w_new, axis=1, keepdims=True)
    out = jnp.dot(w.astype(jnp.bfloat16), v_ref[0], preferred_element_type=jnp.float32)
    out += jnp.dot(w_new.astype(jnp.bfloat16), nv_ref[...], preferred_element_type=jnp.float32)
    out = (out / total).astype(out_ref.dtype)
    for i in range(PACK):
        out_ref[:, i * HEAD : (i + 1) * HEAD] = out[i * tokens : (i + 1) * tokens]


def attention(length, queries, new_keys, new_values, cache_keys, cache_values):
    tokens, width = queries.shape
    cache = cache_keys.shape[1]
    per_group = HEADS // KV_HEADS // PACK
    return pl.pallas_call(
        attention_kernel,
        grid=(HEADS // PACK,),
        in_specs=[
            pl.BlockSpec(memory_space=pltpu.SMEM),
            pl.BlockSpec((tokens, PACK * HEAD), lambda i: (0, i)),
            pl.BlockSpec((tokens, HEAD), lambda i: (0, i // per_group)),
            pl.BlockSpec((tokens, HEAD), lambda i: (0, i // per_group)),
            pl.BlockSpec((1, cache, HEAD), lambda i: (0, 0, i // per_group)),
            pl.BlockSpec((1, cache, HEAD), lambda i: (0, 0, i // per_group)),
        ],
        out_specs=pl.BlockSpec((tokens, PACK * HEAD), lambda i: (0, i)),
        out_shape=jax.ShapeDtypeStruct((tokens, width), jnp.bfloat16),
        cost_estimate=pl.CostEstimate(
            flops=4 * tokens * width * (cache + tokens),
            bytes_accessed=4 * cache * KV_HEADS * HEAD + 4 * tokens * width,
            transcendentals=tokens * HEADS * (cache + tokens),
        ),
    )(length, queries, new_keys, new_values, cache_keys, cache_values)


def run_expert(rows_in, gate_w, up_w, down_w):
    gate_part = jnp.dot(rows_in, gate_w, preferred_element_type=jnp.float32)
    up_part = jnp.dot(rows_in, up_w, preferred_element_type=jnp.float32)
    activated = (jax.nn.silu(gate_part) * up_part).astype(jnp.bfloat16)
    return jnp.dot(activated, down_w, preferred_element_type=jnp.float32)


def sparse_experts(normed, expert_ids, shares, gate_w, up_w, down_w, devices):
    token_count = normed.shape[0]
    capacity = SPAN * TOPK // devices + max(2, SPAN * TOPK // (8 * devices))
    flat_ids = expert_ids.reshape(-1)
    named = expert_ids[:, :, None] == jnp.arange(devices, dtype=jnp.int32)[None, None, :]
    earlier = jnp.tril(jnp.ones((token_count, token_count), jnp.bfloat16), -1)
    before = jnp.dot(
        earlier, jnp.any(named, axis=1).astype(jnp.bfloat16), preferred_element_type=jnp.float32
    )
    ranks = jnp.sum(jnp.where(named, before[:, None, :], 0.0), axis=-1)
    ranks = ranks.astype(jnp.int32).reshape(-1)
    slot_index = flat_ids * capacity + ranks
    token_of = jnp.arange(flat_ids.shape[0], dtype=jnp.int32) // TOPK
    slot_token = (
        jnp.full((devices * capacity,), token_count, jnp.int32).at[slot_index].set(token_of)
    )
    padded = jnp.concatenate([normed, jnp.zeros((1, D), jnp.bfloat16)], axis=0)
    outgoing = padded[slot_token].reshape(devices, capacity, D)
    arrived = lax.all_to_all(outgoing, "wide", split_axis=0, concat_axis=0, tiled=True)
    served = run_expert(arrived.reshape(-1, D), gate_w, up_w, down_w).astype(jnp.bfloat16)
    served = served.reshape(devices, capacity, D)
    returned_rows = lax.all_to_all(served, "wide", split_axis=0, concat_axis=0, tiled=True)
    picked = returned_rows.reshape(devices * capacity, D)[slot_index].reshape(token_count, TOPK, D)
    return jnp.sum(picked.astype(jnp.float32) * shares[..., None], axis=1)


LINE = 4
PAIR = 2
DOWN, UP, ACROSS, TWIN = range(4)


def attend(q, key, value, new_key, new_value, length, tokens):
    rows = q.shape[0]
    dims = (((1,), (1,)), ((), ()))
    s = lax.dot_general(q, key, dims, preferred_element_type=jnp.float32)
    position = lax.broadcasted_iota(jnp.int32, (1, key.shape[0]), 1)
    s = jnp.where(position < length, s, jnp.float32(-1e30))
    s_new = lax.dot_general(q, new_key, dims, preferred_element_type=jnp.float32)
    row = lax.broadcasted_iota(jnp.int32, (rows, tokens), 0) % tokens
    column = lax.broadcasted_iota(jnp.int32, (rows, tokens), 1)
    s_new = jnp.where(column <= row, s_new, jnp.float32(-1e30))
    top = jnp.maximum(jnp.max(s, axis=1, keepdims=True), jnp.max(s_new, axis=1, keepdims=True))
    w = jnp.exp2((s - top) * EXP2_SCALE)
    w_new = jnp.exp2((s_new - top) * EXP2_SCALE)
    total = jnp.sum(w, axis=1, keepdims=True) + jnp.sum(w_new, axis=1, keepdims=True)
    out = jnp.dot(w.astype(jnp.bfloat16), value, preferred_element_type=jnp.float32)
    out += jnp.dot(w_new.astype(jnp.bfloat16), new_value, preferred_element_type=jnp.float32)
    return (out / total).astype(jnp.bfloat16)


class Place:
    def __init__(self):
        self.me = lax.axis_index("wide")
        self.core = self.me % 2
        self.y = (self.me // 2) % PAIR
        self.z = self.me // (2 * PAIR)

    def block(self, z, y, core):
        return (z * PAIR + y) * 2 + core

    def towards(self, way):
        z, y, core = self.z, self.y, self.core
        if way == DOWN:
            return self.block(z - 1, y, core)
        if way == UP:
            return self.block(z + 1, y, core)
        if way == ACROSS:
            return self.block(z, 1 - y, core)
        return self.block(z, y, 1 - core)

    def line_at(self, i):
        low = self.z < LINE // 2
        inner = jnp.where(low, self.z, LINE - 1 - self.z)
        near = jnp.where((inner == 0) | (i >= 2), i, 1 - i)
        return jnp.where(low, near, LINE - 1 - near)

    def barrier(self, with_x=False):
        sem = pltpu.get_barrier_semaphore()

        def greet(way):
            pl.semaphore_signal(
                sem,
                inc=1,
                device_id={"wide": self.towards(way)},
                device_id_type=pl.DeviceIdType.MESH,
            )

        pl.when(self.z > 0)(lambda: greet(DOWN))
        pl.when(self.z < LINE - 1)(lambda: greet(UP))
        greet(ACROSS)
        greet(TWIN)
        if with_x:
            pl.semaphore_signal(
                sem, inc=1, device_id={"groups": 1 - lax.axis_index("groups")},
                device_id_type=pl.DeviceIdType.MESH,
            )
        ends = jnp.where((self.z == 0) | (self.z == LINE - 1), 1, 0)
        pl.semaphore_wait(sem, (5 if with_x else 4) - ends)


UPN, DOWNN = 0, 1
XWAY = 4
TILE = 16
LINE_A, LINE_B, CROSS_A, CROSS_B, A_UP, A_DOWN, ATTEND, READY, PROJECT = range(9)
A_KINDS = {"A": LINE_A, "B": LINE_B, "XA": CROSS_A, "XB": CROSS_B}
A_PLAIN = {"u": A_UP, "d": A_DOWN, "a": ATTEND, "r": READY}
A_END = (
    "a", "a", "a", "0B", "u", "a", "a", "a", "1A", "1B", "a", "2A",
    "a", "3A", "1XA", "2XA", "1XB", "0XB", "r", "2B", "j10", "j21", "j01", "3XA",
    "2XB", "3B", "j00", "j20", "j11", "3XB", "j31", "j30",
)
A_INNER = (
    "a", "a", "2A", "0A", "1B", "u", "d", "a", "a", "3A", "0B", "a",
    "a", "2B", "a", "3B", "a", "1XB", "0XB", "2XA", "3XA", "2XB", "0XA", "3XB",
    "r", "j11", "j21", "j20", "j30", "j01", "j31", "j10", "j00",
)


def gather_code(text):
    if text[0] in A_PLAIN:
        return A_PLAIN[text[0]] * 8
    if text[0] == "j":
        return PROJECT * 8 + int(text[1]) * 2 + int(text[2])
    return A_KINDS[text[1:]] * 8 + int(text[0]) * 2


def packed(codes, words, bits):
    codes = codes + [(1 << bits) - 1] * (words * (28 // bits) - len(codes))
    per = 28 // bits
    return [
        sum(c << (bits * j) for j, c in enumerate(codes[per * w : per * w + per]))
        for w in range(words)
    ]


def pick(index, inner, ends, inners):
    at_end, at_inner = jnp.int32(ends[0]), jnp.int32(inners[0])
    for k in range(1, len(ends)):
        at_end = jnp.where(index == k, jnp.int32(ends[k]), at_end)
        at_inner = jnp.where(index == k, jnp.int32(inners[k]), at_inner)
    return jnp.where(inner == 1, at_inner, at_end)


PIECES = "abcd"
GET, UP_OWN, DOWN_OWN, PASS_OWN, SERVE, PAIR_UP, FOLD, FINISH = range(8)
KINDS = {"g": GET, "u": UP_OWN, "d": DOWN_OWN, "y": PASS_OWN}
KINDS.update({"s": SERVE, "p": PAIR_UP, "f": FOLD, "z": FINISH})
PA, PB, PC, PD = range(4)
SUBS = 2
B_END = (
    "ya1", "uc0", "uc1", "ya0", "g0b1", "yc1", "ua1", "g0b0", "ub1", "ua0", "s01", "g1b0",
    "yc0", "g0d1", "g1b1", "g1a0", "g1a1", "ub0", "g3c0", "g3c1", "s11", "g3d1", "g3d0", "f12",
    "s30", "g3a1", "g0d0", "p3", "f11", "s00", "g3a0", "g3b1", "g3b0", "g2c1", "p0", "f30",
    "s31", "g2b1", "f32", "g2a1", "g2b0", "g2a0", "g2d1", "f31", "g2c0", "s21", "g1c1", "g2d0",
    "f22", "g1c0", "s20", "g1d1", "f21", "g1d0", "p2", "s10", "p1", "f20", "z2", "z0",
    "f10", "z1",
)
B_INNER = (
    "da1", "ya1", "uc1", "ya0", "da0", "ua0", "g0c0", "g1b1", "db1", "g1b0", "db0", "yc1",
    "g0c1", "g0a1", "yc0", "g3c0", "g3c1", "g2a0", "g0b1", "g0d0", "s11", "g2c1", "g0a0", "g0b0",
    "g0d1", "ub1", "g3a1", "ua1", "s00", "uc0", "g3d0", "g3d1", "g3a0", "g1d0", "g3b1", "s30",
    "g3b0", "p3", "g2d1", "g2b1", "g2a1", "ub0", "g1d1", "s31", "g2b0", "p0", "s01", "g2c0",
    "dc1", "f30", "s21", "g2d0", "dc0", "f32", "s20", "f00", "f31", "s10", "p2", "f22",
    "p1", "f02", "f21", "f01", "z2", "f20", "z1", "z0",
)


def code_of(text):
    kind = KINDS[text[0]] * 32
    if kind == GET * 32:
        return kind + int(text[1]) * 8 + PIECES.index(text[2]) * 2 + int(text[3])
    if kind in (UP_OWN * 32, DOWN_OWN * 32, PASS_OWN * 32):
        return kind + PIECES.index(text[1]) * 2 + int(text[2])
    if kind == PAIR_UP * 32:
        return kind + int(text[1]) * 8
    if kind == FINISH * 32:
        return kind + int(text[1]) * 2
    return kind + int(text[1]) * 8 + int(text[2]) * 2


def first_serve(program):
    return [text[0] for text in program].index("s")


def layer_kernel(
    length_ref, nk_ref, nv_ref, res_ref, gain_ref, ids_ref, raw_ref, q_hbm, k_hbm, v_hbm, ow_ref,
    wg_ref, wu_ref, wd_ref, out_ref, q_ref, k_ref, v_ref,
    held, attn, mixed_ref, res_pair, squares, share_tab, share_col, rows, part, from_twin,
    from_pair, from_line, acc, wg, wu, wd,
    own_sem, load_sem, send_sem, recv_sem, recv_twin, near_send, near_recv, share_send,
    share_recv, row_send, row_recv, twin_rows, square_send, square_recv,
    twin_squares, back_send, twin_sem, pair_sem, line_sem,
):
    place = Place()
    z, y, core = place.z, place.y, place.core
    group = lax.axis_index("groups")
    tokens = res_ref.shape[0]
    depth, wide = ow_ref.shape[0], ow_ref.shape[1] // 2
    low = z < LINE // 2
    inner = jnp.where(low, z, LINE - 1 - z)
    step_up = jnp.where(low, 1, -1)
    me = place.me
    my_columns = pl.ds(pl.multiple_of(y * wide, wide), wide)
    pair_columns = pl.ds(pl.multiple_of((1 - y) * wide, wide), wide)
    own = pltpu.make_async_copy(ow_ref.at[:, my_columns], held.at[me], own_sem)
    own.start()
    pairs = ((q_hbm, q_ref), (k_hbm, k_ref), (v_hbm, v_ref), (wg_ref, wg), (wu_ref, wu), (wd_ref, wd))
    fetches = [
        pltpu.make_async_copy(source, dest, load_sem.at[k])
        for k, (source, dest) in enumerate(pairs)
    ]
    fetches, loads = fetches[:3], fetches[3:]
    for fetch in fetches:
        fetch.start()
    place.barrier(True)

    short = depth // 8 * 3
    long = depth - short
    line_rows = pl.ds(pl.multiple_of(jnp.where(group == 0, 0, short), TILE), long)
    give_rows = pl.ds(pl.multiple_of(jnp.where(group == 0, 0, long), TILE), short)
    take_rows = pl.ds(pl.multiple_of(jnp.where(group == 0, long, 0), TILE), short)

    def real(nb):
        return jnp.where(low, nb, LINE - 1 - nb)

    def device(way):
        if way == XWAY:
            return {"groups": 1 - group}
        if way == UPN:
            return {"wide": place.block(z + step_up, y, core)}
        if way == DOWNN:
            return {"wide": place.block(z - step_up, y, core)}
        return {"wide": place.towards(way)}

    def send(source, dest, send_one, recv_one, way):
        return pltpu.make_async_remote_copy(
            src_ref=source, dst_ref=dest, send_sem=send_one, recv_sem=recv_one,
            device_id=device(way), device_id_type=pl.DeviceIdType.MESH,
        )

    def copy(b, way):
        ref = held.at[b, give_rows if way == XWAY else line_rows]
        if way == TWIN:
            return send(ref, ref, send_sem.at[way], recv_twin.at[b // 2], way)
        kind = 1 if way == XWAY else 0
        return send(ref, ref, send_sem.at[way], recv_sem.at[b // 2, kind], way)

    def taken(b):
        ref = held.at[b, take_rows]
        return (
            send(ref, ref, send_sem.at[XWAY], recv_sem.at[b // 2, 1], XWAY),
            send(ref, ref, send_sem.at[TWIN], recv_twin.at[b // 2], TWIN),
        )

    def whole(b):
        return send(held.at[b], held.at[b], send_sem.at[TWIN], recv_twin.at[b // 2], TWIN)

    def share_copy(b, way):
        return send(share_tab.at[b], share_tab.at[b], share_send.at[way], share_recv.at[b], way)

    def block_at(nb, yb, c):
        return place.block(real(nb), yb, c)

    send(
        ow_ref.at[line_rows, pair_columns], held.at[me, line_rows], send_sem.at[ACROSS],
        recv_sem.at[me // 2, 0], ACROSS,
    ).start()
    own.wait()
    copy(me, UPN).start()
    pl.when(inner == 1)(copy(me, DOWNN).start)
    whole(me).start()
    raw = raw_ref[...]
    given_share = raw / jnp.sum(raw, axis=0, keepdims=True)
    expert = lax.broadcasted_iota(jnp.int32, (share_tab.shape[1], 1), 0)
    table = jnp.zeros(share_tab.shape[1:], jnp.float32)
    for k in range(TOPK):
        hit = ids_ref[k : k + 1] == expert
        table = table + jnp.where(hit, given_share[k : k + 1], 0.0)
    share_tab[me] = table
    share_copy(me, UPN).start()
    pl.when(inner == 1)(share_copy(me, DOWNN).start)
    share_copy(me, ACROSS).start()
    share_copy(me, TWIN).start()
    attn_all = attn.at[pl.ds(tokens, tokens)]
    residual_sent = send(
        res_ref.at[:, pair_columns], res_pair, near_send.at[1], near_recv.at[1], ACROSS
    )

    def onward(b, nb, copier):
        pl.when(nb < inner)(copier(b, UPN).start)
        pl.when((nb > inner) & (inner == 1))(copier(b, DOWNN).start)

    def happen(code, turn):
        nb = lax.rem(code // 2, 4)
        flag = lax.rem(code, 2)
        kind = code // 8
        own_b = block_at(nb, y, core)
        other_b = block_at(nb, 1 - y, core)

        @pl.when(kind == LINE_A)
        def _():
            copy(own_b, ACROSS).wait_recv()
            onward(own_b, nb, copy)
            copy(own_b, XWAY).start()
            copy(own_b, TWIN).start()
            share_copy(own_b, TWIN).wait_recv()
            onward(own_b, nb, share_copy)
            share_copy(own_b, ACROSS).start()
            share_copy(own_b, TWIN).start()

        @pl.when(kind == LINE_B)
        def _():
            copy(other_b, ACROSS).wait_recv()
            onward(other_b, nb, copy)
            copy(other_b, XWAY).start()
            copy(other_b, TWIN).start()
            share_copy(other_b, TWIN).wait_recv()
            share_copy(other_b, TWIN).start()

        @pl.when((kind == CROSS_A) | (kind == CROSS_B))
        def _():
            arrival, forward = taken(jnp.where(kind == CROSS_A, own_b, other_b))
            arrival.wait_recv()
            forward.start()

        fresh = block_at(inner, 1 - y, core)
        pl.when(kind == A_UP)(copy(fresh, UPN).start)
        pl.when(kind == A_DOWN)(copy(fresh, DOWNN).start)

        @pl.when(kind == ATTEND)
        def _():
            @pl.when(turn == 0)
            def _():
                for load in loads:
                    load.start()
                for fetch in fetches:
                    fetch.wait()

            attend_step(turn)
            columns = pl.ds(pl.multiple_of(turn * PACK * HEAD, HEAD), PACK * HEAD)
            send(
                attn.at[pl.ds(0, tokens), columns], attn.at[pl.ds(tokens, tokens), columns],
                near_send.at[0], near_recv.at[0], ACROSS,
            ).start()

        @pl.when(kind == READY)
        def _():
            residual_sent.start()
            send(attn_all, attn_all, near_send.at[0], near_recv.at[0], ACROSS).wait_recv()

        pl.when(kind == PROJECT)(lambda: project(nb, flag == 1))

    length = length_ref[place.me]
    per_group = HEADS // KV_HEADS // PACK

    def attend_step(i):
        q = jnp.concatenate(
            [
                q_ref[:, pl.ds(pl.multiple_of((i * PACK + j) * HEAD, HEAD), HEAD)]
                for j in range(PACK)
            ],
            axis=0,
        )
        columns = pl.ds(pl.multiple_of(i // per_group * HEAD, HEAD), HEAD)
        out = attend(
            q, k_ref[0, :, columns], v_ref[0, :, columns], nk_ref[:, columns],
            nv_ref[:, columns], length, tokens,
        )
        for j in range(PACK):
            attn[:tokens, pl.ds(pl.multiple_of((i * PACK + j) * HEAD, HEAD), HEAD)] = out[
                j * tokens : (j + 1) * tokens
            ]

    mixed_ref[...] = jnp.zeros(mixed_ref.shape, jnp.float32)
    chosen = lax.broadcasted_iota(jnp.int32, (1, share_tab.shape[1]), 1) == me

    def project(nb, is_own):
        yb = jnp.where(is_own, y, 1 - y)
        b = block_at(nb, yb, 1 - core)

        whole(b).wait_recv()
        share_copy(b, TWIN).wait_recv()
        first = block_at(nb, yb, 0)
        for c in range(2):
            turned = share_tab[first + c].T
            column = jnp.sum(jnp.where(chosen, turned, 0.0), axis=1, keepdims=True)
            share_col[first + c] = jnp.broadcast_to(column, share_col.shape[1:])
        mine = attn[:, pl.ds(pl.multiple_of(first * depth, 2 * depth), 2 * depth)]
        weight = held[pl.ds(first, 2)].reshape(2 * depth, wide)
        mixed_ref[...] += jnp.dot(mine, weight, preferred_element_type=jnp.float32)

    a_words = -(-max(len(A_END), len(A_INNER)) // 4)
    a_end = packed([gather_code(text) for text in A_END], a_words, 7)
    a_inner = packed([gather_code(text) for text in A_INNER], a_words, 7)

    def gather_route(w, turn):
        def one(j, state):
            word, at = state
            code = lax.rem(word, 128)
            happen(code, at)
            return word // 128, at + jnp.where(code // 8 == ATTEND, 1, 0)

        return lax.fori_loop(0, 4, one, (pick(w, inner, a_end, a_inner), turn))[1]

    lax.fori_loop(0, a_words, gather_route, jnp.int32(0))
    half_rows = tokens // 2
    residual_sent.wait_recv()
    mixed_ref[:tokens] += res_ref[:, my_columns].astype(jnp.float32)
    mixed_ref[tokens:] += res_pair[...].astype(jnp.float32)
    mixed = mixed_ref[...]
    square = jnp.sum(mixed * mixed, axis=1, keepdims=True)
    gained = (mixed * gain_ref[:, my_columns]).astype(jnp.bfloat16)

    def slot(zb, p, yb, c):
        return ((zb * 2 + p) * PAIR + yb) * 2 + c

    for p in range(2):
        mine = slot(z, p, y, core)
        own_half = slice(p * half_rows, (p + 1) * half_rows)
        pair_half = slice(tokens + p * half_rows, tokens + (p + 1) * half_rows)
        rows[mine * SUBS + y] = gained[own_half]
        rows[mine * SUBS + 1 - y] = gained[pair_half]
        both = jnp.where(
            y == 0,
            jnp.concatenate([square[own_half], square[pair_half]], axis=0),
            jnp.concatenate([square[pair_half], square[own_half]], axis=0),
        )
        squares[mine] = jnp.broadcast_to(both, (tokens, HEAD)).T[: squares.shape[1]]

    def square_copy(b, way):
        landed = twin_squares.at[b // 4] if way == TWIN else square_recv.at[b // 2]
        return send(squares.at[b], squares.at[b], square_send.at[way], landed, way)

    def pass_on(b, h, way):
        row_copy(b, h, way).start()
        pl.when(h == 0)(square_copy(b, way).start)

    def row_copy(b, h, way):
        t = b * SUBS + h
        landed = twin_rows.at[b // 4] if way == TWIN else row_recv.at[b // 2 * SUBS + h]
        return send(rows.at[t], rows.at[t], row_send.at[way], landed, way)

    def to_twin(zb, p, yb):
        b = slot(zb, p, yb, 1 - core)
        t = (zb * 2 + p) * PAIR + yb
        return send(part.at[b], from_twin.at[t], back_send.at[0], twin_sem.at[t], TWIN)

    def to_pair(zb, p):
        b = slot(zb, p, 1 - y, core)
        t = LINE if p else zb
        return send(part.at[b], from_pair.at[t], back_send.at[0], pair_sem.at[t], ACROSS)

    def kind_slot(zb, kind):
        p = jnp.minimum(kind, 1)
        yb = jnp.where(kind == 2, 1 - y, y)
        return p, yb, slot(zb, p, yb, core)

    side_up = jnp.where(low, 0, 1)

    def to_line(zb, kind, way):
        b = kind_slot(zb, kind)[2]
        side = side_up if way == UPN else 1 - side_up
        return send(
            part.at[b], from_line.at[side, zb, kind], back_send.at[0],
            line_sem.at[side, zb, kind], way,
        )

    def serve(zb, p):
        first = slot(zb, p, 0, 0)
        bulk = rows.at[pl.ds(0, 2 * SUBS)]
        send(bulk, bulk, row_send.at[TWIN], twin_rows.at[first // 4], TWIN).wait_recv()
        few = squares.at[pl.ds(0, 2)]
        send(few, few, square_send.at[TWIN], twin_squares.at[first // 4], TWIN).wait_recv()
        totals = [squares[first + c] + squares[first + 2 + c] for c in range(2)]
        total = jnp.concatenate(totals, axis=1)
        scale = lax.rsqrt(total * (1.0 / D) + 1e-06).T[:, :1]
        here = pl.ds(pl.multiple_of(p * half_rows, half_rows), half_rows)
        block = place.block(zb, 0, 0)
        share = jnp.concatenate(
            [share_col[block + yb * 2 + c, here] for c in range(2) for yb in range(2)], axis=0
        )
        sides = [
            rows[pl.ds((first + 2 * k) * SUBS, 2 * SUBS)].reshape(4 * half_rows, wide)
            for k in range(2)
        ]

        def times(w):
            first_half = jnp.dot(sides[0], w[:wide], preferred_element_type=jnp.float32)
            other_half = jnp.dot(sides[1], w[wide:], preferred_element_type=jnp.float32)
            return (first_half + other_half) * scale

        gate, up = times(wg), times(wu)
        act = (gate / (1.0 + jnp.exp(-gate)) * up).astype(jnp.bfloat16)
        out = jnp.dot(act, wd[...], preferred_element_type=jnp.float32) * share[:, :1]
        out = out.astype(jnp.bfloat16)
        for k in range(4):
            part[first + k % 2 * 2 + k // 2] = out[k * half_rows : (k + 1) * half_rows]
        to_twin(zb, p, 0).start()
        to_twin(zb, p, 1).start()

    def with_twin(zb, p, yb):
        to_twin(zb, p, yb).wait_recv()
        b = slot(zb, p, yb, core)
        t = (zb * 2 + p) * PAIR + yb
        return part[b].astype(jnp.float32) + from_twin[t].astype(jnp.float32)

    def add_line(zb, kind, way):
        to_line(zb, kind, way).wait_recv()
        side = side_up if way == UPN else 1 - side_up
        acc[...] += from_line[side, zb, kind].astype(jnp.float32)

    def fold(nb, kind):
        zb = real(nb)
        p, yb, b = kind_slot(zb, kind)
        acc[...] = with_twin(zb, p, yb)

        @pl.when(kind == 0)
        def _():
            to_pair(zb, 0).wait_recv()
            acc[...] += from_pair[zb].astype(jnp.float32)

        pl.when((nb > inner) & (inner == 1))(lambda: add_line(zb, kind, UPN))
        pl.when(nb < inner)(lambda: add_line(zb, kind, DOWNN))
        part[b] = acc[...].astype(jnp.bfloat16)
        pl.when(nb > inner)(to_line(zb, kind, UPN).start)
        pl.when(nb < inner)(to_line(zb, kind, DOWNN).start)

    def finish(kind):
        p, yb, b = kind_slot(z, kind)
        acc[...] = with_twin(z, p, yb)
        pl.when(inner == 1)(lambda: add_line(z, kind, UPN))
        add_line(z, kind, DOWNN)

        @pl.when(kind == 2)
        def _():
            acc[:, my_columns] += mixed_ref[pl.ds(tokens + half_rows, half_rows)]
            part[b] = acc[...].astype(jnp.bfloat16)
            to_pair(z, 1).start()

        def close(p, t):
            here = pl.ds(p * half_rows, half_rows)
            to_pair(z, p).wait_recv()
            acc[:, my_columns] += mixed_ref[here]
            out_ref[here] = (acc[...] + from_pair[t].astype(jnp.float32)).astype(jnp.bfloat16)

        pl.when(kind == 0)(lambda: close(0, z))
        pl.when(kind == 1)(lambda: close(1, LINE))

    def act_on(code, first):
        kind = code // 32
        nb = lax.rem(code // 8, 4)
        piece = lax.rem(code // 2, 4)
        h = lax.rem(code, 2)
        zb = real(nb)
        p = jnp.where(piece <= PB, 1, 0)
        yb = jnp.where((piece == PA) | (piece == PC), y, 1 - y)
        own_piece = slot(z, p, yb, core)

        @pl.when(kind == GET)
        def _():
            b = slot(zb, p, yb, core)
            row_copy(b, h, ACROSS).wait_recv()
            pl.when(h == 0)(square_copy(b, ACROSS).wait_recv)
            onward = piece != PD
            pl.when(onward & (nb < inner))(lambda: pass_on(b, h, UPN))
            pl.when(onward & (nb > inner) & (inner == 1))(lambda: pass_on(b, h, DOWNN))
            pl.when((piece == PC) & (nb != inner))(lambda: pass_on(b, h, ACROSS))
            pass_on(b, h, TWIN)

        pl.when(kind == UP_OWN)(lambda: pass_on(own_piece, h, UPN))
        pl.when(kind == DOWN_OWN)(lambda: pass_on(own_piece, h, DOWNN))

        @pl.when(kind == PASS_OWN)
        def _():
            pass_on(own_piece, h, ACROSS)
            pass_on(own_piece, h, TWIN)

        @pl.when(kind == SERVE)
        def _():
            @pl.when(first)
            def _():
                for load in loads:
                    load.wait()

            serve(zb, piece)

        @pl.when(kind == PAIR_UP)
        def _():
            acc[...] = with_twin(zb, 0, 1 - y)

            @pl.when(nb == inner)
            def _():
                acc[:, my_columns] += mixed_ref[pl.ds(tokens, half_rows)]

            part[slot(zb, 0, 1 - y, core)] = acc[...].astype(jnp.bfloat16)
            to_pair(zb, 0).start()

        pl.when(kind == FOLD)(lambda: fold(nb, piece))
        pl.when((kind == FINISH) & (piece < 3))(lambda: finish(piece))

    words = -(-max(len(B_END), len(B_INNER)) // 3)
    end_words = packed([code_of(text) for text in B_END], words, 9)
    inner_words = packed([code_of(text) for text in B_INNER], words, 9)
    serve_at = jnp.where(inner == 1, first_serve(B_INNER), first_serve(B_END))

    def route(w, carry):
        def one(j, word):
            act_on(lax.rem(word, 512), w * 3 + j == serve_at)
            return word // 512

        lax.fori_loop(0, 3, one, pick(w, inner, end_words, inner_words))
        return carry

    lax.fori_loop(0, words, route, 0)

    def sent(ref, sem, way=TWIN):
        send(ref, ref, sem, share_recv.at[0], way).wait_send()

    def sent_by_place(at_end, at_inner):
        pl.when(inner == 0)(at_end)
        pl.when(inner == 1)(at_inner)

    lines = pl.ds(0, long)
    sent_by_place(
        lambda: sent(held.at[pl.ds(0, 2), lines], send_sem.at[UPN]),
        lambda: sent(held.at[pl.ds(0, 4), lines], send_sem.at[UPN]),
    )
    sent_by_place(
        lambda: sent(share_tab.at[pl.ds(0, 1)], share_send.at[UPN]),
        lambda: sent(share_tab.at[pl.ds(0, 2)], share_send.at[UPN]),
    )
    sent_by_place(
        lambda: sent(rows.at[pl.ds(0, 3 * SUBS)], row_send.at[UPN]),
        lambda: sent(rows.at[pl.ds(0, 6 * SUBS)], row_send.at[UPN]),
    )
    sent_by_place(
        lambda: sent(squares.at[pl.ds(0, 3)], square_send.at[UPN]),
        lambda: sent(squares.at[pl.ds(0, 6)], square_send.at[UPN]),
    )

    @pl.when(inner == 1)
    def _():
        sent(held.at[pl.ds(0, 6), lines], send_sem.at[DOWNN])
        sent(share_tab.at[pl.ds(0, 3)], share_send.at[DOWNN])
        sent(rows.at[pl.ds(0, 9 * SUBS)], row_send.at[DOWNN])
        sent(squares.at[pl.ds(0, 9)], square_send.at[DOWNN])

    sent(held.at[0, lines], send_sem.at[ACROSS])
    sent(held.at[pl.ds(0, 2 * LINE - 1), pl.ds(0, short)], send_sem.at[XWAY])
    sent(attn_all, near_send.at[0])
    residual_sent.wait_send()
    sent(held.at[pl.ds(0, 2 * LINE)], send_sem.at[TWIN])
    sent(share_tab.at[pl.ds(0, LINE)], share_send.at[ACROSS])
    sent(share_tab.at[pl.ds(0, 2 * LINE)], share_send.at[TWIN])
    sent(rows.at[pl.ds(0, 5 * SUBS)], row_send.at[ACROSS])
    sent(rows.at[pl.ds(0, 4 * LINE * SUBS)], row_send.at[TWIN])
    sent(squares.at[pl.ds(0, 5)], square_send.at[ACROSS])
    sent(squares.at[pl.ds(0, 4 * LINE)], square_send.at[TWIN])
    sent(part.at[pl.ds(0, 7 * LINE + 2)], back_send.at[0])


def layer(
    cache_len, queries, new_keys, new_values, cache_keys, cache_values, residual, gain, ids, raw,
    o_weight, gate_w, up_w, down_w, devices,
):
    tokens, width = queries.shape
    half = tokens // 2
    vmem = pl.BlockSpec(memory_space=pltpu.VMEM)
    whole = pl.BlockSpec(memory_space=pl.ANY)
    dma = pltpu.SemaphoreType.DMA

    def held(*lead):
        return pltpu.VMEM(lead + (half, D), jnp.bfloat16)

    return pl.pallas_call(
        layer_kernel,
        in_specs=[pl.BlockSpec(memory_space=pltpu.SMEM)] + [vmem] * 6 + [whole] * 7,
        out_specs=vmem,
        out_shape=jax.ShapeDtypeStruct((tokens, D), jnp.bfloat16),
        scratch_shapes=[
            pltpu.VMEM(queries.shape, jnp.bfloat16),
            pltpu.VMEM(cache_keys.shape, jnp.bfloat16),
            pltpu.VMEM(cache_values.shape, jnp.bfloat16),
            pltpu.VMEM((devices, o_weight.shape[0], D // 2), jnp.bfloat16),
            pltpu.VMEM((2 * tokens, width), jnp.bfloat16),
            pltpu.VMEM((2 * tokens, D // 2), jnp.float32),
            pltpu.VMEM((tokens, D // 2), jnp.bfloat16),
            pltpu.VMEM((2 * devices, 8, tokens), jnp.float32),
            pltpu.VMEM((devices, devices, tokens), jnp.float32),
            pltpu.VMEM((devices, tokens, HEAD), jnp.float32),
            pltpu.VMEM((2 * devices * SUBS, half, D // 2), jnp.bfloat16),
            held(2 * devices),
            held(devices),
            held(LINE + 1),
            held(2, LINE, 3),
            pltpu.VMEM((half, D), jnp.float32),
            pltpu.VMEM(gate_w.shape, jnp.bfloat16),
            pltpu.VMEM(up_w.shape, jnp.bfloat16),
            pltpu.VMEM(down_w.shape, jnp.bfloat16),
            dma,
            dma((6,)),
            dma((5,)),
            dma((devices // 2, 2)),
            dma((devices // 2,)),
            dma((2,)),
            dma((2,)),
            dma((4,)),
            dma((devices,)),
            dma((4,)),
            dma((devices * SUBS,)),
            dma((devices // 2,)),
            dma((4,)),
            dma((devices,)),
            dma((devices // 2,)),
            dma((1,)),
            dma((devices,)),
            dma((LINE + 1,)),
            dma((2, LINE, 3)),
        ],
        compiler_params=pltpu.CompilerParams(
            collective_id=0, has_side_effects=True, vmem_limit_bytes=63 << 20
        ),
    )(
        cache_len, new_keys, new_values, residual, gain, ids, raw, queries, cache_keys, cache_values,
        o_weight, gate_w, up_w, down_w,
    )


def grid_device(
    residual, queries, new_keys, new_values, cache_keys, cache_values, cache_len, o_weight,
    norm_gain, expert_ids, gate_raw, w_gate, w_up, w_down,
):
    devices = lax.axis_size("wide")
    return layer(
        cache_len, queries, new_keys, new_values, cache_keys, cache_values, residual,
        norm_gain.reshape(1, D), expert_ids.T, gate_raw.T, o_weight, w_gate[0], w_up[0], w_down[0], devices,
    )


def per_device(
    residual,
    queries,
    new_keys,
    new_values,
    cache_keys,
    cache_values,
    cache_len,
    o_weight,
    norm_gain,
    expert_ids,
    gate_raw,
    w_gate,
    w_up,
    w_down,
):
    devices = lax.axis_size("wide")
    me = lax.axis_index("wide")
    length = lax.dynamic_slice_in_dim(cache_len, me, 1, 0)
    attn = attention(length, queries, new_keys, new_values, cache_keys, cache_values)
    projected = jnp.dot(
        attn,
        lax.all_gather(o_weight, "wide", axis=0, tiled=True),
        preferred_element_type=jnp.float32,
    )
    mixed = residual.astype(jnp.float32) + projected
    normed = (
        mixed * lax.rsqrt(jnp.mean(mixed * mixed, axis=-1, keepdims=True) + 1e-06) * norm_gain
    ).astype(jnp.bfloat16)
    shares = gate_raw / jnp.sum(gate_raw, axis=-1, keepdims=True)
    routed = sparse_experts(normed, expert_ids, shares, w_gate[0], w_up[0], w_down[0], devices)
    return (mixed + routed).astype(jnp.bfloat16)


def solution(mesh):
    rows = P(("groups", "wide"), None)
    blocks = P(("groups", "wide"), None, None)
    weights = P("wide", None, None)
    placed = (rows, rows, rows, rows, blocks, blocks, P("groups"), P("wide", None), P())
    placed += (rows, rows, weights, weights, weights)
    grid = mesh.shape["wide"] == LINE * PAIR * 2 and mesh.shape["groups"] == 2
    return jax.shard_map(
        grid_device if grid else per_device,
        mesh=mesh,
        in_specs=placed,
        out_specs=rows,
        check_vma=False,
    )
```

```python
import functools
import jax
import jax.numpy as jnp
from jax import lax
from jax.experimental import pallas as pl
from jax.experimental.pallas import tpu as pltpu
from jax.sharding import PartitionSpec as P

D = 2048
HEADS = 16
KV_HEADS = 2
HEAD = 128
TOPK = 8
SPAN = 128
PACK = 2
EXP2_SCALE = HEAD ** (-0.5) * 1.4426950408889634


def attention_kernel(length_ref, q_ref, nk_ref, nv_ref, k_ref, v_ref, out_ref):
    tokens = q_ref.shape[0]
    rows = PACK * tokens
    cache = k_ref.shape[1]
    q = jnp.concatenate([q_ref[:, i * HEAD : (i + 1) * HEAD] for i in range(PACK)], axis=0)
    dims = (((1,), (1,)), ((), ()))
    s = lax.dot_general(q, k_ref[0], dims, preferred_element_type=jnp.float32)
    position = lax.broadcasted_iota(jnp.int32, (1, cache), 1)
    s = jnp.where(position < length_ref[0], s, jnp.float32(-1e30))
    s_new = lax.dot_general(q, nk_ref[...], dims, preferred_element_type=jnp.float32)
    row = lax.broadcasted_iota(jnp.int32, (rows, tokens), 0) % tokens
    column = lax.broadcasted_iota(jnp.int32, (rows, tokens), 1)
    s_new = jnp.where(column <= row, s_new, jnp.float32(-1e30))
    top = jnp.maximum(jnp.max(s, axis=1, keepdims=True), jnp.max(s_new, axis=1, keepdims=True))
    w = jnp.exp2((s - top) * EXP2_SCALE)
    w_new = jnp.exp2((s_new - top) * EXP2_SCALE)
    total = jnp.sum(w, axis=1, keepdims=True) + jnp.sum(w_new, axis=1, keepdims=True)
    out = jnp.dot(w.astype(jnp.bfloat16), v_ref[0], preferred_element_type=jnp.float32)
    out += jnp.dot(w_new.astype(jnp.bfloat16), nv_ref[...], preferred_element_type=jnp.float32)
    out = (out / total).astype(out_ref.dtype)
    for i in range(PACK):
        out_ref[:, i * HEAD : (i + 1) * HEAD] = out[i * tokens : (i + 1) * tokens]


def attention(length, queries, new_keys, new_values, cache_keys, cache_values):
    tokens, width = queries.shape
    cache = cache_keys.shape[1]
    per_group = HEADS // KV_HEADS // PACK
    return pl.pallas_call(
        attention_kernel,
        grid=(HEADS // PACK,),
        in_specs=[
            pl.BlockSpec(memory_space=pltpu.SMEM),
            pl.BlockSpec((tokens, PACK * HEAD), lambda i: (0, i)),
            pl.BlockSpec((tokens, HEAD), lambda i: (0, i // per_group)),
            pl.BlockSpec((tokens, HEAD), lambda i: (0, i // per_group)),
            pl.BlockSpec((1, cache, HEAD), lambda i: (0, 0, i // per_group)),
            pl.BlockSpec((1, cache, HEAD), lambda i: (0, 0, i // per_group)),
        ],
        out_specs=pl.BlockSpec((tokens, PACK * HEAD), lambda i: (0, i)),
        out_shape=jax.ShapeDtypeStruct((tokens, width), jnp.bfloat16),
        cost_estimate=pl.CostEstimate(
            flops=4 * tokens * width * (cache + tokens),
            bytes_accessed=4 * cache * KV_HEADS * HEAD + 4 * tokens * width,
            transcendentals=tokens * HEADS * (cache + tokens),
        ),
    )(length, queries, new_keys, new_values, cache_keys, cache_values)


def run_expert(rows_in, gate_w, up_w, down_w):
    gate_part = jnp.dot(rows_in, gate_w, preferred_element_type=jnp.float32)
    up_part = jnp.dot(rows_in, up_w, preferred_element_type=jnp.float32)
    activated = (jax.nn.silu(gate_part) * up_part).astype(jnp.bfloat16)
    return jnp.dot(activated, down_w, preferred_element_type=jnp.float32)


def sparse_experts(normed, expert_ids, shares, gate_w, up_w, down_w, devices):
    token_count = normed.shape[0]
    capacity = SPAN * TOPK // devices + max(2, SPAN * TOPK // (8 * devices))
    flat_ids = expert_ids.reshape(-1)
    named = expert_ids[:, :, None] == jnp.arange(devices, dtype=jnp.int32)[None, None, :]
    earlier = jnp.tril(jnp.ones((token_count, token_count), jnp.bfloat16), -1)
    before = jnp.dot(
        earlier, jnp.any(named, axis=1).astype(jnp.bfloat16), preferred_element_type=jnp.float32
    )
    ranks = jnp.sum(jnp.where(named, before[:, None, :], 0.0), axis=-1)
    ranks = ranks.astype(jnp.int32).reshape(-1)
    slot_index = flat_ids * capacity + ranks
    token_of = jnp.arange(flat_ids.shape[0], dtype=jnp.int32) // TOPK
    slot_token = (
        jnp.full((devices * capacity,), token_count, jnp.int32).at[slot_index].set(token_of)
    )
    padded = jnp.concatenate([normed, jnp.zeros((1, D), jnp.bfloat16)], axis=0)
    outgoing = padded[slot_token].reshape(devices, capacity, D)
    arrived = lax.all_to_all(outgoing, "wide", split_axis=0, concat_axis=0, tiled=True)
    served = run_expert(arrived.reshape(-1, D), gate_w, up_w, down_w).astype(jnp.bfloat16)
    served = served.reshape(devices, capacity, D)
    returned_rows = lax.all_to_all(served, "wide", split_axis=0, concat_axis=0, tiled=True)
    picked = returned_rows.reshape(devices * capacity, D)[slot_index].reshape(token_count, TOPK, D)
    return jnp.sum(picked.astype(jnp.float32) * shares[..., None], axis=1)


LINE = 4
PAIR = 2
DOWN, UP, ACROSS, TWIN = range(4)


def attend(q, key, value, new_key, new_value, length, tokens):
    rows = q.shape[0]
    dims = (((1,), (1,)), ((), ()))
    s = lax.dot_general(q, key, dims, preferred_element_type=jnp.float32)
    position = lax.broadcasted_iota(jnp.int32, (1, key.shape[0]), 1)
    s = jnp.where(position < length, s, jnp.float32(-1e30))
    s_new = lax.dot_general(q, new_key, dims, preferred_element_type=jnp.float32)
    row = lax.broadcasted_iota(jnp.int32, (rows, tokens), 0) % tokens
    column = lax.broadcasted_iota(jnp.int32, (rows, tokens), 1)
    s_new = jnp.where(column <= row, s_new, jnp.float32(-1e30))
    top = jnp.maximum(jnp.max(s, axis=1, keepdims=True), jnp.max(s_new, axis=1, keepdims=True))
    w = jnp.exp2((s - top) * EXP2_SCALE)
    w_new = jnp.exp2((s_new - top) * EXP2_SCALE)
    total = jnp.sum(w, axis=1, keepdims=True) + jnp.sum(w_new, axis=1, keepdims=True)
    out = jnp.dot(w.astype(jnp.bfloat16), value, preferred_element_type=jnp.float32)
    out += jnp.dot(w_new.astype(jnp.bfloat16), new_value, preferred_element_type=jnp.float32)
    return (out / total).astype(jnp.bfloat16)


class Place:
    def __init__(self):
        self.me = lax.axis_index("wide")
        self.core = self.me % 2
        self.y = (self.me // 2) % PAIR
        self.z = self.me // (2 * PAIR)

    def block(self, z, y, core):
        return (z * PAIR + y) * 2 + core

    def towards(self, way):
        z, y, core = self.z, self.y, self.core
        if way == DOWN:
            return self.block(z - 1, y, core)
        if way == UP:
            return self.block(z + 1, y, core)
        if way == ACROSS:
            return self.block(z, 1 - y, core)
        return self.block(z, y, 1 - core)

    def line_at(self, i):
        low = self.z < LINE // 2
        inner = jnp.where(low, self.z, LINE - 1 - self.z)
        near = jnp.where((inner == 0) | (i >= 2), i, 1 - i)
        return jnp.where(low, near, LINE - 1 - near)

    def barrier(self, with_x=False):
        sem = pltpu.get_barrier_semaphore()

        def greet(way):
            pl.semaphore_signal(
                sem,
                inc=1,
                device_id={"wide": self.towards(way)},
                device_id_type=pl.DeviceIdType.MESH,
            )

        pl.when(self.z > 0)(lambda: greet(DOWN))
        pl.when(self.z < LINE - 1)(lambda: greet(UP))
        greet(ACROSS)
        greet(TWIN)
        if with_x:
            pl.semaphore_signal(
                sem, inc=1, device_id={"groups": 1 - lax.axis_index("groups")},
                device_id_type=pl.DeviceIdType.MESH,
            )
        ends = jnp.where((self.z == 0) | (self.z == LINE - 1), 1, 0)
        pl.semaphore_wait(sem, (5 if with_x else 4) - ends)


UPN, DOWNN = 0, 1
XWAY = 4
TILE = 16
LINE_A, LINE_B, CROSS_A, CROSS_B, A_UP, A_DOWN, ATTEND, READY, PROJECT = range(9)
A_KINDS = {"A": LINE_A, "B": LINE_B, "XA": CROSS_A, "XB": CROSS_B}
A_PLAIN = {"u": A_UP, "d": A_DOWN, "a": ATTEND, "r": READY}
A_END = (
    "a", "a", "a", "a", "0B", "u", "1A", "a", "a", "a", "a", "2A",
    "3A", "0XB", "r", "2XA", "1XA", "1B", "j00", "2B", "j01", "3XA", "j21", "1XB",
    "j11", "3B", "2XB", "j31", "j10", "j20", "3XB", "j30",
)
A_INNER = (
    "a", "a", "2A", "0A", "1B", "d", "a", "a", "u", "3A", "a", "0B",
    "a", "2B", "a", "a", "2XA", "3B", "0XA", "0XB", "2XB", "3XA", "r", "j11",
    "1XB", "j20", "j01", "3XB", "j21", "j10", "j31", "j00", "j30",
)


def gather_code(text):
    if text[0] in A_PLAIN:
        return A_PLAIN[text[0]] * 8
    if text[0] == "j":
        return PROJECT * 8 + int(text[1]) * 2 + int(text[2])
    return A_KINDS[text[1:]] * 8 + int(text[0]) * 2


def packed(codes, words, bits):
    codes = codes + [(1 << bits) - 1] * (words * (28 // bits) - len(codes))
    per = 28 // bits
    return [
        sum(c << (bits * j) for j, c in enumerate(codes[per * w : per * w + per]))
        for w in range(words)
    ]


def pick(index, inner, ends, inners):
    at_end, at_inner = jnp.int32(ends[0]), jnp.int32(inners[0])
    for k in range(1, len(ends)):
        at_end = jnp.where(index == k, jnp.int32(ends[k]), at_end)
        at_inner = jnp.where(index == k, jnp.int32(inners[k]), at_inner)
    return jnp.where(inner == 1, at_inner, at_end)


PIECES = "abcd"
GET, UP_OWN, DOWN_OWN, PASS_OWN, SERVE, PAIR_UP, FOLD, FINISH = range(8)
KINDS = {"g": GET, "u": UP_OWN, "d": DOWN_OWN, "y": PASS_OWN}
KINDS.update({"s": SERVE, "p": PAIR_UP, "f": FOLD, "z": FINISH})
PA, PB, PC, PD = range(4)
SUBS = 2
B_END = (
    "ya1", "uc0", "uc1", "ya0", "g0b1", "yc1", "ua1", "g0b0", "ub1", "ua0", "s01", "g1b0",
    "yc0", "g0d1", "g1b1", "g1a0", "g1a1", "ub0", "g3c0", "g3c1", "s11", "g3d1", "g3d0", "f12",
    "s30", "g3a1", "g0d0", "p3", "f11", "s00", "g3a0", "g3b1", "g3b0", "g2c1", "p0", "f30",
    "s31", "g2b1", "f32", "g2a1", "g2b0", "g2a0", "g2d1", "f31", "g2c0", "s21", "g1c1", "g2d0",
    "f22", "g1c0", "s20", "g1d1", "f21", "g1d0", "p2", "s10", "p1", "f20", "z2", "z0",
    "f10", "z1",
)
B_INNER = (
    "da1", "ya1", "uc1", "ya0", "da0", "ua0", "g0c0", "g1b1", "db1", "g1b0", "db0", "yc1",
    "g0c1", "g0a1", "yc0", "g3c0", "g3c1", "g2a0", "g0b1", "g0d0", "s11", "g2c1", "g0a0", "g0b0",
    "g0d1", "ub1", "g3a1", "ua1", "s00", "uc0", "g3d0", "g3d1", "g3a0", "g1d0", "g3b1", "s30",
    "g3b0", "p3", "g2d1", "g2b1", "g2a1", "ub0", "g1d1", "s31", "g2b0", "p0", "s01", "g2c0",
    "dc1", "f30", "s21", "g2d0", "dc0", "f32", "s20", "f00", "f31", "s10", "p2", "f22",
    "p1", "f02", "f21", "f01", "z2", "f20", "z1", "z0",
)


def code_of(text):
    kind = KINDS[text[0]] * 32
    if kind == GET * 32:
        return kind + int(text[1]) * 8 + PIECES.index(text[2]) * 2 + int(text[3])
    if kind in (UP_OWN * 32, DOWN_OWN * 32, PASS_OWN * 32):
        return kind + PIECES.index(text[1]) * 2 + int(text[2])
    if kind == PAIR_UP * 32:
        return kind + int(text[1]) * 8
    if kind == FINISH * 32:
        return kind + int(text[1]) * 2
    return kind + int(text[1]) * 8 + int(text[2]) * 2


def first_serve(program):
    return [text[0] for text in program].index("s")


def layer_kernel(
    length_ref, nk_ref, nv_ref, res_ref, gain_ref, ids_ref, raw_ref, q_hbm, k_hbm, v_hbm, ow_ref,
    wg_ref, wu_ref, wd_ref, out_ref, q_ref, k_ref, v_ref,
    held, attn, mixed_ref, res_pair, squares, share_tab, share_col, rows, part, from_twin,
    from_pair, from_line, acc, wg, wu, wd,
    own_sem, load_sem, send_sem, recv_sem, recv_twin, near_send, near_recv, share_send,
    share_recv, row_send, row_recv, twin_rows, square_send, square_recv,
    twin_squares, back_send, twin_sem, pair_sem, line_sem,
):
    place = Place()
    z, y, core = place.z, place.y, place.core
    group = lax.axis_index("groups")
    tokens = res_ref.shape[0]
    depth, wide = ow_ref.shape[0], ow_ref.shape[1] // 2
    low = z < LINE // 2
    inner = jnp.where(low, z, LINE - 1 - z)
    step_up = jnp.where(low, 1, -1)
    me = place.me
    my_columns = pl.ds(pl.multiple_of(y * wide, wide), wide)
    pair_columns = pl.ds(pl.multiple_of((1 - y) * wide, wide), wide)
    own = pltpu.make_async_copy(ow_ref.at[:, my_columns], held.at[me], own_sem)
    own.start()
    pairs = ((q_hbm, q_ref), (k_hbm, k_ref), (v_hbm, v_ref), (wg_ref, wg), (wu_ref, wu), (wd_ref, wd))
    fetches = [
        pltpu.make_async_copy(source, dest, load_sem.at[k])
        for k, (source, dest) in enumerate(pairs)
    ]
    fetches, loads = fetches[:3], fetches[3:]
    for fetch in fetches:
        fetch.start()
    place.barrier(True)

    short = depth // 8 * 3
    long = depth - short
    line_rows = pl.ds(pl.multiple_of(jnp.where(group == 0, 0, short), TILE), long)
    give_rows = pl.ds(pl.multiple_of(jnp.where(group == 0, 0, long), TILE), short)
    take_rows = pl.ds(pl.multiple_of(jnp.where(group == 0, long, 0), TILE), short)

    def real(nb):
        return jnp.where(low, nb, LINE - 1 - nb)

    def device(way):
        if way == XWAY:
            return {"groups": 1 - group}
        if way == UPN:
            return {"wide": place.block(z + step_up, y, core)}
        if way == DOWNN:
            return {"wide": place.block(z - step_up, y, core)}
        return {"wide": place.towards(way)}

    def send(source, dest, send_one, recv_one, way):
        return pltpu.make_async_remote_copy(
            src_ref=source, dst_ref=dest, send_sem=send_one, recv_sem=recv_one,
            device_id=device(way), device_id_type=pl.DeviceIdType.MESH,
        )

    def copy(b, way):
        ref = held.at[b, give_rows if way == XWAY else line_rows]
        if way == TWIN:
            return send(ref, ref, send_sem.at[way], recv_twin.at[b // 2], way)
        kind = 1 if way == XWAY else 0
        return send(ref, ref, send_sem.at[way], recv_sem.at[b // 2, kind], way)

    def taken(b):
        ref = held.at[b, take_rows]
        return (
            send(ref, ref, send_sem.at[XWAY], recv_sem.at[b // 2, 1], XWAY),
            send(ref, ref, send_sem.at[TWIN], recv_twin.at[b // 2], TWIN),
        )

    def whole(b):
        return send(held.at[b], held.at[b], send_sem.at[TWIN], recv_twin.at[b // 2], TWIN)

    def share_copy(b, way):
        return send(share_tab.at[b], share_tab.at[b], share_send.at[way], share_recv.at[b], way)

    def block_at(nb, yb, c):
        return place.block(real(nb), yb, c)

    send(
        ow_ref.at[line_rows, pair_columns], held.at[me, line_rows], send_sem.at[ACROSS],
        recv_sem.at[me // 2, 0], ACROSS,
    ).start()
    own.wait()
    copy(me, UPN).start()
    pl.when(inner == 1)(copy(me, DOWNN).start)
    whole(me).start()
    raw = raw_ref[...]
    given_share = raw / jnp.sum(raw, axis=0, keepdims=True)
    expert = lax.broadcasted_iota(jnp.int32, (share_tab.shape[1], 1), 0)
    table = jnp.zeros(share_tab.shape[1:], jnp.float32)
    for k in range(TOPK):
        hit = ids_ref[k : k + 1] == expert
        table = table + jnp.where(hit, given_share[k : k + 1], 0.0)
    share_tab[me] = table
    share_copy(me, UPN).start()
    pl.when(inner == 1)(share_copy(me, DOWNN).start)
    share_copy(me, ACROSS).start()
    share_copy(me, TWIN).start()
    attn_all = attn.at[pl.ds(tokens, tokens)]
    residual_sent = send(
        res_ref.at[:, pair_columns], res_pair, near_send.at[1], near_recv.at[1], ACROSS
    )

    def onward(b, nb, copier):
        pl.when(nb < inner)(copier(b, UPN).start)
        pl.when((nb > inner) & (inner == 1))(copier(b, DOWNN).start)

    def happen(code, turn):
        nb = lax.rem(code // 2, 4)
        flag = lax.rem(code, 2)
        kind = code // 8
        own_b = block_at(nb, y, core)
        other_b = block_at(nb, 1 - y, core)

        @pl.when(kind == LINE_A)
        def _():
            copy(own_b, ACROSS).wait_recv()
            onward(own_b, nb, copy)
            copy(own_b, XWAY).start()
            copy(own_b, TWIN).start()
            share_copy(own_b, TWIN).wait_recv()
            onward(own_b, nb, share_copy)
            share_copy(own_b, ACROSS).start()
            share_copy(own_b, TWIN).start()

        @pl.when(kind == LINE_B)
        def _():
            copy(other_b, ACROSS).wait_recv()
            onward(other_b, nb, copy)
            copy(other_b, XWAY).start()
            copy(other_b, TWIN).start()
            share_copy(other_b, TWIN).wait_recv()
            share_copy(other_b, TWIN).start()

        @pl.when((kind == CROSS_A) | (kind == CROSS_B))
        def _():
            arrival, forward = taken(jnp.where(kind == CROSS_A, own_b, other_b))
            arrival.wait_recv()
            forward.start()

        fresh = block_at(inner, 1 - y, core)
        pl.when(kind == A_UP)(copy(fresh, UPN).start)
        pl.when(kind == A_DOWN)(copy(fresh, DOWNN).start)

        @pl.when(kind == ATTEND)
        def _():
            @pl.when(turn == 0)
            def _():
                for load in loads:
                    load.start()
                for fetch in fetches:
                    fetch.wait()

            attend_step(turn)
            columns = pl.ds(pl.multiple_of(turn * PACK * HEAD, HEAD), PACK * HEAD)
            send(
                attn.at[pl.ds(0, tokens), columns], attn.at[pl.ds(tokens, tokens), columns],
                near_send.at[0], near_recv.at[0], ACROSS,
            ).start()

        @pl.when(kind == READY)
        def _():
            residual_sent.start()
            send(attn_all, attn_all, near_send.at[0], near_recv.at[0], ACROSS).wait_recv()

        pl.when(kind == PROJECT)(lambda: project(nb, flag == 1))

    length = length_ref[place.me]
    per_group = HEADS // KV_HEADS // PACK

    def attend_step(i):
        q = jnp.concatenate(
            [
                q_ref[:, pl.ds(pl.multiple_of((i * PACK + j) * HEAD, HEAD), HEAD)]
                for j in range(PACK)
            ],
            axis=0,
        )
        columns = pl.ds(pl.multiple_of(i // per_group * HEAD, HEAD), HEAD)
        out = attend(
            q, k_ref[0, :, columns], v_ref[0, :, columns], nk_ref[:, columns],
            nv_ref[:, columns], length, tokens,
        )
        for j in range(PACK):
            attn[:tokens, pl.ds(pl.multiple_of((i * PACK + j) * HEAD, HEAD), HEAD)] = out[
                j * tokens : (j + 1) * tokens
            ]

    mixed_ref[...] = jnp.zeros(mixed_ref.shape, jnp.float32)
    chosen = lax.broadcasted_iota(jnp.int32, (1, share_tab.shape[1]), 1) == me

    def project(nb, is_own):
        yb = jnp.where(is_own, y, 1 - y)
        b = block_at(nb, yb, 1 - core)

        whole(b).wait_recv()
        share_copy(b, TWIN).wait_recv()
        first = block_at(nb, yb, 0)
        for c in range(2):
            turned = share_tab[first + c].T
            column = jnp.sum(jnp.where(chosen, turned, 0.0), axis=1, keepdims=True)
            share_col[first + c] = jnp.broadcast_to(column, share_col.shape[1:])
        mine = attn[:, pl.ds(pl.multiple_of(first * depth, 2 * depth), 2 * depth)]
        weight = held[pl.ds(first, 2)].reshape(2 * depth, wide)
        mixed_ref[...] += jnp.dot(mine, weight, preferred_element_type=jnp.float32)

    a_words = -(-max(len(A_END), len(A_INNER)) // 4)
    a_end = packed([gather_code(text) for text in A_END], a_words, 7)
    a_inner = packed([gather_code(text) for text in A_INNER], a_words, 7)

    def gather_route(w, turn):
        def one(j, state):
            word, at = state
            code = lax.rem(word, 128)
            happen(code, at)
            return word // 128, at + jnp.where(code // 8 == ATTEND, 1, 0)

        return lax.fori_loop(0, 4, one, (pick(w, inner, a_end, a_inner), turn))[1]

    lax.fori_loop(0, a_words, gather_route, jnp.int32(0))
    half_rows = tokens // 2
    residual_sent.wait_recv()
    mixed_ref[:tokens] += res_ref[:, my_columns].astype(jnp.float32)
    mixed_ref[tokens:] += res_pair[...].astype(jnp.float32)
    mixed = mixed_ref[...]
    square = jnp.sum(mixed * mixed, axis=1, keepdims=True)
    gained = (mixed * gain_ref[:, my_columns]).astype(jnp.bfloat16)

    def slot(zb, p, yb, c):
        return ((zb * 2 + p) * PAIR + yb) * 2 + c

    for p in range(2):
        mine = slot(z, p, y, core)
        own_half = slice(p * half_rows, (p + 1) * half_rows)
        pair_half = slice(tokens + p * half_rows, tokens + (p + 1) * half_rows)
        rows[mine * SUBS + y] = gained[own_half]
        rows[mine * SUBS + 1 - y] = gained[pair_half]
        both = jnp.where(
            y == 0,
            jnp.concatenate([square[own_half], square[pair_half]], axis=0),
            jnp.concatenate([square[pair_half], square[own_half]], axis=0),
        )
        squares[mine] = jnp.broadcast_to(both, (tokens, HEAD)).T[: squares.shape[1]]

    def square_copy(b, way):
        landed = twin_squares.at[b // 4] if way == TWIN else square_recv.at[b // 2]
        return send(squares.at[b], squares.at[b], square_send.at[way], landed, way)

    def pass_on(b, h, way):
        row_copy(b, h, way).start()
        pl.when(h == 0)(square_copy(b, way).start)

    def row_copy(b, h, way):
        t = b * SUBS + h
        landed = twin_rows.at[b // 4] if way == TWIN else row_recv.at[b // 2 * SUBS + h]
        return send(rows.at[t], rows.at[t], row_send.at[way], landed, way)

    def to_twin(zb, p, yb):
        b = slot(zb, p, yb, 1 - core)
        t = (zb * 2 + p) * PAIR + yb
        return send(part.at[b], from_twin.at[t], back_send.at[0], twin_sem.at[t], TWIN)

    def to_pair(zb, p):
        b = slot(zb, p, 1 - y, core)
        t = LINE if p else zb
        return send(part.at[b], from_pair.at[t], back_send.at[0], pair_sem.at[t], ACROSS)

    def kind_slot(zb, kind):
        p = jnp.minimum(kind, 1)
        yb = jnp.where(kind == 2, 1 - y, y)
        return p, yb, slot(zb, p, yb, core)

    side_up = jnp.where(low, 0, 1)

    def to_line(zb, kind, way):
        b = kind_slot(zb, kind)[2]
        side = side_up if way == UPN else 1 - side_up
        return send(
            part.at[b], from_line.at[side, zb, kind], back_send.at[0],
            line_sem.at[side, zb, kind], way,
        )

    def serve(zb, p):
        first = slot(zb, p, 0, 0)
        bulk = rows.at[pl.ds(0, 2 * SUBS)]
        send(bulk, bulk, row_send.at[TWIN], twin_rows.at[first // 4], TWIN).wait_recv()
        few = squares.at[pl.ds(0, 2)]
        send(few, few, square_send.at[TWIN], twin_squares.at[first // 4], TWIN).wait_recv()
        totals = [squares[first + c] + squares[first + 2 + c] for c in range(2)]
        total = jnp.concatenate(totals, axis=1)
        scale = lax.rsqrt(total * (1.0 / D) + 1e-06).T[:, :1]
        here = pl.ds(pl.multiple_of(p * half_rows, half_rows), half_rows)
        block = place.block(zb, 0, 0)
        share = jnp.concatenate(
            [share_col[block + yb * 2 + c, here] for c in range(2) for yb in range(2)], axis=0
        )
        sides = [
            rows[pl.ds((first + 2 * k) * SUBS, 2 * SUBS)].reshape(4 * half_rows, wide)
            for k in range(2)
        ]

        def times(w):
            first_half = jnp.dot(sides[0], w[:wide], preferred_element_type=jnp.float32)
            other_half = jnp.dot(sides[1], w[wide:], preferred_element_type=jnp.float32)
            return (first_half + other_half) * scale

        gate, up = times(wg), times(wu)
        act = (gate / (1.0 + jnp.exp(-gate)) * up).astype(jnp.bfloat16)
        out = jnp.dot(act, wd[...], preferred_element_type=jnp.float32) * share[:, :1]
        out = out.astype(jnp.bfloat16)
        for k in range(4):
            part[first + k % 2 * 2 + k // 2] = out[k * half_rows : (k + 1) * half_rows]
        to_twin(zb, p, 0).start()
        to_twin(zb, p, 1).start()

    def with_twin(zb, p, yb):
        to_twin(zb, p, yb).wait_recv()
        b = slot(zb, p, yb, core)
        t = (zb * 2 + p) * PAIR + yb
        return part[b].astype(jnp.float32) + from_twin[t].astype(jnp.float32)

    def add_line(zb, kind, way):
        to_line(zb, kind, way).wait_recv()
        side = side_up if way == UPN else 1 - side_up
        acc[...] += from_line[side, zb, kind].astype(jnp.float32)

    def fold(nb, kind):
        zb = real(nb)
        p, yb, b = kind_slot(zb, kind)
        acc[...] = with_twin(zb, p, yb)

        @pl.when(kind == 0)
        def _():
            to_pair(zb, 0).wait_recv()
            acc[...] += from_pair[zb].astype(jnp.float32)

        pl.when((nb > inner) & (inner == 1))(lambda: add_line(zb, kind, UPN))
        pl.when(nb < inner)(lambda: add_line(zb, kind, DOWNN))
        part[b] = acc[...].astype(jnp.bfloat16)
        pl.when(nb > inner)(to_line(zb, kind, UPN).start)
        pl.when(nb < inner)(to_line(zb, kind, DOWNN).start)

    def finish(kind):
        p, yb, b = kind_slot(z, kind)
        acc[...] = with_twin(z, p, yb)
        pl.when(inner == 1)(lambda: add_line(z, kind, UPN))
        add_line(z, kind, DOWNN)

        @pl.when(kind == 2)
        def _():
            acc[:, my_columns] += mixed_ref[pl.ds(tokens + half_rows, half_rows)]
            part[b] = acc[...].astype(jnp.bfloat16)
            to_pair(z, 1).start()

        def close(p, t):
            here = pl.ds(p * half_rows, half_rows)
            to_pair(z, p).wait_recv()
            acc[:, my_columns] += mixed_ref[here]
            out_ref[here] = (acc[...] + from_pair[t].astype(jnp.float32)).astype(jnp.bfloat16)

        pl.when(kind == 0)(lambda: close(0, z))
        pl.when(kind == 1)(lambda: close(1, LINE))

    def act_on(code, first):
        kind = code // 32
        nb = lax.rem(code // 8, 4)
        piece = lax.rem(code // 2, 4)
        h = lax.rem(code, 2)
        zb = real(nb)
        p = jnp.where(piece <= PB, 1, 0)
        yb = jnp.where((piece == PA) | (piece == PC), y, 1 - y)
        own_piece = slot(z, p, yb, core)

        @pl.when(kind == GET)
        def _():
            b = slot(zb, p, yb, core)
            row_copy(b, h, ACROSS).wait_recv()
            pl.when(h == 0)(square_copy(b, ACROSS).wait_recv)
            onward = piece != PD
            pl.when(onward & (nb < inner))(lambda: pass_on(b, h, UPN))
            pl.when(onward & (nb > inner) & (inner == 1))(lambda: pass_on(b, h, DOWNN))
            pl.when((piece == PC) & (nb != inner))(lambda: pass_on(b, h, ACROSS))
            pass_on(b, h, TWIN)

        pl.when(kind == UP_OWN)(lambda: pass_on(own_piece, h, UPN))
        pl.when(kind == DOWN_OWN)(lambda: pass_on(own_piece, h, DOWNN))

        @pl.when(kind == PASS_OWN)
        def _():
            pass_on(own_piece, h, ACROSS)
            pass_on(own_piece, h, TWIN)

        @pl.when(kind == SERVE)
        def _():
            @pl.when(first)
            def _():
                for load in loads:
                    load.wait()

            serve(zb, piece)

        @pl.when(kind == PAIR_UP)
        def _():
            acc[...] = with_twin(zb, 0, 1 - y)

            @pl.when(nb == inner)
            def _():
                acc[:, my_columns] += mixed_ref[pl.ds(tokens, half_rows)]

            part[slot(zb, 0, 1 - y, core)] = acc[...].astype(jnp.bfloat16)
            to_pair(zb, 0).start()

        pl.when(kind == FOLD)(lambda: fold(nb, piece))
        pl.when((kind == FINISH) & (piece < 3))(lambda: finish(piece))

    words = -(-max(len(B_END), len(B_INNER)) // 3)
    end_words = packed([code_of(text) for text in B_END], words, 9)
    inner_words = packed([code_of(text) for text in B_INNER], words, 9)
    serve_at = jnp.where(inner == 1, first_serve(B_INNER), first_serve(B_END))

    def route(w, carry):
        def one(j, word):
            act_on(lax.rem(word, 512), w * 3 + j == serve_at)
            return word // 512

        lax.fori_loop(0, 3, one, pick(w, inner, end_words, inner_words))
        return carry

    lax.fori_loop(0, words, route, 0)

    def sent(ref, sem, way=TWIN):
        send(ref, ref, sem, share_recv.at[0], way).wait_send()

    def sent_by_place(at_end, at_inner):
        pl.when(inner == 0)(at_end)
        pl.when(inner == 1)(at_inner)

    lines = pl.ds(0, long)
    sent_by_place(
        lambda: sent(held.at[pl.ds(0, 2), lines], send_sem.at[UPN]),
        lambda: sent(held.at[pl.ds(0, 4), lines], send_sem.at[UPN]),
    )
    sent_by_place(
        lambda: sent(share_tab.at[pl.ds(0, 1)], share_send.at[UPN]),
        lambda: sent(share_tab.at[pl.ds(0, 2)], share_send.at[UPN]),
    )
    sent_by_place(
        lambda: sent(rows.at[pl.ds(0, 3 * SUBS)], row_send.at[UPN]),
        lambda: sent(rows.at[pl.ds(0, 6 * SUBS)], row_send.at[UPN]),
    )
    sent_by_place(
        lambda: sent(squares.at[pl.ds(0, 3)], square_send.at[UPN]),
        lambda: sent(squares.at[pl.ds(0, 6)], square_send.at[UPN]),
    )

    @pl.when(inner == 1)
    def _():
        sent(held.at[pl.ds(0, 6), lines], send_sem.at[DOWNN])
        sent(share_tab.at[pl.ds(0, 3)], share_send.at[DOWNN])
        sent(rows.at[pl.ds(0, 9 * SUBS)], row_send.at[DOWNN])
        sent(squares.at[pl.ds(0, 9)], square_send.at[DOWNN])

    sent(held.at[0, lines], send_sem.at[ACROSS])
    sent(held.at[pl.ds(0, 2 * LINE - 1), pl.ds(0, short)], send_sem.at[XWAY])
    sent(attn_all, near_send.at[0])
    residual_sent.wait_send()
    sent(held.at[pl.ds(0, 2 * LINE)], send_sem.at[TWIN])
    sent(share_tab.at[pl.ds(0, LINE)], share_send.at[ACROSS])
    sent(share_tab.at[pl.ds(0, 2 * LINE)], share_send.at[TWIN])
    sent(rows.at[pl.ds(0, 5 * SUBS)], row_send.at[ACROSS])
    sent(rows.at[pl.ds(0, 4 * LINE * SUBS)], row_send.at[TWIN])
    sent(squares.at[pl.ds(0, 5)], square_send.at[ACROSS])
    sent(squares.at[pl.ds(0, 4 * LINE)], square_send.at[TWIN])
    sent(part.at[pl.ds(0, 7 * LINE + 2)], back_send.at[0])


def layer(
    cache_len, queries, new_keys, new_values, cache_keys, cache_values, residual, gain, ids, raw,
    o_weight, gate_w, up_w, down_w, devices,
):
    tokens, width = queries.shape
    half = tokens // 2
    vmem = pl.BlockSpec(memory_space=pltpu.VMEM)
    whole = pl.BlockSpec(memory_space=pl.ANY)
    dma = pltpu.SemaphoreType.DMA

    def held(*lead):
        return pltpu.VMEM(lead + (half, D), jnp.bfloat16)

    return pl.pallas_call(
        layer_kernel,
        in_specs=[pl.BlockSpec(memory_space=pltpu.SMEM)] + [vmem] * 6 + [whole] * 7,
        out_specs=vmem,
        out_shape=jax.ShapeDtypeStruct((tokens, D), jnp.bfloat16),
        scratch_shapes=[
            pltpu.VMEM(queries.shape, jnp.bfloat16),
            pltpu.VMEM(cache_keys.shape, jnp.bfloat16),
            pltpu.VMEM(cache_values.shape, jnp.bfloat16),
            pltpu.VMEM((devices, o_weight.shape[0], D // 2), jnp.bfloat16),
            pltpu.VMEM((2 * tokens, width), jnp.bfloat16),
            pltpu.VMEM((2 * tokens, D // 2), jnp.float32),
            pltpu.VMEM((tokens, D // 2), jnp.bfloat16),
            pltpu.VMEM((2 * devices, 8, tokens), jnp.float32),
            pltpu.VMEM((devices, devices, tokens), jnp.float32),
            pltpu.VMEM((devices, tokens, HEAD), jnp.float32),
            pltpu.VMEM((2 * devices * SUBS, half, D // 2), jnp.bfloat16),
            held(2 * devices),
            held(devices),
            held(LINE + 1),
            held(2, LINE, 3),
            pltpu.VMEM((half, D), jnp.float32),
            pltpu.VMEM(gate_w.shape, jnp.bfloat16),
            pltpu.VMEM(up_w.shape, jnp.bfloat16),
            pltpu.VMEM(down_w.shape, jnp.bfloat16),
            dma,
            dma((6,)),
            dma((5,)),
            dma((devices // 2, 2)),
            dma((devices // 2,)),
            dma((2,)),
            dma((2,)),
            dma((4,)),
            dma((devices,)),
            dma((4,)),
            dma((devices * SUBS,)),
            dma((devices // 2,)),
            dma((4,)),
            dma((devices,)),
            dma((devices // 2,)),
            dma((1,)),
            dma((devices,)),
            dma((LINE + 1,)),
            dma((2, LINE, 3)),
        ],
        compiler_params=pltpu.CompilerParams(
            collective_id=0, has_side_effects=True, vmem_limit_bytes=63 << 20
        ),
    )(
        cache_len, new_keys, new_values, residual, gain, ids, raw, queries, cache_keys, cache_values,
        o_weight, gate_w, up_w, down_w,
    )


def grid_device(
    residual, queries, new_keys, new_values, cache_keys, cache_values, cache_len, o_weight,
    norm_gain, expert_ids, gate_raw, w_gate, w_up, w_down,
):
    devices = lax.axis_size("wide")
    return layer(
        cache_len, queries, new_keys, new_values, cache_keys, cache_values, residual,
        norm_gain.reshape(1, D), expert_ids.T, gate_raw.T, o_weight, w_gate[0], w_up[0], w_down[0], devices,
    )


def per_device(
    residual,
    queries,
    new_keys,
    new_values,
    cache_keys,
    cache_values,
    cache_len,
    o_weight,
    norm_gain,
    expert_ids,
    gate_raw,
    w_gate,
    w_up,
    w_down,
):
    devices = lax.axis_size("wide")
    me = lax.axis_index("wide")
    length = lax.dynamic_slice_in_dim(cache_len, me, 1, 0)
    attn = attention(length, queries, new_keys, new_values, cache_keys, cache_values)
    projected = jnp.dot(
        attn,
        lax.all_gather(o_weight, "wide", axis=0, tiled=True),
        preferred_element_type=jnp.float32,
    )
    mixed = residual.astype(jnp.float32) + projected
    normed = (
        mixed * lax.rsqrt(jnp.mean(mixed * mixed, axis=-1, keepdims=True) + 1e-06) * norm_gain
    ).astype(jnp.bfloat16)
    shares = gate_raw / jnp.sum(gate_raw, axis=-1, keepdims=True)
    routed = sparse_experts(normed, expert_ids, shares, w_gate[0], w_up[0], w_down[0], devices)
    return (mixed + routed).astype(jnp.bfloat16)


def solution(mesh):
    rows = P(("groups", "wide"), None)
    blocks = P(("groups", "wide"), None, None)
    weights = P("wide", None, None)
    placed = (rows, rows, rows, rows, blocks, blocks, P("groups"), P("wide", None), P())
    placed += (rows, rows, weights, weights, weights)
    grid = mesh.shape["wide"] == LINE * PAIR * 2 and mesh.shape["groups"] == 2
    return jax.shard_map(
        grid_device if grid else per_device,
        mesh=mesh,
        in_specs=placed,
        out_specs=rows,
        check_vma=False,
    )
```
